32 devices in a mesh: dp: 16 (over z, y, core), mp: 2 (over x).
Axes of the slice: x: 2, y: 2, z: 4, core: 2. Of those that a mesh axis runs over, the one named last changes fastest.
Arguments:
- tokens: bfloat16 [16384, 1024], P('dp', 'mp'), may hold values from -6 to 6
- cotangent: bfloat16 [16384, 1024], P('dp', 'mp'), may hold values from -6 to 6
- route: int32 [16384], P('dp'), may hold values from 0 to 16383, as said below
- seq_lengths: int32 [16, 4], P('dp'), may hold values from 1 to 512, 1024 in all within a row
- norm1_gain: float32 [1024], replicated, may hold values from 0.25 to 1.75
- in_weight: bfloat16 [3, 1024, 1024], P(None, None, 'mp'), may hold values from -0.1875 to 0.1875
- conv_weight: float32 [3, 1024], P(None, 'mp'), may hold values from -3 to 3
- out_weight: bfloat16 [1024, 1024], P('mp'), may hold values from -0.1875 to 0.1875
- norm2_gain: float32 [1024], replicated, may hold values from 0.25 to 1.75
- gate_weight: bfloat16 [1024, 4608], P(None, 'mp'), may hold values from -0.1875 to 0.1875
- up_weight: bfloat16 [1024, 4608], P(None, 'mp'), may hold values from -0.1875 to 0.1875
- down_weight: bfloat16 [4608, 1024], P('mp'), may hold values from -0.09375 to 0.09375
Outputs:
- block_out: bfloat16 [16384, 1024], P('dp', 'mp')
- tokens_grad: float32 [16384, 1024], P('dp', 'mp')
- norm1_gain_grad: float32 [1024], replicated
- in_weight_grad: float32 [3, 1024, 1024], P(None, None, 'mp')
- conv_weight_grad: float32 [3, 1024], P(None, 'mp')
- out_weight_grad: float32 [1024, 1024], P('mp')
- norm2_gain_grad: float32 [1024], replicated
- gate_weight_grad: float32 [1024, 4608], P(None, 'mp')
- up_weight_grad: float32 [1024, 4608], P(None, 'mp')
- down_weight_grad: float32 [4608, 1024], P('mp')
The draws below stay inside these ranges and needn't reach their ends.
Inputs may be any that keep to these rules, and one draw needn't show every extreme that they name: route is a permutation of the packed places; the 1024 arrival rows of one dp shard go 96 to one group, 32 to another and 64 to each other group, which groups drawn from the seed. `seq_lengths`: each row sums to 1024.
All inputs are finite; a program needn't handle non-finite values.
Results may differ from the reference program's by a relative error of at most 0.011.
Values may be sent and summed in bfloat16 or wider, within the bound.
No kernel may reach another device: no remote copies, remote signals or barrier semaphores. Data moves between devices by JAX's collectives and lax.ppermute only.
A program may use at most 192 MiB of HBM per device.

```python
import math
import jax
import jax.numpy as jnp
import numpy as np
from jax import lax

D = 1024
FF = 4608
KERNEL = 3
SEQS = 4
TOK_GRP = 1024
GROUPS = 16
TOKENS = 16384
SEQ_MOST = 512
N_DP = 16


def draw_route(key, part):
    key_pairs = jax.random.fold_in(key, 11)
    key_local = jax.random.fold_in(key, 23)
    key_group = jax.random.fold_in(key, 37)
    pair_share = TOK_GRP // N_DP
    surplus = pair_share // 2
    ordering = jax.random.permutation(key_pairs, N_DP).astype(jnp.int32)
    following = jnp.roll(ordering, -1)
    columns = jnp.arange(N_DP, dtype=jnp.int32)
    counts = pair_share + surplus * (columns[None, :] == ordering[:, None]).astype(jnp.int32) - surplus * (columns[None, :] == following[:, None]).astype(jnp.int32)
    send_ends = jnp.cumsum(counts, axis=1, dtype=jnp.int32)
    send_start = send_ends - counts
    recv_start = jnp.cumsum(counts, axis=0, dtype=jnp.int32) - counts
    slot_ids = jnp.arange(TOK_GRP, dtype=jnp.int32)
    target = jnp.sum((slot_ids[None, :, None] >= send_ends[:, None, :]).astype(jnp.int32), axis=2, dtype=jnp.int32)
    within = slot_ids[None, :] - jnp.take_along_axis(send_start, target, axis=1)
    inner = jnp.take_along_axis(recv_start, target, axis=1) + within
    local_perm = jax.vmap(lambda sub: jax.random.permutation(sub, TOK_GRP))(jax.random.split(key_local, N_DP)).astype(jnp.int32)
    group_perm = jax.vmap(lambda sub: jax.random.permutation(sub, TOK_GRP))(jax.random.split(key_group, N_DP)).astype(jnp.int32)
    packed = target * TOK_GRP + group_perm[target, inner]
    arrival = columns[:, None] * TOK_GRP + local_perm
    route = jnp.zeros((TOKENS,), jnp.int32).at[arrival.reshape(-1)].set(packed.reshape(-1))
    return route


def steps_of(own_key, extent, cuts, smallest, top_value):
    def one(axis_at, shards_of):
        draws = jax.random.uniform(jax.random.fold_in(jax.random.fold_in(own_key, 6), axis_at), (shards_of,), jnp.float32, smallest / len(cuts), top_value / len(cuts))
        return jnp.repeat(jnp.exp(draws), extent[axis_at] // shards_of).reshape((-1,) + (1,) * (len(extent) - axis_at - 1))

    gain = one(*cuts[0])
    for cut in cuts[1:]:
        gain = gain * one(*cut)
    return gain


def length_profile(count, total, bound, slope):
    loads = [(1 << 20) // math.isqrt(rank ** slope) + 1 for rank in range(2, count + 1)]
    spare, given = total - bound - (count - 1), [1] * (count - 1)
    while spare > 0:
        movable = [i for i in range(count - 1) if given[i] < bound]
        mass, budget = sum([loads[i] for i in movable]), spare
        for i in movable:
            addition = min(bound - given[i], max(1, budget * loads[i] // mass), spare)
            given[i] = given[i] + addition
            spare = spare - addition
    return np.array([bound] + given)


def uneven_parts(rng, count, total, limit, lean):
    if count == 2:
        one = jax.random.randint(rng, (), max(1, total - limit), min(limit, total - 1) + 1)
        return jnp.stack([one, total - one])
    sizes = jnp.asarray(length_profile(count, total, limit, lean), jnp.int32)
    couples = (count - 1) // 2
    source_of, sink = sizes[1:1 + 2 * couples:2], sizes[2:2 + 2 * couples:2]
    slack = jnp.minimum(source_of - 1, limit - sink)
    moved = jax.random.randint(jax.random.fold_in(rng, 1), (couples,), 0, 1 << 20) % (slack + 1)
    sizes = sizes.at[1:1 + 2 * couples:2].set(source_of - moved).at[2:2 + 2 * couples:2].set(sink + moved)
    return sizes[jax.random.permutation(jax.random.fold_in(rng, 2), count)]


def centred(own_key, shape, spread, bound, cuts=(), kind=jnp.bfloat16):
    array = spread * jax.random.normal(own_key, shape, jnp.float32)
    if cuts:
        array = array * steps_of(own_key, shape, cuts, -0.22, 0.18)
    return jnp.clip(array, -bound, bound).astype(kind)


def setup_inputs(seed: int = 0) -> dict:
    key_of = jax.random.split(jax.random.key(seed), 13)
    tokens = centred(key_of[0], (TOKENS, D), 1.0, 6.0, ((0, 16), (1, 2)))
    cotangent = centred(key_of[1], (TOKENS, D), 1.0, 6.0, ((0, 16), (1, 2)))
    route = draw_route(jax.random.fold_in(key_of[12], 71), 0)
    seq_lengths = jax.vmap(lambda own: uneven_parts(own, SEQS, TOK_GRP, SEQ_MOST, 1))(jax.random.split(key_of[3], GROUPS)).reshape((GROUPS, SEQS)).astype(jnp.int32)
    norm1_gain = jnp.clip(1.0 + 0.15 * jax.random.normal(key_of[4], (D,), jnp.float32), 0.25, 1.75)
    in_weight = centred(key_of[5], (KERNEL, D, D), D ** -0.5, 0.1875, ((2, 2),))
    conv_weight = centred(key_of[6], (KERNEL, D), 0.6, 3.0, ((1, 2),), jnp.float32)
    out_weight = centred(key_of[7], (D, D), D ** -0.5, 0.1875, ((0, 2),))
    norm2_gain = jnp.clip(1.0 + 0.15 * jax.random.normal(key_of[8], (D,), jnp.float32), 0.25, 1.75)
    gate_weight = centred(key_of[9], (D, FF), D ** -0.5, 0.1875, ((1, 2),))
    up_weight = centred(key_of[10], (D, FF), D ** -0.5, 0.1875, ((1, 2),))
    down_weight = centred(key_of[11], (FF, D), FF ** -0.5, 0.09375, ((0, 2),))
    return dict(tokens=tokens, cotangent=cotangent, route=route, seq_lengths=seq_lengths, norm1_gain=norm1_gain, in_weight=in_weight, conv_weight=conv_weight, out_weight=out_weight, norm2_gain=norm2_gain, gate_weight=gate_weight, up_weight=up_weight, down_weight=down_weight)


epsilon = 1e-05
highest = lax.Precision.HIGHEST

@jax.custom_vjp
def low(v):
    return lax.optimization_barrier(v.astype(jnp.bfloat16)).astype(jnp.float32)

@jax.custom_vjp
def low_back(v):
    return v

def low_keep(v):
    return (low(v), None)

def low_pass(kept, grad):
    return (grad,)

def back_keep(v):
    return (v, None)

def back_low(kept, grad):
    return (low(grad),)
low.defvjp(low_keep, low_pass)
low_back.defvjp(back_keep, back_low)

def matmul(left, right):
    return jnp.dot(left, right, precision=highest, preferred_element_type=jnp.float32)

def lag_rows(values, shift):
    return jnp.concatenate([jnp.zeros((shift, values.shape[1]), values.dtype), values[:-shift]], axis=0)

def seq_masks(lengths, row_count):
    starts = jnp.cumsum(lengths, dtype=jnp.int32) - lengths
    position = jnp.arange(row_count, dtype=jnp.int32)
    started = position[:, None] >= starts[None, :]
    seq_first = lax.optimization_barrier(jnp.max(jnp.where(started, starts[None, :], 0), axis=1)).astype(jnp.int32)
    offset = position - seq_first
    return ((offset >= 1).astype(jnp.float32)[:, None], (offset >= 2).astype(jnp.float32)[:, None])

def layer(packed, gain_one, w_in, w_conv, w_out, gain_two, w_gate, w_up, w_down, first_mask, second_mask):
    scale_one = lax.rsqrt(lax.optimization_barrier(jnp.mean(packed * packed, axis=1, keepdims=True)) + epsilon)
    normed_one = low(packed * scale_one * gain_one)
    in_gate = low_back(matmul(normed_one, w_in[0]))
    out_gate = low_back(matmul(normed_one, w_in[1]))
    value_part = low_back(matmul(normed_one, w_in[2]))
    mixed = in_gate * value_part
    convolved = w_conv[2] * mixed + w_conv[1] * lag_rows(mixed, 1) * first_mask + w_conv[0] * lag_rows(mixed, 2) * second_mask
    gated = low(out_gate * convolved)
    middle = packed + low_back(matmul(gated, w_out))
    scale_two = lax.rsqrt(lax.optimization_barrier(jnp.mean(middle * middle, axis=1, keepdims=True)) + epsilon)
    normed_two = low(middle * scale_two * gain_two)
    gate_val = low_back(matmul(normed_two, w_gate))
    up_val = low_back(matmul(normed_two, w_up))
    hidden = low(jax.nn.silu(gate_val) * up_val)
    return middle + low_back(matmul(hidden, w_down))

def reference(tokens, cotangent, route, seq_lengths, norm1_gain, in_weight, conv_weight, out_weight, norm2_gain, gate_weight, up_weight, down_weight):
    model_width = tokens.shape[1]
    packed_x = jnp.zeros(tokens.shape, jnp.float32).at[route].set(tokens.astype(jnp.float32))
    packed_g = jnp.zeros(tokens.shape, jnp.float32).at[route].set(cotangent.astype(jnp.float32))
    weight_set = (norm1_gain.astype(jnp.float32), in_weight.astype(jnp.float32), conv_weight.astype(jnp.float32), out_weight.astype(jnp.float32), norm2_gain.astype(jnp.float32), gate_weight.astype(jnp.float32), up_weight.astype(jnp.float32), down_weight.astype(jnp.float32))
    group_x = packed_x.reshape(N_DP, TOK_GRP, model_width)
    group_g = packed_g.reshape(N_DP, TOK_GRP, model_width)

    def one_group(running, group_item):
        rows_x, rows_g, lengths = group_item
        first_mask, second_mask = seq_masks(lengths, TOK_GRP)

        def forward(packed, gain_one, w_in, w_conv, w_out, gain_two, w_gate, w_up, w_down):
            return layer(packed, gain_one, w_in, w_conv, w_out, gain_two, w_gate, w_up, w_down, first_mask, second_mask)
        result, pullback = jax.vjp(forward, rows_x, *weight_set)
        gradients = pullback(rows_g)
        updated = tuple((first + second for first, second in zip(running, gradients[1:])))
        return (updated, (result, gradients[0]))
    zero_set = tuple((jnp.zeros_like(item) for item in weight_set))
    totals, (out_rows, grad_rows) = lax.scan(one_group, zero_set, (group_x, group_g, seq_lengths))
    block_out = out_rows.reshape(TOKENS, model_width)[route].astype(jnp.bfloat16)
    tokens_grad = grad_rows.reshape(TOKENS, model_width)[route]
    return (block_out, tokens_grad, totals[0], totals[1], totals[2], totals[3], totals[4], totals[5], totals[6], totals[7])
```

```python
import jax
import jax.numpy as jnp
from jax import lax
from jax.experimental import pallas as pl
from jax.experimental.pallas import tpu as pltpu
from jax.sharding import PartitionSpec as P

epsilon = 1e-05
f32 = jnp.float32
bf16 = jnp.bfloat16


def lag_rows(values, shift):
    return jnp.concatenate(
        [jnp.zeros((shift, values.shape[1]), values.dtype), values[:-shift]], axis=0
    )


def lead_rows(values, shift):
    return jnp.concatenate(
        [values[shift:], jnp.zeros((shift, values.shape[1]), values.dtype)], axis=0
    )


def seq_masks(lengths, row_count):
    count = lengths.shape[0]
    before = jnp.arange(count)[:, None] < jnp.arange(count)[None, :]
    starts = jnp.sum(jnp.where(before, lengths[:, None], 0), axis=0, dtype=jnp.int32)
    position = jnp.arange(row_count, dtype=jnp.int32)
    started = position[:, None] >= starts[None, :]
    seq_first = jnp.max(jnp.where(started, starts[None, :], 0), axis=1)
    offset = position - seq_first
    return ((offset >= 1).astype(f32)[:, None], (offset >= 2).astype(f32)[:, None])


def pack_kernel(rows, slots, route_ref, x_ref, g_ref, sx_ref, sg_ref, place_ref, slot_ref):
    j = pl.program_id(0)
    members = pl.num_programs(0)
    width = min(rows, 512)

    @pl.when(j == 0)
    def _():
        route = route_ref[...]
        target = route // rows
        owner = lax.broadcasted_iota(jnp.int32, (members, rows), 0)
        one_hot = jnp.where(owner == target, 1.0, 0.0)
        for start in range(0, rows, width):
            first = lax.broadcasted_iota(jnp.int32, (rows, width), 0)
            second = lax.broadcasted_iota(jnp.int32, (rows, width), 1) + start
            earlier = jnp.where(first < second, 1.0, 0.0).astype(bf16)
            rank = jnp.dot(one_hot.astype(bf16), earlier, preferred_element_type=f32)
            piece = one_hot[:, start : start + width]
            mine = jnp.sum(rank * piece, axis=0, keepdims=True).astype(jnp.int32)
            slot_ref[:, start : start + width] = (
                target[:, start : start + width] * slots + mine
            )

    ids = lax.broadcasted_iota(jnp.int32, (slots, rows), 0) + j * slots
    pick = jnp.where(slot_ref[...] == ids, 1.0, 0.0).astype(bf16)
    sx_ref[...] = jnp.dot(pick, x_ref[...], preferred_element_type=f32).astype(bf16)
    sg_ref[...] = jnp.dot(pick, g_ref[...], preferred_element_type=f32).astype(bf16)
    place = route_ref[...] % rows
    row = lax.broadcasted_iota(jnp.int32, (16, rows), 0)
    digits = jnp.where(
        row == 0,
        (place // 64).astype(f32),
        jnp.where(row == 1, (place % 64).astype(f32), 1.0),
    ).astype(bf16)
    sent = lax.dot_general(
        digits, pick, (((1,), (1,)), ((), ())), preferred_element_type=f32
    )
    value = sent[0:1] * 64.0 + sent[1:2] + (1.0 - sent[2:3]) * rows
    place_ref[...] = jnp.broadcast_to(value, (8, slots)).astype(jnp.int32)


def pack(route, tokens, cotangent, members, slots):
    rows, width = tokens.shape
    whole = lambda j: (0, 0)
    return pl.pallas_call(
        lambda *refs: pack_kernel(rows, slots, *refs),
        grid=(members,),
        in_specs=[
            pl.BlockSpec((1, rows), whole),
            pl.BlockSpec((rows, width), whole),
            pl.BlockSpec((rows, width), whole),
        ],
        out_specs=[
            pl.BlockSpec((None, slots, width), lambda j: (j, 0, 0)),
            pl.BlockSpec((None, slots, width), lambda j: (j, 0, 0)),
            pl.BlockSpec((None, 8, slots), lambda j: (j, 0, 0)),
            pl.BlockSpec((1, rows), whole),
        ],
        out_shape=[
            jax.ShapeDtypeStruct((members, slots, width), bf16),
            jax.ShapeDtypeStruct((members, slots, width), bf16),
            jax.ShapeDtypeStruct((members, 8, slots), jnp.int32),
            jax.ShapeDtypeStruct((1, rows), jnp.int32),
        ],
        compiler_params=pltpu.CompilerParams(vmem_limit_bytes=56 << 20),
        name="pack",
    )(route.reshape(1, rows), tokens, cotangent)


def place_kernel(block, places_ref, got_ref, out_ref):
    base = pl.program_id(0) * block
    ids = lax.broadcasted_iota(jnp.int32, (block, places_ref.shape[1]), 0) + base
    pick = jnp.where(places_ref[...] == ids, 1.0, 0.0).astype(bf16)
    out_ref[...] = jnp.dot(pick, got_ref[...], preferred_element_type=f32).astype(bf16)


def place_rows(places, got, rows):
    total, width = got.shape
    block = min(rows, 256)
    return pl.pallas_call(
        lambda *refs: place_kernel(block, *refs),
        grid=(rows // block,),
        in_specs=[
            pl.BlockSpec((1, total), lambda i: (0, 0)),
            pl.BlockSpec((total, width), lambda i: (0, 0)),
        ],
        out_specs=pl.BlockSpec((block, width), lambda i: (i, 0)),
        out_shape=jax.ShapeDtypeStruct((rows, width), bf16),
        compiler_params=pltpu.CompilerParams(vmem_limit_bytes=56 << 20),
        name="place_rows",
    )(places, got)


def take_kernel(ids_ref, from_ref, out_ref):
    cols = lax.broadcasted_iota(jnp.int32, (out_ref.shape[0], from_ref.shape[0]), 1)
    pick = jnp.where(ids_ref[...] == cols, 1.0, 0.0).astype(bf16)
    out_ref[...] = jnp.dot(
        pick, from_ref[...].astype(bf16), preferred_element_type=f32
    ).astype(out_ref.dtype)


def take_rows(ids, source, block, dtype):
    count = ids.shape[0]
    total, width = source.shape
    return pl.pallas_call(
        take_kernel,
        grid=(count // block,),
        in_specs=[
            pl.BlockSpec((block, 1), lambda i: (i, 0)),
            pl.BlockSpec((total, width), lambda i: (0, 0)),
        ],
        out_specs=pl.BlockSpec((block, width), lambda i: (i, 0)),
        out_shape=jax.ShapeDtypeStruct((count, width), dtype),
        compiler_params=pltpu.CompilerParams(vmem_limit_bytes=56 << 20),
        name="take_rows",
    )(ids, source)


def swap_mp(value):
    return lax.ppermute(value, "mp", [(0, 1), (1, 0)])


def gather_features(piece, members, index):
    if members != 2:
        return lax.all_gather(piece, "mp", axis=1, tiled=True)
    other = swap_mp(piece)
    return jnp.where(
        index == 0,
        jnp.concatenate([piece, other], axis=1),
        jnp.concatenate([other, piece], axis=1),
    )


def sum_mp(partial, members):
    if members != 2:
        return lax.psum(partial, "mp")
    return partial + swap_mp(partial.astype(bf16)).astype(f32)


def sum_features(partial, members, index):
    if members != 2:
        return lax.psum_scatter(partial, "mp", scatter_dimension=1, tiled=True)
    narrow = partial.shape[1] // 2
    low, high = partial[:, :narrow], partial[:, narrow:]
    sent = jnp.where(index == 0, high, low).astype(bf16)
    kept = jnp.where(index == 0, low, high)
    return kept + swap_mp(sent).astype(f32)


def flip(value, bit, size):
    return lax.ppermute(value, "dp", [(i, i ^ bit) for i in range(size)])


def sum_dp(partial, size, index):
    bits = []
    bit = 1
    while bit < size:
        bits.append(bit)
        bit *= 2
    value = partial
    for bit in bits:
        half = value.shape[0] // 2
        side = (index // bit) % 2
        sent = lax.dynamic_slice_in_dim(value, (1 - side) * half, half, 0)
        kept = lax.dynamic_slice_in_dim(value, side * half, half, 0)
        value = (kept.astype(f32) + flip(sent, bit, size).astype(f32)).astype(bf16)
    for bit in reversed(bits):
        side = (index // bit) % 2
        other = flip(value, bit, size)
        value = jnp.where(
            side == 0,
            jnp.concatenate([value, other], axis=0),
            jnp.concatenate([other, value], axis=0),
        )
    return value


def on_device(
    tokens,
    cotangent,
    route,
    seq_lengths,
    norm1_gain,
    in_weight,
    conv_weight,
    out_weight,
    norm2_gain,
    gate_weight,
    up_weight,
    down_weight,
):
    dp_size = lax.axis_size("dp")
    mp_size = lax.axis_size("mp")
    dp_index = lax.axis_index("dp")
    mp_index = lax.axis_index("mp")
    row_count = tokens.shape[0]
    narrow = tokens.shape[1]
    model_width = norm1_gain.shape[0]
    pair_share = row_count // dp_size
    slot_count = pair_share + pair_share // 2
    slot_total = dp_size * slot_count

    send_rows, send_seeds, send_places, slots = pack(
        route, tokens, cotangent, dp_size, slot_count
    )
    got_places = lax.all_to_all(
        send_places[:, 0, :], "dp", split_axis=0, concat_axis=0, tiled=True
    )
    got_rows = lax.all_to_all(send_rows, "dp", split_axis=0, concat_axis=0, tiled=True)
    got_seeds = lax.all_to_all(send_seeds, "dp", split_axis=0, concat_axis=0, tiled=True)
    places = got_places.reshape(1, slot_total)
    place_ids = got_places.reshape(slot_total, 1)
    slot_of = slots.reshape(row_count, 1)

    input_piece = place_rows(places, got_rows.reshape(slot_total, narrow), row_count)
    seed_piece = place_rows(places, got_seeds.reshape(slot_total, narrow), row_count)
    input_full = gather_features(input_piece, mp_size, mp_index)
    seed_full = gather_features(seed_piece, mp_size, mp_index)

    first_mask, second_mask = seq_masks(seq_lengths[0], row_count)
    column_start = mp_index * narrow
    gain_one = lax.dynamic_slice_in_dim(norm1_gain, column_start, narrow)
    residual = input_full.astype(f32)
    scale_one = lax.rsqrt(jnp.mean(residual * residual, axis=1) + epsilon)
    normed_one = (residual * scale_one[:, None] * norm1_gain).astype(bf16)
    projected = jnp.einsum("rd,kdc->krc", normed_one, in_weight, preferred_element_type=f32)
    in_gate, out_gate, value_part = (projected[0], projected[1], projected[2])
    mixed = in_gate * value_part
    lag_one = lag_rows(mixed, 1) * first_mask
    lag_two = lag_rows(mixed, 2) * second_mask
    convolved = conv_weight[2] * mixed + conv_weight[1] * lag_one + conv_weight[0] * lag_two
    gated = (out_gate * convolved).astype(bf16)
    mix_terms = jnp.dot(gated, out_weight, preferred_element_type=f32)
    middle = residual + sum_mp(mix_terms, mp_size)
    scale_two = lax.rsqrt(jnp.mean(middle * middle, axis=1) + epsilon)
    normed_two = (middle * scale_two[:, None] * norm2_gain).astype(bf16)

    gate_val = jnp.dot(normed_two, gate_weight, preferred_element_type=f32)
    up_val = jnp.dot(normed_two, up_weight, preferred_element_type=f32)
    sigmoid_val = jax.nn.sigmoid(gate_val)
    silu_val = gate_val * sigmoid_val
    hidden = (silu_val * up_val).astype(bf16)
    grad_hidden = jnp.einsum("rd,fd->rf", seed_full, down_weight, preferred_element_type=f32)
    grad_gate_val = (
        grad_hidden * up_val * sigmoid_val * (1.0 + gate_val * (1.0 - sigmoid_val))
    ).astype(bf16)
    grad_up_val = (grad_hidden * silu_val).astype(bf16)
    normed_terms = jnp.einsum(
        "rf,df->rd", grad_gate_val, gate_weight, preferred_element_type=f32
    ) + jnp.einsum("rf,df->rd", grad_up_val, up_weight, preferred_element_type=f32)
    grad_normed_two = sum_mp(normed_terms, mp_size)

    down_terms = jnp.dot(hidden, down_weight, preferred_element_type=f32)
    middle_piece = lax.dynamic_slice_in_dim(middle, column_start, narrow, 1)
    block_piece = middle_piece + sum_features(down_terms, mp_size, mp_index)

    grad_down = jnp.einsum("rf,rd->fd", hidden, seed_full, preferred_element_type=f32)
    grad_gate = jnp.einsum("rd,rf->df", normed_two, grad_gate_val, preferred_element_type=f32)
    grad_up = jnp.einsum("rd,rf->df", normed_two, grad_up_val, preferred_element_type=f32)
    total_down = sum_dp(grad_down.astype(bf16), dp_size, dp_index)
    total_gate = sum_dp(grad_gate.astype(bf16), dp_size, dp_index)
    total_up = sum_dp(grad_up.astype(bf16), dp_size, dp_index)

    grad_gain_two = jnp.sum(grad_normed_two * middle * scale_two[:, None], axis=0)
    dot_two = jnp.sum(norm2_gain * grad_normed_two * middle, axis=1)
    grad_middle = (
        seed_full.astype(f32)
        + scale_two[:, None] * norm2_gain * grad_normed_two
        - middle * (scale_two * scale_two * scale_two * dot_two / model_width)[:, None]
    )
    grad_mix = grad_middle.astype(bf16)
    grad_out_weight = jnp.einsum("rc,rd->cd", gated, grad_mix, preferred_element_type=f32)
    grad_gated = jnp.einsum("rd,cd->rc", grad_mix, out_weight, preferred_element_type=f32)
    grad_conv = grad_gated * out_gate
    grad_conv_weight = jnp.stack(
        [
            jnp.sum(grad_conv * lag_two, axis=0),
            jnp.sum(grad_conv * lag_one, axis=0),
            jnp.sum(grad_conv * mixed, axis=0),
        ],
        axis=0,
    )
    grad_mixed = (
        conv_weight[2] * grad_conv
        + conv_weight[1] * lead_rows(grad_conv * first_mask, 1)
        + conv_weight[0] * lead_rows(grad_conv * second_mask, 2)
    )
    grad_parts = jnp.stack(
        [grad_mixed * value_part, grad_gated * convolved, grad_mixed * in_gate], axis=0
    ).astype(bf16)
    first_terms = jnp.einsum("krc,kdc->rd", grad_parts, in_weight, preferred_element_type=f32)
    grad_in_weight = jnp.einsum("rd,krc->kdc", normed_one, grad_parts, preferred_element_type=f32)
    total_in = sum_dp(
        grad_in_weight.astype(bf16).reshape(-1, narrow), dp_size, dp_index
    ).reshape(in_weight.shape)
    total_out = sum_dp(grad_out_weight.astype(bf16), dp_size, dp_index)

    grad_normed_one = sum_features(first_terms, mp_size, mp_index)
    dot_one = jnp.sum(norm1_gain * first_terms * residual, axis=1)
    dot_one = dot_one + swap_mp(dot_one) if mp_size == 2 else lax.psum(dot_one, "mp")
    residual_piece = input_piece.astype(f32)
    gain_one_piece = jnp.sum(grad_normed_one * residual_piece * scale_one[:, None], axis=0)
    grad_middle_piece = lax.dynamic_slice_in_dim(grad_middle, column_start, narrow, 1)
    input_grad = (
        grad_middle_piece
        + scale_one[:, None] * gain_one * grad_normed_one
        - residual_piece * (scale_one * scale_one * scale_one * dot_one / model_width)[:, None]
    )

    small = lax.psum(
        jnp.concatenate(
            [gain_one_piece, grad_gain_two, grad_conv_weight.reshape(-1)], axis=0
        ),
        "dp",
    )
    total_gain_one = lax.all_gather(small[:narrow], "mp", axis=0, tiled=True)
    total_gain_two = small[narrow : narrow + model_width]
    total_conv = small[narrow + model_width :].reshape(conv_weight.shape)

    back_out = take_rows(place_ids, block_piece.astype(bf16), slot_count, bf16)
    back_grad = take_rows(place_ids, input_grad.astype(bf16), slot_count, bf16)
    shape = (dp_size, slot_count, narrow)
    home_out = lax.all_to_all(
        back_out.reshape(shape), "dp", split_axis=0, concat_axis=0, tiled=True
    )
    home_grad = lax.all_to_all(
        back_grad.reshape(shape), "dp", split_axis=0, concat_axis=0, tiled=True
    )
    block_rows = min(row_count, 256)
    block_out = take_rows(slot_of, home_out.reshape(slot_total, narrow), block_rows, bf16)
    tokens_grad = take_rows(slot_of, home_grad.reshape(slot_total, narrow), block_rows, f32)
    return (
        block_out,
        tokens_grad,
        total_gain_one,
        total_in.astype(f32),
        total_conv,
        total_out.astype(f32),
        total_gain_two,
        total_gate.astype(f32),
        total_up.astype(f32),
        total_down.astype(f32),
    )


def solution(mesh):
    in_specs = (
        P("dp", "mp"),
        P("dp", "mp"),
        P("dp"),
        P("dp", None),
        P(),
        P(None, None, "mp"),
        P(None, "mp"),
        P("mp", None),
        P(),
        P(None, "mp"),
        P(None, "mp"),
        P("mp", None),
    )
    out_specs = (
        P("dp", "mp"),
        P("dp", "mp"),
        P(),
        P(None, None, "mp"),
        P(None, "mp"),
        P("mp", None),
        P(),
        P(None, "mp"),
        P(None, "mp"),
        P("mp", None),
    )
    return jax.shard_map(
        on_device, mesh=mesh, in_specs=in_specs, out_specs=out_specs, check_vma=False
    )
```

```python
import jax
import jax.numpy as jnp
from jax import lax
from jax.experimental import pallas as pl
from jax.experimental.pallas import tpu as pltpu
from jax.sharding import PartitionSpec as P

epsilon = 1e-05
f32 = jnp.float32
bf16 = jnp.bfloat16
halo = 8
spare = 8
big_vmem = pltpu.CompilerParams(vmem_limit_bytes=58 << 20)


def cost(flops, moved, transcendentals=0):
    return pl.CostEstimate(
        flops=int(flops), bytes_accessed=int(moved), transcendentals=int(transcendentals)
    )


def lag_rows(values, shift):
    return jnp.concatenate(
        [jnp.zeros((shift, values.shape[1]), values.dtype), values[:-shift]], axis=0
    )


def lead_rows(values, shift):
    return jnp.concatenate(
        [values[shift:], jnp.zeros((shift, values.shape[1]), values.dtype)], axis=0
    )


def seq_masks(lengths, positions, row_count):
    count = lengths.shape[0]
    before = jnp.arange(count)[:, None] < jnp.arange(count)[None, :]
    starts = jnp.sum(jnp.where(before, lengths[:, None], 0), axis=0, dtype=jnp.int32)
    started = positions[:, None] >= starts[None, :]
    seq_first = jnp.max(jnp.where(started, starts[None, :], 0), axis=1)
    offset = positions - seq_first
    inside = (positions >= 0) & (positions < row_count)
    return (
        ((offset >= 1) & inside).astype(f32)[:, None],
        ((offset >= 2) & inside).astype(f32)[:, None],
    )


def nt_dot(left, right):
    return lax.dot_general(
        left, right, (((1,), (1,)), ((), ())), preferred_element_type=f32
    )


def tn_dot(left, right):
    return lax.dot_general(
        left, right, (((0,), (0,)), ((), ())), preferred_element_type=f32
    )


def rank_kernel(rows, members, slots, route_ref, slot_ref):
    target = route_ref[...] // rows
    width = min(rows, 512)
    owner = lax.broadcasted_iota(jnp.int32, (members, rows), 0)
    one_hot = jnp.where(owner == target, 1.0, 0.0)
    left = one_hot.astype(bf16)
    for start in range(0, rows, width):
        first = lax.broadcasted_iota(jnp.int32, (rows, width), 0)
        second = lax.broadcasted_iota(jnp.int32, (rows, width), 1) + start
        earlier = jnp.where(first < second, 1.0, 0.0).astype(bf16)
        rank = jnp.dot(left, earlier, preferred_element_type=f32)
        piece = one_hot[:, start : start + width]
        mine = jnp.sum(rank * piece, axis=0, keepdims=True).astype(jnp.int32)
        slot_ref[:, start : start + width] = (
            target[:, start : start + width] * slots + mine
        )


def pack_kernel(rows, members, slots, route_ref, x_ref, sx_ref, digit_ref, slot_ref):
    step = pl.program_id(0)
    group = sx_ref.shape[0]

    @pl.when(step == 0)
    def _():
        rank_kernel(rows, members, slots, route_ref, slot_ref)

    place = route_ref[...] % rows
    row = lax.broadcasted_iota(jnp.int32, (8, rows), 0)
    digits = jnp.where(
        row == 0,
        (place // 64).astype(f32),
        jnp.where(row == 1, (place % 64).astype(f32), 1.0),
    ).astype(bf16)
    ids = lax.broadcasted_iota(jnp.int32, (group * slots, rows), 0)
    pick = jnp.where(slot_ref[...] == ids + step * group * slots, 1.0, 0.0).astype(bf16)
    sent = jnp.dot(pick, x_ref[...], preferred_element_type=f32).astype(bf16)
    for k in range(group):
        here = slice(k * slots, (k + 1) * slots)
        sx_ref[k, 0:slots] = sent[here]
        coded = nt_dot(digits, pick[here]).astype(bf16)
        if sx_ref.shape[1] > slots:
            sx_ref[k, slots : slots + spare] = jnp.zeros((spare, sx_ref.shape[2]), bf16)
            sx_ref[k, slots : slots + spare, 0:slots] = coded
        else:
            digit_ref[k] = jnp.zeros(digit_ref.shape[1:], bf16)
            digit_ref[k, :, 0:slots] = coded


def pack(route, tokens, members, slots):
    rows, width = tokens.shape
    group = min(members, 4)
    inside = slots <= width
    span = slots + spare if inside else slots
    whole = lambda j: (0, 0)
    block = lambda *tail: pl.BlockSpec((group, *tail), lambda j: (j, 0, 0))
    lanes = 8 if inside else 256
    return pl.pallas_call(
        lambda *refs: pack_kernel(rows, members, slots, *refs),
        grid=(members // group,),
        in_specs=[pl.BlockSpec((1, rows), whole), pl.BlockSpec((rows, width), whole)],
        out_specs=[block(span, width), block(8, lanes), pl.BlockSpec((1, rows), whole)],
        out_shape=[
            jax.ShapeDtypeStruct((members, span, width), bf16),
            jax.ShapeDtypeStruct((members, 8, lanes), bf16),
            jax.ShapeDtypeStruct((1, rows), jnp.int32),
        ],
        compiler_params=big_vmem,
        cost_estimate=cost(2 * members * slots * rows * width, 5 * rows * width),
        name="pack",
    )(route.reshape(1, rows), tokens)


def send_kernel(slots, slot_ref, x_ref, out_ref):
    group = out_ref.shape[0]
    count = group * slots
    ids = lax.broadcasted_iota(jnp.int32, (count, x_ref.shape[0]), 0)
    pick = jnp.where(slot_ref[...] == ids + pl.program_id(0) * count, 1.0, 0.0)
    sent = jnp.dot(pick.astype(bf16), x_ref[...], preferred_element_type=f32)
    for k in range(group):
        out_ref[k] = sent[k * slots : (k + 1) * slots].astype(bf16)


def send_rows(slot_of, source, members, slots):
    rows, width = source.shape
    group = min(members, 8)
    return pl.pallas_call(
        lambda *refs: send_kernel(slots, *refs),
        grid=(members // group,),
        in_specs=[
            pl.BlockSpec((1, rows), lambda j: (0, 0)),
            pl.BlockSpec((rows, width), lambda j: (0, 0)),
        ],
        out_specs=pl.BlockSpec((group, slots, width), lambda j: (j, 0, 0)),
        out_shape=jax.ShapeDtypeStruct((members, slots, width), bf16),
        compiler_params=big_vmem,
        cost_estimate=cost(2 * members * slots * rows * width, 5 * rows * width),
        name="send_rows",
    )(slot_of, source)


def place_kernel(rows, bases_ref, digit_ref, got_ref, out_ref, place_ref, src, pick):
    members, slots = got_ref.shape[0], got_ref.shape[1]
    count = out_ref.shape[0]
    span = src.shape[0] // members
    base = bases_ref[pl.program_id(0)]
    ids = lax.broadcasted_iota(jnp.int32, (count, span), 0) + base

    @pl.when(pl.program_id(0) == 0)
    def _():
        for j in range(members):
            src[j * span : j * span + slots] = got_ref[j]
            if span > slots:
                src[j * span + slots : (j + 1) * span] = jnp.zeros(
                    (span - slots, src.shape[1]), bf16
                )

    for j in range(members):
        coded = digit_ref[j].astype(f32)[:, 0:span]
        value = coded[0:1] * 64.0 + coded[1:2]
        places = jnp.where(coded[2:3] > 0.5, value, 4.0 * rows).astype(jnp.int32)
        pick[:, j * span : (j + 1) * span] = jnp.where(places == ids, 1.0, 0.0).astype(bf16)
        place_ref[j : j + 1, :] = places[:, 0:slots]
    out_ref[...] = jnp.dot(pick[...], src[...], preferred_element_type=f32).astype(bf16)


def place_rows(bases, digits, got, slots, rows, count):
    members, width = got.shape[0], got.shape[2]
    at = digits.shape[1] // 8 - 1
    span = -(-slots // 128) * 128
    return pl.pallas_call(
        lambda *refs: place_kernel(rows, *refs),
        grid_spec=pltpu.PrefetchScalarGridSpec(
            num_scalar_prefetch=1,
            grid=(bases.shape[0],),
            in_specs=[
                pl.BlockSpec((members, 8, digits.shape[2]), lambda i, b: (0, at, 0)),
                pl.BlockSpec((members, slots, width), lambda i, b: (0, 0, 0)),
            ],
            out_specs=[
                pl.BlockSpec((None, count, width), lambda i, b: (i, 0, 0)),
                pl.BlockSpec((members, slots), lambda i, b: (0, 0)),
            ],
            scratch_shapes=[
                pltpu.VMEM((members * span, width), bf16),
                pltpu.VMEM((count, members * span), bf16),
            ],
        ),
        out_shape=[
            jax.ShapeDtypeStruct((bases.shape[0], count, width), bf16),
            jax.ShapeDtypeStruct((members, slots), jnp.int32),
        ],
        compiler_params=big_vmem,
        cost_estimate=cost(0, (bases.shape[0] * count + members * slots) * width // 8),
        name="place_rows",
    )(bases, digits, got)


def take_kernel(ids_ref, from_ref, out_ref):
    cols = lax.broadcasted_iota(jnp.int32, (out_ref.shape[0], from_ref.shape[0]), 1)
    pick = jnp.where(ids_ref[...] == cols, 1.0, 0.0).astype(bf16)
    out_ref[...] = jnp.dot(pick, from_ref[...], preferred_element_type=f32).astype(
        out_ref.dtype
    )


def take_rows(ids, source, block, dtype):
    count = ids.shape[0]
    total, width = source.shape
    return pl.pallas_call(
        take_kernel,
        grid=(count // block,),
        in_specs=[
            pl.BlockSpec((block, 1), lambda i: (i, 0)),
            pl.BlockSpec((total, width), lambda i: (0, 0)),
        ],
        out_specs=pl.BlockSpec((block, width), lambda i: (i, 0)),
        out_shape=jax.ShapeDtypeStruct((count, width), dtype),
        compiler_params=big_vmem,
        cost_estimate=cost(2 * count * total * width, 2 * (count + total) * width),
        name="take_rows",
    )(ids, source)


def swap_mp(value):
    return lax.ppermute(value, "mp", [(0, 1), (1, 0)])


def side_by_side(mine, other, index):
    return jnp.where(
        index == 0,
        jnp.concatenate([mine, other], axis=1),
        jnp.concatenate([other, mine], axis=1),
    )


def rolled(full, shift):
    return jnp.roll(full, shift, axis=0)


def flip(value, bit):
    size = lax.axis_size("dp")
    return lax.ppermute(value, "dp", [(i, i ^ bit) for i in range(size)])


def dp_bits():
    return [1 << k for k in range(lax.axis_size("dp").bit_length() - 1)]


def halve(value, bit):
    half = value.shape[0] // 2
    side = (lax.axis_index("dp") // bit) % 2
    sent = lax.dynamic_slice_in_dim(value, (1 - side) * half, half, 0)
    kept = lax.dynamic_slice_in_dim(value, side * half, half, 0)
    return (kept.astype(f32) + flip(sent, bit).astype(f32)).astype(bf16)


def double(value, bit):
    side = (lax.axis_index("dp") // bit) % 2
    other = flip(value, bit)
    return jnp.where(
        side == 0,
        jnp.concatenate([value, other], axis=0),
        jnp.concatenate([other, value], axis=0),
    )


def sum_dp(value):
    bits = dp_bits()
    for bit in bits:
        value = halve(value, bit)
    for bit in reversed(bits):
        value = double(value, bit)
    return value


def after(value, *others):
    return lax.optimization_barrier((value, *others))[0]


class Ring:
    def __init__(self, parts):
        self.parts = parts
        self.nodes = nodes = lax.axis_size("dp") // 2
        chip = lax.axis_index("dp") // 2
        self.here = jnp.where(chip % 2 == 0, chip // 2, nodes - 1 - chip // 2)
        top = nodes // 2
        self.chips = [2 * p if p < top else 2 * (nodes - 1 - p) + 1 for p in range(nodes)]
        self.half = parts[0].shape[1] // 2
        self.held = {way: self.terms(self.here, way).astype(bf16) for way in (1, -1)}
        self.pieces = {1: [], -1: []}
        self.steps = 0

    def send(self, value, way):
        pairs = [
            (2 * self.chips[p] + c, 2 * self.chips[(p + way) % self.nodes] + c)
            for p in range(self.nodes)
            for c in range(2)
        ]
        return lax.ppermute(value, "dp", pairs)

    def terms(self, block, way):
        at = (block % self.nodes, 0 if way == 1 else self.half, 0)
        size = (1, self.half, self.parts[0].shape[2])
        pieces = [lax.dynamic_slice(v, at, size) for v in self.parts]
        return sum(piece.astype(f32) for piece in pieces)

    def step(self, *gates):
        count = self.steps
        if count == 2 * self.nodes - 2:
            return
        self.steps += 1
        adding = count < self.nodes - 1
        if gates:
            both = lax.optimization_barrier((self.held[1], self.held[-1], *gates))
            self.held = {1: both[0], -1: both[1]}
        for way in (1, -1):
            if count == self.nodes - 1:
                self.pieces[way].append(self.held[way])
            came = self.send(self.held[way], way)
            if adding:
                own = self.terms(self.here - way * (count + 1) + self.nodes, way)
                came = (came.astype(f32) + own).astype(bf16)
            else:
                self.pieces[way].append(came)
            self.held[way] = came

    def first(self, value):
        return after(value, *self.held.values())

    def total(self):
        return gather_pieces([p[0] for way in (1, -1) for p in self.pieces[way]])

    def order(self):
        block = jnp.arange(self.nodes, dtype=jnp.int32)
        up = (self.here + 1 - block + self.nodes) % self.nodes
        down = (block - self.here + 1 + self.nodes) % self.nodes + self.nodes
        core = lax.axis_index("dp")[None] % 2
        return jnp.concatenate([up, down, core]).astype(jnp.int32)


def gather_kernel(*refs):
    *sources, out_ref = refs
    for k, ref in enumerate(sources):
        out_ref[k] = ref[...]


def gather_pieces(pieces):
    count = len(pieces)
    vmem = pl.BlockSpec(memory_space=pltpu.VMEM)
    return pl.pallas_call(
        gather_kernel,
        in_specs=[vmem] * count,
        out_specs=vmem,
        out_shape=jax.ShapeDtypeStruct((count, *pieces[0].shape), bf16),
        compiler_params=big_vmem,
        cost_estimate=cost(0, 4 * count * pieces[0].size),
        name="gather_pieces",
    )(*pieces)


def core_parts(value):
    count = value.shape[0] // 2
    core = lax.axis_index("dp") % 2
    sent = lax.dynamic_slice_in_dim(value, (1 - core) * count, count, 0)
    kept = lax.dynamic_slice_in_dim(value, core * count, count, 0)
    return kept, flip(sent, 1)


def ff_kernel(sub, x_ref, g_ref, wg_ref, wu_ref, wd_ref, gx_ref, y_ref, h_ref, gg_ref, gu_ref):
    step = pl.program_id(0)
    for at in range(0, wg_ref.shape[1], sub):
        c = slice(at, at + sub)
        gate = jnp.dot(x_ref[...], wg_ref[:, c], preferred_element_type=f32)
        up = jnp.dot(x_ref[...], wu_ref[:, c], preferred_element_type=f32)
        grad = nt_dot(g_ref[...], wd_ref[c])
        sig = 1.0 / (1.0 + jnp.exp(-gate))
        silu = gate * sig
        h_ref[:, c] = (silu * up).astype(bf16)
        gg_ref[:, c] = (grad * up * (sig + silu * (1.0 - sig))).astype(bf16)
        gu_ref[:, c] = (grad * silu).astype(bf16)
    def back(first):
        w = 256
        for at in range(0, gx_ref.shape[1], w):
            c = slice(at, at + w)
            gx = nt_dot(gg_ref[...], wg_ref[c, :]) + nt_dot(gu_ref[...], wu_ref[c, :])
            y = jnp.dot(h_ref[...], wd_ref[:, c], preferred_element_type=f32)
            if first:
                gx_ref[:, c] = gx
                y_ref[:, c] = y
            else:
                gx_ref[:, c] += gx
                y_ref[:, c] += y
    pl.when(step == 0)(lambda: back(True))
    pl.when(step > 0)(lambda: back(False))

def feed_forward(x, g, wg, wu, wd, sub=384):
    r, d = x.shape
    hid = wg.shape[1]
    chunk = hid // 3
    whole = pl.BlockSpec((r, d), lambda i: (0, 0))
    tall = pl.BlockSpec((d, chunk), lambda i: (0, i))
    wide = pl.BlockSpec((r, chunk), lambda i: (0, i))
    return pl.pallas_call(
        lambda *refs: ff_kernel(sub, *refs),
        grid=(hid // chunk,),
        in_specs=[
            whole,
            whole,
            tall,
            tall,
            pl.BlockSpec((chunk, d), lambda i: (i, 0)),
        ],
        out_specs=[whole, whole, wide, wide, wide],
        out_shape=[jax.ShapeDtypeStruct((r, d), f32)] * 2 + [jax.ShapeDtypeStruct((r, hid), bf16)] * 3,
        compiler_params=big_vmem,
        cost_estimate=cost(24 * r * d * hid, 6 * (d + r) * hid + 12 * r * d, 2 * r * hid),
        name="feed_forward",
    )(x, g, wg, wu, wd)

def grads_kernel(x0, x1, gg0, gg1, gu0, gu1, h0, h1, g0, g1, out_ref, xt, ht):
    step = pl.program_id(0)
    nodes, count, lanes = out_ref.shape
    rows = x0.shape[1] // nodes
    deep = h0.shape[1] // nodes
    r = x0.shape[0]
    @pl.when(step == 0)
    def _():
        xt[:, :r] = x0[...].T
        xt[:, r:] = x1[...].T
    @pl.when(step == 5)
    def _():
        ht[:, :r] = h0[...].T
        ht[:, r:] = h1[...].T
    def put(c, d, at):
        v = jnp.dot(xt[:, :r], c[...], preferred_element_type=f32) + jnp.dot(xt[:, r:], d[...], preferred_element_type=f32)
        out_ref[:, pl.ds(pl.multiple_of(at, 64), rows)] = v.astype(bf16).reshape(nodes, rows, lanes)
    @pl.when(step < 3)
    def _(): put(gg0, gg1, step * rows)
    @pl.when((step >= 3) & (step < 6))
    def _(): put(gu0, gu1, step * rows)
    @pl.when(step == 6)
    def _():
        v = jnp.dot(ht[:, :r], g0[:, :lanes], preferred_element_type=f32) + jnp.dot(ht[:, r:], g1[:, :lanes], preferred_element_type=f32)
        out_ref[:, 6 * rows : 6 * rows + deep] = v.astype(bf16).reshape(nodes, deep, lanes)
        v = jnp.dot(ht[:, :r], g0[:, lanes:], preferred_element_type=f32) + jnp.dot(ht[:, r:], g1[:, lanes:], preferred_element_type=f32)
        v = v.astype(bf16).reshape(nodes, deep, v.shape[1])
        short, rest = deep // 3, v.shape[2]
        for k in range(3):
            out_ref[:, 6 * rows + deep :, k * rest : (k + 1) * rest] = v[:, k * short : (k + 1) * short]

def ff_grads(side, nodes, x0, x1, gg0, gg1, gu0, gu1, h0, h1, g0, g1):
    r, d = x0.shape
    hid = gg0.shape[1]
    lanes = hid // 3
    rows, deep = d // (2 * nodes), hid // (2 * nodes)
    count = 6 * rows + deep + deep // 3
    half = lambda n: pl.BlockSpec((r, n), lambda i, s: (0, s[0]))
    first = pl.BlockSpec((r, lanes), lambda i, s: (0, jnp.minimum(i, 2)))
    second = pl.BlockSpec((r, lanes), lambda i, s: (0, jnp.clip(i - 3, 0, 2)))
    whole = pl.BlockSpec((r, d), lambda i, s: (0, 0))
    return pl.pallas_call(
        lambda s, *refs: grads_kernel(*refs),
        grid_spec=pltpu.PrefetchScalarGridSpec(
            num_scalar_prefetch=1, grid=(7,),
            in_specs=[half(d // 2)] * 2 + [first] * 2 + [second] * 2 + [half(hid // 2)] * 2 + [whole] * 2,
            out_specs=pl.BlockSpec((nodes, count, lanes), lambda i, s: (0, 0, 0)),
            scratch_shapes=[pltpu.VMEM((d // 2, 2 * r), bf16), pltpu.VMEM((hid // 2, 2 * r), bf16)],
        ),
        out_shape=jax.ShapeDtypeStruct((nodes, count, lanes), bf16),
        compiler_params=big_vmem,
        cost_estimate=cost(12 * r * d * hid, 6 * r * hid + 5 * d * hid),
        name="ff_grads",
    )(side.astype(jnp.int32).reshape(1), x0, x1, gg0, gg1, gu0, gu1, h0, h1, g0, g1)


def open_specs(nodes, group, half, lanes):
    specs = []
    for _ in range(2):
        for b in range(group):
            for at in (0, nodes):
                specs.append(
                    pl.BlockSpec(
                        (None, half, lanes),
                        lambda j, h, order, b=b, at=at: (order[at + j * group + b], 0, 0),
                    )
                )
    return specs


def open_blocks(group, order_ref, refs, write):
    core = order_ref[order_ref.shape[0] - 1]
    half = refs[0].shape[0]

    def reader(first, second):
        def read(start, stop):
            if stop <= half:
                return first[start:stop].astype(f32)
            if start >= half:
                return second[start - half : stop - half].astype(f32)
            pieces = [first[start:half], second[0 : stop - half]]
            return jnp.concatenate([p.astype(f32) for p in pieces], axis=0)

        return read

    def hand(refs):
        for b in range(group):
            write(b, reader(refs[2 * b], refs[2 * b + 1]))

    own = pl.program_id(1) == core
    pl.when(own)(lambda: hand(refs[: 2 * group]))
    pl.when(jnp.logical_not(own))(lambda: hand(refs[2 * group :]))


def open_ff_kernel(group, order_ref, *refs):
    *pieces, gate_ref, up_ref, down_ref = refs
    lanes = pieces[0].shape[1]
    rows, deep = gate_ref.shape[0] // group, down_ref.shape[0] // group
    rest = down_ref.shape[1] - lanes
    short = deep // 3

    def write(b, read):
        here = slice(b * rows, (b + 1) * rows)
        for k, out in enumerate((gate_ref, up_ref)):
            for c in range(3):
                part = read((3 * k + c) * rows, (3 * k + c + 1) * rows)
                out[here, c * lanes : (c + 1) * lanes] = part
        low, at = b * deep, 6 * rows
        down_ref[low : low + deep, :lanes] = read(at, at + deep)
        for c in range(3):
            part = read(at + deep, at + deep + short)[:, c * rest : (c + 1) * rest]
            down_ref[low + c * short : low + (c + 1) * short, lanes:] = part

    open_blocks(group, order_ref, pieces, write)


def open_ff(ring, width, hidden):
    mine = ring.total()
    other = flip(mine, 1)
    _, half, lanes = mine.shape
    nodes, group = ring.nodes, 2
    steps = nodes // group
    rows, deep = width // (2 * nodes), hidden // (2 * nodes)
    out = lambda tall, wide: pl.BlockSpec(
        (group * tall, wide), lambda j, h, order: (h * steps + j, 0)
    )
    return pl.pallas_call(
        lambda *refs: open_ff_kernel(group, *refs),
        grid_spec=pltpu.PrefetchScalarGridSpec(
            num_scalar_prefetch=1,
            grid=(steps, 2),
            in_specs=open_specs(nodes, group, half, lanes),
            out_specs=[out(rows, hidden), out(rows, hidden), out(deep, width)],
        ),
        out_shape=[
            jax.ShapeDtypeStruct((width, hidden), f32),
            jax.ShapeDtypeStruct((width, hidden), f32),
            jax.ShapeDtypeStruct((hidden, width), f32),
        ],
        compiler_params=big_vmem,
        cost_estimate=cost(0, 24 * width * hidden),
        name="open_ff",
    )(ring.order(), *[mine] * (2 * group), *[other] * (2 * group))


def pack_conv_kernel(in_ref, out_w_ref, tail_ref, out_ref):
    blocks = out_ref.shape[0]
    rows = in_ref.shape[0] // (2 * blocks)
    deep = out_w_ref.shape[0] // blocks
    lanes = in_ref.shape[1]
    for k in range(blocks):
        out_ref[k, 0:rows, 0:lanes] = in_ref[2 * k * rows : (2 * k + 1) * rows]
        out_ref[k, 0:rows, lanes:] = in_ref[(2 * k + 1) * rows : (2 * k + 2) * rows]
        out_ref[k, rows : rows + deep] = out_w_ref[k * deep : (k + 1) * deep]
        out_ref[k, rows + deep :] = tail_ref[...]


def pack_conv(grad_in, grad_out, tail, blocks):
    total, lanes = grad_in.shape
    rows, deep, spared = total // blocks, grad_out.shape[0] // blocks, tail.shape[0]
    count = rows // 2 + deep + spared
    return pl.pallas_call(
        pack_conv_kernel,
        grid=(4,),
        in_specs=[
            pl.BlockSpec((total // 4, lanes), lambda i: (i, 0)),
            pl.BlockSpec((grad_out.shape[0] // 4, 2 * lanes), lambda i: (i, 0)),
            pl.BlockSpec((spared, 2 * lanes), lambda i: (0, 0)),
        ],
        out_specs=pl.BlockSpec((blocks // 4, count, 2 * lanes), lambda i: (i, 0, 0)),
        out_shape=jax.ShapeDtypeStruct((blocks, count, 2 * lanes), bf16),
        compiler_params=big_vmem,
        cost_estimate=cost(0, 4 * (grad_in.size + grad_out.size)),
        name="pack_conv",
    )(grad_in, grad_out, tail)


def open_conv_kernel(group, order_ref, *refs):
    *pieces, in_ref, out_w_ref, tail_ref = refs
    rows, lanes = in_ref.shape[0] // (2 * group), in_ref.shape[1]
    deep = out_w_ref.shape[0] // group

    def write(b, read):
        low = 2 * b * rows
        in_ref[low : low + rows] = read(0, rows)[:, :lanes]
        in_ref[low + rows : low + 2 * rows] = read(0, rows)[:, lanes:]
        out_w_ref[b * deep : (b + 1) * deep] = read(rows, rows + deep)
        tail_ref[b] = read(rows + deep, rows + deep + tail_ref.shape[1])

    open_blocks(group, order_ref, pieces, write)


def open_conv(ring, gate, total, deep_total):
    mine = after(ring.total(), gate)
    other = flip(mine, 1)
    _, half, width = mine.shape
    nodes, group = ring.nodes, ring.nodes // 2
    blocks = 2 * nodes
    steps = nodes // group
    rows, deep = total // blocks, deep_total // blocks
    spared = 2 * half - rows // 2 - deep
    at = lambda j, h, order: (h * steps + j, 0)
    return pl.pallas_call(
        lambda *refs: open_conv_kernel(group, *refs),
        grid_spec=pltpu.PrefetchScalarGridSpec(
            num_scalar_prefetch=1,
            grid=(steps, 2),
            in_specs=open_specs(nodes, group, half, width),
            out_specs=[
                pl.BlockSpec((group * rows, width // 2), at),
                pl.BlockSpec((group * deep, width), at),
                pl.BlockSpec(
                    (group, spared, width), lambda j, h, order: (h * steps + j, 0, 0)
                ),
            ],
        ),
        out_shape=[
            jax.ShapeDtypeStruct((total, width // 2), f32),
            jax.ShapeDtypeStruct((deep_total, width), f32),
            jax.ShapeDtypeStruct((blocks, spared, width), f32),
        ],
        compiler_params=big_vmem,
        cost_estimate=cost(0, 8 * (total + deep_total) * width),
        name="open_conv",
    )(ring.order(), *[mine] * (2 * group), *[other] * (2 * group))


def on_device(
    tokens,
    cotangent,
    route,
    seq_lengths,
    norm1_gain,
    in_weight,
    conv_weight,
    out_weight,
    norm2_gain,
    gate_weight,
    up_weight,
    down_weight,
):
    dp_size = lax.axis_size("dp")
    mp_size = lax.axis_size("mp")
    dp_index = lax.axis_index("dp")
    mp_index = lax.axis_index("mp")
    rows = tokens.shape[0]
    narrow = tokens.shape[1]
    width = norm1_gain.shape[0]
    own = rows // mp_size
    start = mp_index * own
    column = mp_index * narrow
    pair_share = rows // dp_size
    slots = pair_share + pair_share // 2
    paired = mp_size == 2

    if paired:
        core = dp_index % 2
        deep = width // 2
        part_in = lax.dynamic_slice_in_dim(in_weight, core * deep, deep, 1)
        part_out = lax.dynamic_slice_in_dim(out_weight, core * deep, deep, 1)
        part = jnp.concatenate([part_in, part_out.reshape(1, deep, deep)], axis=0)
        there = swap_mp(part)
        route = after(route, part)
        taps = jnp.concatenate([conv_weight, swap_mp(conv_weight)], axis=1)
    else:
        full_in = lax.all_gather(in_weight, "mp", axis=2, tiled=True)
        full_out = lax.all_gather(out_weight, "mp", axis=0, tiled=True)
        taps = lax.all_gather(conv_weight, "mp", axis=1, tiled=True)

    sent_rows, digits, slot_of = pack(route, tokens, dp_size, slots)
    sent_seeds = send_rows(after(slot_of, sent_rows), cotangent, dp_size, slots)
    over = dict(split_axis=0, concat_axis=0, tiled=True)
    got_rows = lax.all_to_all(sent_rows, "dp", **over)
    digits = got_rows if slots <= narrow else lax.all_to_all(digits, "dp", **over)
    got_rows, sent_seeds = lax.optimization_barrier((got_rows, sent_seeds))
    got_seeds = lax.all_to_all(sent_seeds, "dp", **over)
    slot_of = slot_of.reshape(rows, 1)
    window = own + 2 * halo
    if paired:
        bases = jnp.stack([start, own - start]).astype(jnp.int32)
        digits = got_rows if slots <= narrow else digits
        pieces, places = place_rows(bases - halo, digits, got_rows, slots, rows, window)
        there, _ = lax.optimization_barrier((there, pieces))
        here = flip(there, 1)
        both = [jnp.where(core == k, there, here) for k in range(2)]
        other_in = jnp.concatenate([v[:3] for v in both], axis=1)
        other_out = jnp.concatenate([v[3] for v in both], axis=1)
        full_in = jnp.concatenate([in_weight, other_in], axis=2)
        full_out = jnp.concatenate([out_weight, other_out], axis=0)
        input_rows = side_by_side(pieces[0], swap_mp(pieces[1]), mp_index)
        pieces, _ = place_rows(bases, digits, got_seeds, slots, rows, own)
        input_rows = after(input_rows, pieces)
        came = swap_mp(pieces[1])
        seeds_own = side_by_side(pieces[0], came, mp_index)
        seeds_other = side_by_side(pieces[1], swap_mp(after(pieces[0], came)), mp_index)
        place_ids = ((places - start) % rows).reshape(-1, 1)
    else:
        bases = (jnp.arange(mp_size) * own).astype(jnp.int32)
        pieces, places = place_rows(bases, digits, got_rows, slots, rows, own)
        full = lax.all_gather(pieces.reshape(rows, narrow), "mp", axis=1, tiled=True)
        full = jnp.pad(full, ((halo, halo), (0, 0)))
        input_rows = lax.dynamic_slice_in_dim(full, start, window, 0)
        pieces, _ = place_rows(bases, digits, got_seeds, slots, rows, own)
        full = lax.all_gather(pieces.reshape(rows, narrow), "mp", axis=1, tiled=True)
        seeds = rolled(full, -start)
        seeds_own, seeds_other = seeds[:own], seeds[own:]
        place_ids = places.reshape(-1, 1)

    positions = start - halo + jnp.arange(window, dtype=jnp.int32)
    first_mask, second_mask = seq_masks(seq_lengths[0], positions, rows)
    residual = input_rows.astype(f32)
    scale_one = lax.rsqrt(jnp.mean(residual * residual, axis=1) + epsilon)[:, None]
    normed_one = (residual * scale_one * norm1_gain).astype(bf16)
    projected = jnp.einsum("rd,kdc->krc", normed_one, full_in, preferred_element_type=f32)
    in_gate, out_gate, value_part = (projected[0], projected[1], projected[2])
    mixed = in_gate * value_part
    lag_one = lag_rows(mixed, 1) * first_mask
    lag_two = lag_rows(mixed, 2) * second_mask
    convolved = taps[2] * mixed + taps[1] * lag_one + taps[0] * lag_two
    gated = (out_gate * convolved).astype(bf16)
    gated = after(gated, seeds_own)
    middle = (residual + jnp.dot(gated, full_out, preferred_element_type=f32))[halo:]
    scale_two = lax.rsqrt(jnp.mean(middle * middle, axis=1) + epsilon)[:, None]
    normed_own = (middle[:own] * scale_two[:own] * norm2_gain).astype(bf16)

    weights = (gate_weight, up_weight, down_weight)
    if paired:
        normed_other = swap_mp(normed_own)
        first = feed_forward(normed_own, seeds_own, *weights)
        second = feed_forward(normed_other, seeds_other, *weights)
        sent = jnp.concatenate([second[0], first[0][:halo]], axis=0).astype(bf16)
        came = swap_mp(sent)
        saved = (normed_other, first[3], second[3], first[4], second[4])
        saved += (first[2], second[2], seeds_own, seeds_other)
        away = ff_grads(1 - core, dp_size // 2, after(normed_own, sent), *saved)
        kept = ff_grads(core, dp_size // 2, after(normed_own, away), *saved)
        away = flip(away, 1)
        came, _ = lax.optimization_barrier((came, kept))
        grad_normed_two = jnp.concatenate([first[0], second[0][:halo]], axis=0)
        grad_normed_two = grad_normed_two + came.astype(f32)
        down_came = swap_mp(after(second[1].astype(bf16), came))
        ring = Ring((kept, away))
        grad_normed_two = ring.first(grad_normed_two)
        ring.step()
    else:
        normed_two = rolled(lax.all_gather(normed_own, "mp", axis=0, tiled=True), -start)
        gate_val = jnp.dot(normed_two, gate_weight, preferred_element_type=f32)
        up_val = jnp.dot(normed_two, up_weight, preferred_element_type=f32)
        sigmoid_val = jax.nn.sigmoid(gate_val)
        silu_val = gate_val * sigmoid_val
        hidden = (silu_val * up_val).astype(bf16)
        grad_hidden = nt_dot(seeds, down_weight)
        grad_gate_val = (
            grad_hidden * up_val * sigmoid_val * (1.0 + gate_val * (1.0 - sigmoid_val))
        ).astype(bf16)
        grad_up_val = (grad_hidden * silu_val).astype(bf16)
        normed_terms = nt_dot(grad_gate_val, gate_weight) + nt_dot(grad_up_val, up_weight)
        down_terms = jnp.dot(hidden, down_weight, preferred_element_type=f32)
        full = rolled(lax.psum(rolled(normed_terms, start), "mp"), -start)
        grad_normed_two = full[: own + halo]
        down_sum = rolled(lax.psum(rolled(down_terms, start), "mp"), -start)[:own]
        total_gate = sum_dp(tn_dot(normed_two, grad_gate_val).astype(bf16)).astype(f32)
        total_up = sum_dp(tn_dot(normed_two, grad_up_val).astype(bf16)).astype(f32)
        total_down = sum_dp(tn_dot(hidden, seeds).astype(bf16)).astype(f32)

    gain_two_term = jnp.sum((grad_normed_two * middle * scale_two)[:own], axis=0)
    dot_two = jnp.sum(norm2_gain * grad_normed_two * middle, axis=1, keepdims=True)
    grad_middle = (
        jnp.concatenate([seeds_own, seeds_other[:halo]], axis=0).astype(f32)
        + scale_two * norm2_gain * grad_normed_two
        - middle * (scale_two * scale_two * scale_two * dot_two / width)
    )
    grad_mix = grad_middle.astype(bf16)
    grad_gated = jnp.einsum("rd,cd->rc", grad_mix, full_out, preferred_element_type=f32)
    if paired:
        grad_gated = ring.first(grad_gated)
        ring.step()
    grad_conv = grad_gated * out_gate[halo:]
    inner = slice(halo, halo + own)
    conv_terms = jnp.stack(
        [
            jnp.sum(grad_conv[:own] * lag_two[inner], axis=0),
            jnp.sum(grad_conv[:own] * lag_one[inner], axis=0),
            jnp.sum(grad_conv[:own] * mixed[inner], axis=0),
        ],
        axis=0,
    )
    grad_mixed = (
        taps[2] * grad_conv
        + taps[1] * lead_rows(grad_conv * first_mask[halo:], 1)
        + taps[0] * lead_rows(grad_conv * second_mask[halo:], 2)
    )[:own]
    grad_parts = jnp.stack(
        [
            grad_mixed * value_part[inner],
            grad_gated[:own] * convolved[inner],
            grad_mixed * in_gate[inner],
        ],
        axis=0,
    ).astype(bf16)
    parts_late = grad_parts
    if paired:
        grad_parts = ring.first(grad_parts)
        ring.step()
        ring.step()
        parts_late = ring.first(grad_parts)
    grad_normed_one = jnp.einsum("krc,kdc->rd", parts_late, full_in, preferred_element_type=f32)
    residual_own = residual[inner]
    scale_own = scale_one[inner]
    gain_one_term = jnp.sum(grad_normed_one * residual_own * scale_own, axis=0)
    dot_one = jnp.sum(norm1_gain * grad_normed_one * residual_own, axis=1, keepdims=True)
    input_own = (
        grad_middle[:own]
        + scale_own * norm1_gain * grad_normed_one
        - residual_own * (scale_own * scale_own * scale_own * dot_one / width)
    ).astype(bf16)

    grad_in = jnp.einsum(
        "rd,krc->kdc", normed_one[inner], grad_parts, preferred_element_type=f32
    ).astype(bf16)
    grad_out = jnp.einsum(
        "rc,rd->cd", gated[inner], grad_mix[:own], preferred_element_type=f32
    ).astype(bf16)
    if paired:
        down_sum = first[1] + after(down_came, grad_parts).astype(f32)
    block_own = (middle[:own] + down_sum).astype(bf16)
    gains = jnp.stack([gain_one_term, gain_two_term], axis=0)
    count = 2 + conv_weight.shape[0]

    def to_features(mine):
        if not paired:
            full = lax.all_gather(mine, "mp", axis=0, tiled=True)
            return lax.dynamic_slice_in_dim(full, column, narrow, 1)
        low, high = mine[:, :narrow], mine[:, narrow:]
        other = swap_mp(jnp.where(mp_index == 0, high, low))
        return jnp.concatenate([jnp.where(mp_index == 0, low, high), other], axis=0)

    shape = (dp_size, slots, narrow)
    back_block = min(8 * slots, slots * dp_size)
    home_block = min(rows, 512)

    def leave(piece):
        back = take_rows(place_ids, piece, back_block, bf16)
        return lax.all_to_all(back.reshape(shape), "dp", **over)

    def arrive(home, dtype):
        return take_rows(slot_of, home.reshape(-1, narrow), home_block, dtype)

    if paired:
        def packed_half(k, parts):
            lanes = slice(k * narrow, (k + 1) * narrow)
            terms = jnp.pad(conv_terms[:, lanes], ((0, 16 - count), (0, width - narrow)))
            ends = jnp.concatenate([gains, terms], axis=0).astype(bf16)
            lane_in = parts[:, :, lanes].reshape(-1, narrow)
            return core_parts(pack_conv(lane_in, grad_out[lanes], ends, dp_size))

        other = packed_half(1, grad_in)
        passed = (other[0].astype(f32) + other[1].astype(f32)).astype(bf16)
        gate_in = ring.first(after(grad_in, passed))
        passed = swap_mp(passed)
        block_piece = to_features(block_own)
        out_home = leave(block_piece)
        ring.step(block_piece)
        mine = packed_half(0, gate_in)
        input_piece = to_features(input_own)
        ring.step()
        ring.step(input_piece)
        grad_home = leave(after(input_piece, out_home))
        ring.step(out_home)
        ring.step(mine[1])
        ring.step()
        ring.step(grad_home)
        second = Ring((*mine, passed))
        while ring.steps < 2 * ring.nodes - 2:
            ring.step(*second.held.values())
            second.step()
        for _ in range(4):
            second.step()
        ring_done = open_ff(ring, width, gate_weight.shape[1])
        total_gate, total_up, total_down = ring_done
        while second.steps < 2 * second.nodes - 3:
            second.step()
        second.step(total_gate)
        total_in, total_out, ends = open_conv(
            second, total_gate, grad_in.size // (2 * narrow), narrow
        )
        tail = ends[0]
    else:
        out_home = leave(to_features(block_own))
        grad_home = leave(to_features(input_own))
        total_in = lax.psum_scatter(
            grad_in.astype(f32), "mp", scatter_dimension=2, tiled=True
        )
        total_in = sum_dp(total_in.astype(bf16).reshape(-1, narrow)).astype(f32)
        total_out = lax.psum_scatter(
            grad_out.astype(f32), "mp", scatter_dimension=0, tiled=True
        )
        total_out = sum_dp(total_out.astype(bf16)).astype(f32)
        gains = lax.psum(gains, ("dp", "mp"))
        terms = lax.psum_scatter(conv_terms, "mp", scatter_dimension=1, tiled=True)
        terms = jnp.pad(lax.psum(terms, "dp"), ((0, 0), (0, width - narrow)))
        tail = jnp.concatenate([gains, terms], axis=0)
    total_taps = tail[2:count, :narrow]
    block_out = arrive(out_home, bf16)
    tokens_grad = arrive(grad_home, f32)
    return (
        block_out,
        tokens_grad,
        tail[0],
        total_in.reshape(in_weight.shape),
        total_taps,
        total_out,
        tail[1],
        total_gate,
        total_up,
        total_down,
    )


def solution(mesh):
    in_specs = (
        P("dp", "mp"),
        P("dp", "mp"),
        P("dp"),
        P("dp", None),
        P(),
        P(None, None, "mp"),
        P(None, "mp"),
        P("mp", None),
        P(),
        P(None, "mp"),
        P(None, "mp"),
        P("mp", None),
    )
    out_specs = (
        P("dp", "mp"),
        P("dp", "mp"),
        P(),
        P(None, None, "mp"),
        P(None, "mp"),
        P("mp", None),
        P(),
        P(None, "mp"),
        P(None, "mp"),
        P("mp", None),
    )
    return jax.shard_map(
        on_device, mesh=mesh, in_specs=in_specs, out_specs=out_specs, check_vma=False
    )
```

```python
import jax
import jax.numpy as jnp
from jax import lax
from jax.experimental import pallas as pl
from jax.experimental.pallas import tpu as pltpu
from jax.sharding import PartitionSpec as P

epsilon = 1e-05
f32 = jnp.float32
bf16 = jnp.bfloat16
halo = 8
spare = 8
big_vmem = pltpu.CompilerParams(vmem_limit_bytes=58 << 20)


def cost(flops, moved, transcendentals=0):
    return pl.CostEstimate(
        flops=int(flops), bytes_accessed=int(moved), transcendentals=int(transcendentals)
    )


def lag_rows(values, shift):
    return jnp.concatenate(
        [jnp.zeros((shift, values.shape[1]), values.dtype), values[:-shift]], axis=0
    )


def lead_rows(values, shift):
    return jnp.concatenate(
        [values[shift:], jnp.zeros((shift, values.shape[1]), values.dtype)], axis=0
    )


def seq_masks(lengths, positions, row_count):
    count = lengths.shape[0]
    before = jnp.arange(count)[:, None] < jnp.arange(count)[None, :]
    starts = jnp.sum(jnp.where(before, lengths[:, None], 0), axis=0, dtype=jnp.int32)
    started = positions[:, None] >= starts[None, :]
    seq_first = jnp.max(jnp.where(started, starts[None, :], 0), axis=1)
    offset = positions - seq_first
    inside = (positions >= 0) & (positions < row_count)
    return (
        ((offset >= 1) & inside).astype(f32)[:, None],
        ((offset >= 2) & inside).astype(f32)[:, None],
    )


def nt_dot(left, right):
    return lax.dot_general(
        left, right, (((1,), (1,)), ((), ())), preferred_element_type=f32
    )


def tn_dot(left, right):
    return lax.dot_general(
        left, right, (((0,), (0,)), ((), ())), preferred_element_type=f32
    )


def rank_kernel(rows, members, slots, route_ref, slot_ref):
    target = route_ref[...] // rows
    width = min(rows, 512)
    owner = lax.broadcasted_iota(jnp.int32, (members, rows), 0)
    one_hot = jnp.where(owner == target, 1.0, 0.0)
    left = one_hot.astype(bf16)
    for start in range(0, rows, width):
        first = lax.broadcasted_iota(jnp.int32, (rows, width), 0)
        second = lax.broadcasted_iota(jnp.int32, (rows, width), 1) + start
        earlier = jnp.where(first < second, 1.0, 0.0).astype(bf16)
        rank = jnp.dot(left, earlier, preferred_element_type=f32)
        piece = one_hot[:, start : start + width]
        mine = jnp.sum(rank * piece, axis=0, keepdims=True).astype(jnp.int32)
        slot_ref[:, start : start + width] = (
            target[:, start : start + width] * slots + mine
        )


def pack_kernel(rows, members, slots, route_ref, x_ref, sx_ref, digit_ref, slot_ref):
    step = pl.program_id(0)
    group = sx_ref.shape[0]

    @pl.when(step == 0)
    def _():
        rank_kernel(rows, members, slots, route_ref, slot_ref)

    place = route_ref[...] % rows
    row = lax.broadcasted_iota(jnp.int32, (8, rows), 0)
    digits = jnp.where(
        row == 0,
        (place // 64).astype(f32),
        jnp.where(row == 1, (place % 64).astype(f32), 1.0),
    ).astype(bf16)
    ids = lax.broadcasted_iota(jnp.int32, (group * slots, rows), 0)
    pick = jnp.where(slot_ref[...] == ids + step * group * slots, 1.0, 0.0).astype(bf16)
    sent = jnp.dot(pick, x_ref[...], preferred_element_type=f32).astype(bf16)
    for k in range(group):
        here = slice(k * slots, (k + 1) * slots)
        sx_ref[k, 0:slots] = sent[here]
        coded = nt_dot(digits, pick[here]).astype(bf16)
        if sx_ref.shape[1] > slots:
            sx_ref[k, slots : slots + spare] = jnp.zeros((spare, sx_ref.shape[2]), bf16)
            sx_ref[k, slots : slots + spare, 0:slots] = coded
        else:
            digit_ref[k] = jnp.zeros(digit_ref.shape[1:], bf16)
            digit_ref[k, :, 0:slots] = coded


def pack(route, tokens, members, slots):
    rows, width = tokens.shape
    group = min(members, 4)
    inside = slots <= width
    span = slots + spare if inside else slots
    whole = lambda j: (0, 0)
    block = lambda *tail: pl.BlockSpec((group, *tail), lambda j: (j, 0, 0))
    lanes = 8 if inside else 256
    return pl.pallas_call(
        lambda *refs: pack_kernel(rows, members, slots, *refs),
        grid=(members // group,),
        in_specs=[pl.BlockSpec((1, rows), whole), pl.BlockSpec((rows, width), whole)],
        out_specs=[block(span, width), block(8, lanes), pl.BlockSpec((1, rows), whole)],
        out_shape=[
            jax.ShapeDtypeStruct((members, span, width), bf16),
            jax.ShapeDtypeStruct((members, 8, lanes), bf16),
            jax.ShapeDtypeStruct((1, rows), jnp.int32),
        ],
        compiler_params=big_vmem,
        cost_estimate=cost(2 * members * slots * rows * width, 5 * rows * width),
        name="pack",
    )(route.reshape(1, rows), tokens)


def send_kernel(slots, slot_ref, x_ref, out_ref):
    group = out_ref.shape[0]
    count = group * slots
    ids = lax.broadcasted_iota(jnp.int32, (count, x_ref.shape[0]), 0)
    pick = jnp.where(slot_ref[...] == ids + pl.program_id(0) * count, 1.0, 0.0)
    sent = jnp.dot(pick.astype(bf16), x_ref[...], preferred_element_type=f32)
    for k in range(group):
        out_ref[k] = sent[k * slots : (k + 1) * slots].astype(bf16)


def send_rows(slot_of, source, members, slots):
    rows, width = source.shape
    group = min(members, 8)
    return pl.pallas_call(
        lambda *refs: send_kernel(slots, *refs),
        grid=(members // group,),
        in_specs=[
            pl.BlockSpec((1, rows), lambda j: (0, 0)),
            pl.BlockSpec((rows, width), lambda j: (0, 0)),
        ],
        out_specs=pl.BlockSpec((group, slots, width), lambda j: (j, 0, 0)),
        out_shape=jax.ShapeDtypeStruct((members, slots, width), bf16),
        compiler_params=big_vmem,
        cost_estimate=cost(2 * members * slots * rows * width, 5 * rows * width),
        name="send_rows",
    )(slot_of, source)


def place_kernel(rows, bases_ref, digit_ref, got_ref, out_ref, place_ref, src, pick):
    members, slots = got_ref.shape[0], got_ref.shape[1]
    count = out_ref.shape[0]
    span = src.shape[0] // members
    base = bases_ref[pl.program_id(0)]
    ids = lax.broadcasted_iota(jnp.int32, (count, span), 0) + base

    @pl.when(pl.program_id(0) == 0)
    def _():
        for j in range(members):
            src[j * span : j * span + slots] = got_ref[j]
            if span > slots:
                src[j * span + slots : (j + 1) * span] = jnp.zeros(
                    (span - slots, src.shape[1]), bf16
                )

    for j in range(members):
        coded = digit_ref[j].astype(f32)[:, 0:span]
        value = coded[0:1] * 64.0 + coded[1:2]
        places = jnp.where(coded[2:3] > 0.5, value, 4.0 * rows).astype(jnp.int32)
        pick[:, j * span : (j + 1) * span] = jnp.where(places == ids, 1.0, 0.0).astype(bf16)
        place_ref[j : j + 1, :] = places[:, 0:slots]
    out_ref[...] = jnp.dot(pick[...], src[...], preferred_element_type=f32).astype(bf16)


def place_rows(bases, digits, got, slots, rows, count):
    members, width = got.shape[0], got.shape[2]
    at = digits.shape[1] // 8 - 1
    span = -(-slots // 128) * 128
    return pl.pallas_call(
        lambda *refs: place_kernel(rows, *refs),
        grid_spec=pltpu.PrefetchScalarGridSpec(
            num_scalar_prefetch=1,
            grid=(bases.shape[0],),
            in_specs=[
                pl.BlockSpec((members, 8, digits.shape[2]), lambda i, b: (0, at, 0)),
                pl.BlockSpec((members, slots, width), lambda i, b: (0, 0, 0)),
            ],
            out_specs=[
                pl.BlockSpec((None, count, width), lambda i, b: (i, 0, 0)),
                pl.BlockSpec((members, slots), lambda i, b: (0, 0)),
            ],
            scratch_shapes=[
                pltpu.VMEM((members * span, width), bf16),
                pltpu.VMEM((count, members * span), bf16),
            ],
        ),
        out_shape=[
            jax.ShapeDtypeStruct((bases.shape[0], count, width), bf16),
            jax.ShapeDtypeStruct((members, slots), jnp.int32),
        ],
        compiler_params=big_vmem,
        cost_estimate=cost(0, (bases.shape[0] * count + members * slots) * width // 8),
        name="place_rows",
    )(bases, digits, got)


def take_kernel(ids_ref, from_ref, out_ref):
    cols = lax.broadcasted_iota(jnp.int32, (out_ref.shape[0], from_ref.shape[0]), 1)
    pick = jnp.where(ids_ref[...] == cols, 1.0, 0.0).astype(bf16)
    out_ref[...] = jnp.dot(pick, from_ref[...], preferred_element_type=f32).astype(
        out_ref.dtype
    )


def take_rows(ids, source, block, dtype):
    count = ids.shape[0]
    total, width = source.shape
    return pl.pallas_call(
        take_kernel,
        grid=(count // block,),
        in_specs=[
            pl.BlockSpec((block, 1), lambda i: (i, 0)),
            pl.BlockSpec((total, width), lambda i: (0, 0)),
        ],
        out_specs=pl.BlockSpec((block, width), lambda i: (i, 0)),
        out_shape=jax.ShapeDtypeStruct((count, width), dtype),
        compiler_params=big_vmem,
        cost_estimate=cost(2 * count * total * width, 2 * (count + total) * width),
        name="take_rows",
    )(ids, source)


def swap_mp(value):
    return lax.ppermute(value, "mp", [(0, 1), (1, 0)])


def side_by_side(mine, other, index):
    return jnp.where(
        index == 0,
        jnp.concatenate([mine, other], axis=1),
        jnp.concatenate([other, mine], axis=1),
    )


def rolled(full, shift):
    return jnp.roll(full, shift, axis=0)


def flip(value, bit):
    size = lax.axis_size("dp")
    return lax.ppermute(value, "dp", [(i, i ^ bit) for i in range(size)])


def dp_bits():
    return [1 << k for k in range(lax.axis_size("dp").bit_length() - 1)]


def halve(value, bit):
    half = value.shape[0] // 2
    side = (lax.axis_index("dp") // bit) % 2
    sent = lax.dynamic_slice_in_dim(value, (1 - side) * half, half, 0)
    kept = lax.dynamic_slice_in_dim(value, side * half, half, 0)
    return (kept.astype(f32) + flip(sent, bit).astype(f32)).astype(bf16)


def double(value, bit):
    side = (lax.axis_index("dp") // bit) % 2
    other = flip(value, bit)
    return jnp.where(
        side == 0,
        jnp.concatenate([value, other], axis=0),
        jnp.concatenate([other, value], axis=0),
    )


def sum_dp(value):
    bits = dp_bits()
    for bit in bits:
        value = halve(value, bit)
    for bit in reversed(bits):
        value = double(value, bit)
    return value


def after(value, *others):
    return lax.optimization_barrier((value, *others))[0]


class Ring:
    def __init__(self, parts):
        self.parts = parts
        self.nodes = nodes = lax.axis_size("dp") // 2
        chip = lax.axis_index("dp") // 2
        self.here = jnp.where(chip % 2 == 0, chip // 2, nodes - 1 - chip // 2)
        top = nodes // 2
        self.chips = [2 * p if p < top else 2 * (nodes - 1 - p) + 1 for p in range(nodes)]
        self.half = parts[0].shape[1] // 2
        self.held = {way: self.terms(self.here, way).astype(bf16) for way in (1, -1)}
        self.pieces = {1: [], -1: []}
        self.steps = 0

    def send(self, value, way):
        pairs = [
            (2 * self.chips[p] + c, 2 * self.chips[(p + way) % self.nodes] + c)
            for p in range(self.nodes)
            for c in range(2)
        ]
        return lax.ppermute(value, "dp", pairs)

    def terms(self, block, way):
        at = (block % self.nodes, 0 if way == 1 else self.half, 0)
        size = (1, self.half, self.parts[0].shape[2])
        pieces = [lax.dynamic_slice(v, at, size) for v in self.parts]
        return sum(piece.astype(f32) for piece in pieces)

    def step(self, *gates):
        count = self.steps
        if count == 2 * self.nodes - 2:
            return
        self.steps += 1
        adding = count < self.nodes - 1
        if gates:
            both = lax.optimization_barrier((self.held[1], self.held[-1], *gates))
            self.held = {1: both[0], -1: both[1]}
        for way in (1, -1):
            if count == self.nodes - 1:
                self.pieces[way].append(self.held[way])
            came = self.send(self.held[way], way)
            if adding:
                own = self.terms(self.here - way * (count + 1) + self.nodes, way)
                came = (came.astype(f32) + own).astype(bf16)
            else:
                self.pieces[way].append(came)
            self.held[way] = came

    def first(self, value):
        return after(value, *self.held.values())

    def total(self):
        return gather_pieces([p[0] for way in (1, -1) for p in self.pieces[way]])

    def order(self):
        block = jnp.arange(self.nodes, dtype=jnp.int32)
        up = (self.here + 1 - block + self.nodes) % self.nodes
        down = (block - self.here + 1 + self.nodes) % self.nodes + self.nodes
        core = lax.axis_index("dp")[None] % 2
        return jnp.concatenate([up, down, core]).astype(jnp.int32)


def gather_kernel(*refs):
    *sources, out_ref = refs
    for k, ref in enumerate(sources):
        out_ref[k] = ref[...]


def gather_pieces(pieces):
    count = len(pieces)
    vmem = pl.BlockSpec(memory_space=pltpu.VMEM)
    return pl.pallas_call(
        gather_kernel,
        in_specs=[vmem] * count,
        out_specs=vmem,
        out_shape=jax.ShapeDtypeStruct((count, *pieces[0].shape), bf16),
        compiler_params=big_vmem,
        cost_estimate=cost(0, 4 * count * pieces[0].size),
        name="gather_pieces",
    )(*pieces)


def ff_kernel(sub, x_ref, g_ref, wg_ref, wu_ref, wd_ref, gx_ref, y_ref, h_ref, gg_ref, gu_ref):
    step = pl.program_id(0)
    for at in range(0, wg_ref.shape[1], sub):
        c = slice(at, at + sub)
        gate = jnp.dot(x_ref[...], wg_ref[:, c], preferred_element_type=f32)
        up = jnp.dot(x_ref[...], wu_ref[:, c], preferred_element_type=f32)
        grad = nt_dot(g_ref[...], wd_ref[c])
        sig = 1.0 / (1.0 + jnp.exp(-gate))
        silu = gate * sig
        h_ref[:, c] = (silu * up).astype(bf16)
        gg_ref[:, c] = (grad * up * (sig + silu * (1.0 - sig))).astype(bf16)
        gu_ref[:, c] = (grad * silu).astype(bf16)
    def back(first):
        w = 256
        for at in range(0, gx_ref.shape[1], w):
            c = slice(at, at + w)
            gx = nt_dot(gg_ref[...], wg_ref[c, :]) + nt_dot(gu_ref[...], wu_ref[c, :])
            y = jnp.dot(h_ref[...], wd_ref[:, c], preferred_element_type=f32)
            if first:
                gx_ref[:, c] = gx
                y_ref[:, c] = y
            else:
                gx_ref[:, c] += gx
                y_ref[:, c] += y
    pl.when(step == 0)(lambda: back(True))
    pl.when(step > 0)(lambda: back(False))

def feed_forward(x, g, wg, wu, wd, sub=384):
    r, d = x.shape
    hid = wg.shape[1]
    chunk = hid // 3
    whole = pl.BlockSpec((r, d), lambda i: (0, 0))
    tall = pl.BlockSpec((d, chunk), lambda i: (0, i))
    wide = pl.BlockSpec((r, chunk), lambda i: (0, i))
    return pl.pallas_call(
        lambda *refs: ff_kernel(sub, *refs),
        grid=(hid // chunk,),
        in_specs=[
            whole,
            whole,
            tall,
            tall,
            pl.BlockSpec((chunk, d), lambda i: (i, 0)),
        ],
        out_specs=[whole, whole, wide, wide, wide],
        out_shape=[jax.ShapeDtypeStruct((r, d), f32)] * 2 + [jax.ShapeDtypeStruct((r, hid), bf16)] * 3,
        compiler_params=big_vmem,
        cost_estimate=cost(24 * r * d * hid, 6 * (d + r) * hid + 12 * r * d, 2 * r * hid),
        name="feed_forward",
    )(x, g, wg, wu, wd)

def grads_kernel(x0, x1, gg0, gg1, gu0, gu1, h0, h1, g0, g1, out_ref, xt, ht):
    step = pl.program_id(0)
    nodes, count, lanes = out_ref.shape
    rows = x0.shape[1] // nodes
    deep = h0.shape[1] // nodes
    r = x0.shape[0]
    @pl.when(step == 0)
    def _():
        xt[:, :r] = x0[...].T
        xt[:, r:] = x1[...].T
    @pl.when(step == 5)
    def _():
        ht[:, :r] = h0[...].T
        ht[:, r:] = h1[...].T
    def put(c, d, at):
        v = jnp.dot(xt[:, :r], c[...], preferred_element_type=f32) + jnp.dot(xt[:, r:], d[...], preferred_element_type=f32)
        out_ref[:, pl.ds(pl.multiple_of(at, 64), rows)] = v.astype(bf16).reshape(nodes, rows, lanes)
    @pl.when(step < 3)
    def _(): put(gg0, gg1, step * rows)
    @pl.when((step >= 3) & (step < 6))
    def _(): put(gu0, gu1, step * rows)
    @pl.when(step == 6)
    def _():
        v = jnp.dot(ht[:, :r], g0[:, :lanes], preferred_element_type=f32) + jnp.dot(ht[:, r:], g1[:, :lanes], preferred_element_type=f32)
        out_ref[:, 6 * rows : 6 * rows + deep] = v.astype(bf16).reshape(nodes, deep, lanes)
        v = jnp.dot(ht[:, :r], g0[:, lanes:], preferred_element_type=f32) + jnp.dot(ht[:, r:], g1[:, lanes:], preferred_element_type=f32)
        v = v.astype(bf16).reshape(nodes, deep, v.shape[1])
        short, rest = deep // 3, v.shape[2]
        for k in range(3):
            out_ref[:, 6 * rows + deep :, k * rest : (k + 1) * rest] = v[:, k * short : (k + 1) * short]

def ff_grads(side, nodes, x0, x1, gg0, gg1, gu0, gu1, h0, h1, g0, g1):
    r, d = x0.shape
    hid = gg0.shape[1]
    lanes = hid // 3
    rows, deep = d // (2 * nodes), hid // (2 * nodes)
    count = 6 * rows + deep + deep // 3
    half = lambda n: pl.BlockSpec((r, n), lambda i, s: (0, s[0]))
    first = pl.BlockSpec((r, lanes), lambda i, s: (0, jnp.minimum(i, 2)))
    second = pl.BlockSpec((r, lanes), lambda i, s: (0, jnp.clip(i - 3, 0, 2)))
    whole = pl.BlockSpec((r, d), lambda i, s: (0, 0))
    return pl.pallas_call(
        lambda s, *refs: grads_kernel(*refs),
        grid_spec=pltpu.PrefetchScalarGridSpec(
            num_scalar_prefetch=1, grid=(7,),
            in_specs=[half(d // 2)] * 2 + [first] * 2 + [second] * 2 + [half(hid // 2)] * 2 + [whole] * 2,
            out_specs=pl.BlockSpec((nodes, count, lanes), lambda i, s: (0, 0, 0)),
            scratch_shapes=[pltpu.VMEM((d // 2, 2 * r), bf16), pltpu.VMEM((hid // 2, 2 * r), bf16)],
        ),
        out_shape=jax.ShapeDtypeStruct((nodes, count, lanes), bf16),
        compiler_params=big_vmem,
        cost_estimate=cost(12 * r * d * hid, 6 * r * hid + 5 * d * hid),
        name="ff_grads",
    )(side.astype(jnp.int32).reshape(1), x0, x1, gg0, gg1, gu0, gu1, h0, h1, g0, g1)


def open_specs(nodes, group, half, lanes, first=0):
    specs = []
    for _ in range(2):
        for b in range(group):
            for at in (0, nodes):
                specs.append(
                    pl.BlockSpec(
                        (None, half, lanes),
                        lambda j, h, order, b=b, at=at: (
                            order[at + (first + j) * group + b],
                            0,
                            0,
                        ),
                    )
                )
    return specs


def open_blocks(group, order_ref, refs, write):
    core = order_ref[order_ref.shape[0] - 1]
    half = refs[0].shape[0]

    def reader(first, second):
        def read(start, stop):
            if stop <= half:
                return first[start:stop].astype(f32)
            if start >= half:
                return second[start - half : stop - half].astype(f32)
            pieces = [first[start:half], second[0 : stop - half]]
            return jnp.concatenate([p.astype(f32) for p in pieces], axis=0)

        return read

    def hand(refs):
        for b in range(group):
            write(b, reader(refs[2 * b], refs[2 * b + 1]))

    own = pl.program_id(1) == core
    pl.when(own)(lambda: hand(refs[: 2 * group]))
    pl.when(jnp.logical_not(own))(lambda: hand(refs[2 * group :]))


def open_ff_kernel(group, order_ref, *refs):
    *pieces, gate_ref, up_ref, down_ref = refs
    lanes = pieces[0].shape[1]
    rows, deep = gate_ref.shape[0] // group, down_ref.shape[0] // group
    rest = down_ref.shape[1] - lanes
    short = deep // 3

    def write(b, read):
        here = slice(b * rows, (b + 1) * rows)
        for k, out in enumerate((gate_ref, up_ref)):
            for c in range(3):
                part = read((3 * k + c) * rows, (3 * k + c + 1) * rows)
                out[here, c * lanes : (c + 1) * lanes] = part
        low, at = b * deep, 6 * rows
        down_ref[low : low + deep, :lanes] = read(at, at + deep)
        for c in range(3):
            part = read(at + deep, at + deep + short)[:, c * rest : (c + 1) * rest]
            down_ref[low + c * short : low + (c + 1) * short, lanes:] = part

    open_blocks(group, order_ref, pieces, write)


def open_ff(pieces, order, at, so_far, width, hidden):
    mine, other = pieces
    half, lanes = mine.shape[1:]
    nodes, group = mine.shape[0] // 2, 2
    steps = nodes // group
    rows, deep = width // (2 * nodes), hidden // (2 * nodes)
    out = lambda tall, wide: pl.BlockSpec(
        (group * tall, wide), lambda j, h, order: (h * steps + at, 0)
    )
    specs = open_specs(nodes, group, half, lanes, at)
    shapes = [(width, hidden), (width, hidden), (hidden, width)]
    kernel = lambda order, *refs: open_ff_kernel(
        group, order, *refs[: 4 * group], *refs[4 * group + len(so_far) :]
    )
    return pl.pallas_call(
        kernel,
        grid_spec=pltpu.PrefetchScalarGridSpec(
            num_scalar_prefetch=1,
            grid=(1, 2),
            in_specs=specs + [pl.BlockSpec(memory_space=pl.ANY)] * len(so_far),
            out_specs=[out(rows, hidden), out(rows, hidden), out(deep, width)],
        ),
        out_shape=[jax.ShapeDtypeStruct(shape, f32) for shape in shapes],
        input_output_aliases={1 + 4 * group + k: k for k in range(len(so_far))},
        compiler_params=big_vmem,
        cost_estimate=cost(0, 24 * width * hidden // steps),
        name="open_ff",
    )(order, *[mine] * (2 * group), *[other] * (2 * group), *so_far)


def pack_conv_kernel(core_ref, in_ref, out_w_ref, tail_ref, away_ref, own_ref):
    blocks, _, width = own_ref.shape
    rows = in_ref.shape[0] // (2 * blocks)
    deep = out_w_ref.shape[0] // blocks
    lanes = width // 2

    def write(ref):
        for k in range(blocks):
            ref[k, 0:rows, 0:lanes] = in_ref[2 * k * rows : (2 * k + 1) * rows]
            ref[k, 0:rows, lanes:] = in_ref[(2 * k + 1) * rows : (2 * k + 2) * rows]
            ref[k, rows : rows + deep] = out_w_ref[k * deep : (k + 1) * deep]
            ref[k, rows + deep :] = tail_ref[...]

    pl.when(pl.program_id(0) == 0)(lambda: write(away_ref))
    pl.when(pl.program_id(0) == 1)(lambda: write(own_ref))


def pack_conv(grad_in, grad_out, tail, part, nodes):
    total, width = grad_in.shape
    half_in, half_out = total // 2, grad_out.shape[0] // 4
    spared = tail.shape[0]
    count = half_in // (2 * nodes) + half_out // nodes + spared
    core = (lax.axis_index("dp") % 2).astype(jnp.int32).reshape(1)
    side = lambda i, c: jnp.where(i == 0, 1 - c[0], c[0])
    out = pl.BlockSpec((nodes, count, width), lambda i, c: (0, 0, 0))
    return pl.pallas_call(
        pack_conv_kernel,
        grid_spec=pltpu.PrefetchScalarGridSpec(
            num_scalar_prefetch=1,
            grid=(2,),
            in_specs=[
                pl.BlockSpec((half_in, width // 2), lambda i, c: (side(i, c), part)),
                pl.BlockSpec((half_out, width), lambda i, c: (2 * part + side(i, c), 0)),
                pl.BlockSpec((spared, width), lambda i, c: (0, 0)),
            ],
            out_specs=[out, out],
        ),
        out_shape=[jax.ShapeDtypeStruct((nodes, count, width), bf16)] * 2,
        compiler_params=big_vmem,
        cost_estimate=cost(0, 2 * (grad_in.size + grad_out.size)),
        name="pack_conv",
    )(core, grad_in, grad_out, tail)


def open_conv_kernel(group, order_ref, *refs):
    *pieces, in_ref, out_w_ref, tail_ref = refs
    rows, lanes = in_ref.shape[0] // (2 * group), in_ref.shape[1]
    deep = out_w_ref.shape[0] // group

    def write(b, read):
        low = 2 * b * rows
        in_ref[low : low + rows] = read(0, rows)[:, :lanes]
        in_ref[low + rows : low + 2 * rows] = read(0, rows)[:, lanes:]
        out_w_ref[b * deep : (b + 1) * deep] = read(rows, rows + deep)
        tail_ref[b] = read(rows + deep, rows + deep + tail_ref.shape[1])

    open_blocks(group, order_ref, pieces, write)


def open_conv(ring, gate, total, deep_total):
    mine = after(ring.total(), gate)
    other = flip(mine, 1)
    _, half, width = mine.shape
    nodes, group = ring.nodes, ring.nodes // 2
    blocks = 2 * nodes
    steps = nodes // group
    rows, deep = total // blocks, deep_total // blocks
    spared = 2 * half - rows // 2 - deep
    at = lambda j, h, order: (h * steps + j, 0)
    return pl.pallas_call(
        lambda *refs: open_conv_kernel(group, *refs),
        grid_spec=pltpu.PrefetchScalarGridSpec(
            num_scalar_prefetch=1,
            grid=(steps, 2),
            in_specs=open_specs(nodes, group, half, width),
            out_specs=[
                pl.BlockSpec((group * rows, width // 2), at),
                pl.BlockSpec((group * deep, width), at),
                pl.BlockSpec(
                    (group, spared, width), lambda j, h, order: (h * steps + j, 0, 0)
                ),
            ],
        ),
        out_shape=[
            jax.ShapeDtypeStruct((total, width // 2), f32),
            jax.ShapeDtypeStruct((deep_total, width), f32),
            jax.ShapeDtypeStruct((blocks, spared, width), f32),
        ],
        compiler_params=big_vmem,
        cost_estimate=cost(0, 8 * (total + deep_total) * width),
        name="open_conv",
    )(ring.order(), *[mine] * (2 * group), *[other] * (2 * group))


def on_device(
    tokens,
    cotangent,
    route,
    seq_lengths,
    norm1_gain,
    in_weight,
    conv_weight,
    out_weight,
    norm2_gain,
    gate_weight,
    up_weight,
    down_weight,
):
    dp_size = lax.axis_size("dp")
    mp_size = lax.axis_size("mp")
    dp_index = lax.axis_index("dp")
    mp_index = lax.axis_index("mp")
    rows = tokens.shape[0]
    narrow = tokens.shape[1]
    width = norm1_gain.shape[0]
    own = rows // mp_size
    start = mp_index * own
    column = mp_index * narrow
    pair_share = rows // dp_size
    slots = pair_share + pair_share // 2
    paired = mp_size == 2

    if paired:
        core = dp_index % 2
        deep = width // 2
        part_in = lax.dynamic_slice_in_dim(in_weight, core * deep, deep, 1)
        part_out = lax.dynamic_slice_in_dim(out_weight, core * deep, deep, 1)
        part = jnp.concatenate([part_in, part_out.reshape(1, deep, deep)], axis=0)
        there = swap_mp(part)
        route = after(route, part)
        taps = jnp.concatenate([conv_weight, swap_mp(conv_weight)], axis=1)
    else:
        full_in = lax.all_gather(in_weight, "mp", axis=2, tiled=True)
        full_out = lax.all_gather(out_weight, "mp", axis=0, tiled=True)
        taps = lax.all_gather(conv_weight, "mp", axis=1, tiled=True)

    sent_rows, digits, slot_of = pack(route, tokens, dp_size, slots)
    sent_seeds = send_rows(after(slot_of, sent_rows), cotangent, dp_size, slots)
    over = dict(split_axis=0, concat_axis=0, tiled=True)
    got_rows = lax.all_to_all(sent_rows, "dp", **over)
    digits = got_rows if slots <= narrow else lax.all_to_all(digits, "dp", **over)
    got_rows, sent_seeds = lax.optimization_barrier((got_rows, sent_seeds))
    got_seeds = lax.all_to_all(sent_seeds, "dp", **over)
    slot_of = slot_of.reshape(rows, 1)
    window = own + 2 * halo
    if paired:
        bases = jnp.stack([start, own - start]).astype(jnp.int32)
        digits = got_rows if slots <= narrow else digits
        pieces, places = place_rows(bases - halo, digits, got_rows, slots, rows, window)
        there, _ = lax.optimization_barrier((there, pieces))
        here = flip(there, 1)
        both = [jnp.where(core == k, there, here) for k in range(2)]
        other_in = jnp.concatenate([v[:3] for v in both], axis=1)
        other_out = jnp.concatenate([v[3] for v in both], axis=1)
        full_in = jnp.concatenate([in_weight, other_in], axis=2)
        full_out = jnp.concatenate([out_weight, other_out], axis=0)
        input_rows = side_by_side(pieces[0], swap_mp(pieces[1]), mp_index)
        pieces, _ = place_rows(bases, digits, got_seeds, slots, rows, own)
        input_rows = after(input_rows, pieces)
        came = swap_mp(pieces[1])
        seeds_own = side_by_side(pieces[0], came, mp_index)
        seeds_other = side_by_side(pieces[1], swap_mp(after(pieces[0], came)), mp_index)
        place_ids = ((places - start) % rows).reshape(-1, 1)
    else:
        bases = (jnp.arange(mp_size) * own).astype(jnp.int32)
        pieces, places = place_rows(bases, digits, got_rows, slots, rows, own)
        full = lax.all_gather(pieces.reshape(rows, narrow), "mp", axis=1, tiled=True)
        full = jnp.pad(full, ((halo, halo), (0, 0)))
        input_rows = lax.dynamic_slice_in_dim(full, start, window, 0)
        pieces, _ = place_rows(bases, digits, got_seeds, slots, rows, own)
        full = lax.all_gather(pieces.reshape(rows, narrow), "mp", axis=1, tiled=True)
        seeds = rolled(full, -start)
        seeds_own, seeds_other = seeds[:own], seeds[own:]
        place_ids = places.reshape(-1, 1)

    positions = start - halo + jnp.arange(window, dtype=jnp.int32)
    first_mask, second_mask = seq_masks(seq_lengths[0], positions, rows)
    residual = input_rows.astype(f32)
    scale_one = lax.rsqrt(jnp.mean(residual * residual, axis=1) + epsilon)[:, None]
    normed_one = (residual * scale_one * norm1_gain).astype(bf16)
    projected = jnp.einsum("rd,kdc->krc", normed_one, full_in, preferred_element_type=f32)
    in_gate, out_gate, value_part = (projected[0], projected[1], projected[2])
    mixed = in_gate * value_part
    lag_one = lag_rows(mixed, 1) * first_mask
    lag_two = lag_rows(mixed, 2) * second_mask
    convolved = taps[2] * mixed + taps[1] * lag_one + taps[0] * lag_two
    gated = (out_gate * convolved).astype(bf16)
    gated = after(gated, seeds_own)
    middle = (residual + jnp.dot(gated, full_out, preferred_element_type=f32))[halo:]
    scale_two = lax.rsqrt(jnp.mean(middle * middle, axis=1) + epsilon)[:, None]
    normed_own = (middle[:own] * scale_two[:own] * norm2_gain).astype(bf16)

    weights = (gate_weight, up_weight, down_weight)
    if paired:
        normed_other = swap_mp(normed_own)
        first = feed_forward(normed_own, seeds_own, *weights)
        second = feed_forward(normed_other, seeds_other, *weights)
        sent = jnp.concatenate([second[0], first[0][:halo]], axis=0).astype(bf16)
        came = swap_mp(sent)
        saved = (normed_other, first[3], second[3], first[4], second[4])
        saved += (first[2], second[2], seeds_own, seeds_other)
        away = ff_grads(1 - core, dp_size // 2, after(normed_own, sent), *saved)
        kept = ff_grads(core, dp_size // 2, after(normed_own, away), *saved)
        away = flip(away, 1)
        came, _ = lax.optimization_barrier((came, kept))
        grad_normed_two = jnp.concatenate([first[0], second[0][:halo]], axis=0)
        grad_normed_two = grad_normed_two + came.astype(f32)
        down_came = swap_mp(after(second[1].astype(bf16), came))
        ring = Ring((kept, away))
        grad_normed_two = ring.first(grad_normed_two)
        ring.step()
    else:
        normed_two = rolled(lax.all_gather(normed_own, "mp", axis=0, tiled=True), -start)
        gate_val = jnp.dot(normed_two, gate_weight, preferred_element_type=f32)
        up_val = jnp.dot(normed_two, up_weight, preferred_element_type=f32)
        sigmoid_val = jax.nn.sigmoid(gate_val)
        silu_val = gate_val * sigmoid_val
        hidden = (silu_val * up_val).astype(bf16)
        grad_hidden = nt_dot(seeds, down_weight)
        grad_gate_val = (
            grad_hidden * up_val * sigmoid_val * (1.0 + gate_val * (1.0 - sigmoid_val))
        ).astype(bf16)
        grad_up_val = (grad_hidden * silu_val).astype(bf16)
        normed_terms = nt_dot(grad_gate_val, gate_weight) + nt_dot(grad_up_val, up_weight)
        down_terms = jnp.dot(hidden, down_weight, preferred_element_type=f32)
        full = rolled(lax.psum(rolled(normed_terms, start), "mp"), -start)
        grad_normed_two = full[: own + halo]
        down_sum = rolled(lax.psum(rolled(down_terms, start), "mp"), -start)[:own]
        total_gate = sum_dp(tn_dot(normed_two, grad_gate_val).astype(bf16)).astype(f32)
        total_up = sum_dp(tn_dot(normed_two, grad_up_val).astype(bf16)).astype(f32)
        total_down = sum_dp(tn_dot(hidden, seeds).astype(bf16)).astype(f32)
        block_own = (middle[:own] + down_sum).astype(bf16)

    def to_features(mine):
        if not paired:
            full = lax.all_gather(mine, "mp", axis=0, tiled=True)
            return lax.dynamic_slice_in_dim(full, column, narrow, 1)
        low, high = mine[:, :narrow], mine[:, narrow:]
        other = swap_mp(jnp.where(mp_index == 0, high, low))
        return jnp.concatenate([jnp.where(mp_index == 0, low, high), other], axis=0)

    shape = (dp_size, slots, narrow)
    back_block = min(8 * slots, slots * dp_size)
    home_block = min(rows, 512)

    def leave(piece):
        return take_rows(place_ids, piece, back_block, bf16).reshape(shape)

    def to_home(back):
        return lax.all_to_all(back, "dp", **over)

    def arrive(home, dtype):
        return take_rows(slot_of, home.reshape(-1, narrow), home_block, dtype)

    gain_two_term = jnp.sum((grad_normed_two * middle * scale_two)[:own], axis=0)
    dot_two = jnp.sum(norm2_gain * grad_normed_two * middle, axis=1, keepdims=True)
    grad_middle = (
        jnp.concatenate([seeds_own, seeds_other[:halo]], axis=0).astype(f32)
        + scale_two * norm2_gain * grad_normed_two
        - middle * (scale_two * scale_two * scale_two * dot_two / width)
    )
    grad_mix = grad_middle.astype(bf16)
    grad_gated = jnp.einsum("rd,cd->rc", grad_mix, full_out, preferred_element_type=f32)
    if paired:
        grad_gated = ring.first(grad_gated)
        ring.step()
    grad_conv = grad_gated * out_gate[halo:]
    inner = slice(halo, halo + own)
    conv_terms = jnp.stack(
        [
            jnp.sum(grad_conv[:own] * lag_two[inner], axis=0),
            jnp.sum(grad_conv[:own] * lag_one[inner], axis=0),
            jnp.sum(grad_conv[:own] * mixed[inner], axis=0),
        ],
        axis=0,
    )
    grad_mixed = (
        taps[2] * grad_conv
        + taps[1] * lead_rows(grad_conv * first_mask[halo:], 1)
        + taps[0] * lead_rows(grad_conv * second_mask[halo:], 2)
    )[:own]
    grad_parts = jnp.stack(
        [
            grad_mixed * value_part[inner],
            grad_gated[:own] * convolved[inner],
            grad_mixed * in_gate[inner],
        ],
        axis=0,
    ).astype(bf16)
    grad_in = jnp.einsum(
        "rd,krc->kdc", normed_one[inner], grad_parts, preferred_element_type=f32
    ).astype(bf16)
    grad_out = jnp.einsum(
        "rc,rd->cd", gated[inner], grad_mix[:own], preferred_element_type=f32
    ).astype(bf16)
    taps_end = 2 + conv_weight.shape[0]

    parts_late = grad_parts
    if paired:
        ring.step()
        parts_late = ring.first(grad_parts)
    grad_normed_one = jnp.einsum("krc,kdc->rd", parts_late, full_in, preferred_element_type=f32)
    residual_own = residual[inner]
    scale_own = scale_one[inner]
    gain_one_term = jnp.sum(grad_normed_one * residual_own * scale_own, axis=0)
    dot_one = jnp.sum(norm1_gain * grad_normed_one * residual_own, axis=1, keepdims=True)
    input_own = (
        grad_middle[:own]
        + scale_own * norm1_gain * grad_normed_one
        - residual_own * (scale_own * scale_own * scale_own * dot_one / width)
    ).astype(bf16)

    def packed_half(k, *gates):
        lanes = slice(k * narrow, (k + 1) * narrow)
        terms = jnp.pad(conv_terms[:, lanes], ((0, 16 - taps_end), (0, width - narrow)))
        gains = jnp.stack([gain_one_term, gain_two_term], axis=0)
        ends = after(jnp.concatenate([gains, terms], axis=0).astype(bf16), *gates)
        return pack_conv(grad_in.reshape(-1, width), grad_out, ends, k, dp_size // 2)

    if paired:
        away, other = packed_half(1)
        passed = (other.astype(f32) + flip(away, 1).astype(f32)).astype(bf16)
        down_came = after(down_came, grad_parts)
        block_own = (middle[:own] + (first[1] + down_came.astype(f32))).astype(bf16)
        block_piece = to_features(block_own)
        block_back = leave(block_piece)
        out_home = to_home(block_back)
        ring.step(block_piece)
        away, own_half = packed_half(0, passed, *ring.held.values())
        passed = swap_mp(passed)
        input_piece = to_features(input_own)
        ring.step()
        ring.step(input_piece)
        input_back = leave(after(input_piece, out_home))
        grad_home = to_home(input_back)
        ring.step(out_home)
        ring.step(away)
        block_out = arrive(out_home, bf16)
        ring.step()
        second = Ring((own_half, flip(away, 1), passed))
        ring.step(*second.held.values(), grad_home)
        second.step()
        tokens_grad = arrive(grad_home, f32)
        while ring.steps < 2 * ring.nodes - 2:
            ring.step(*second.held.values())
            second.step()
        mine = ring.total()
        pieces = (mine, flip(mine, 1))
        second.step(mine)
        second.step(tokens_grad)
        totals = ()
        for at in range(ring.nodes // 2):
            totals = open_ff(pieces, ring.order(), at, totals, width, gate_weight.shape[1])
            second.step(*totals)
        while second.steps < 2 * second.nodes - 2:
            second.step()
        total_gate, total_up, total_down = totals
        total_in, total_out, ends = open_conv(
            second, total_gate, grad_in.size // (2 * narrow), narrow
        )
        tail = ends[0]
    else:
        block_out = arrive(to_home(leave(to_features(block_own))), bf16)
        tokens_grad = arrive(to_home(leave(to_features(input_own))), f32)
        total_in = lax.psum_scatter(
            grad_in.astype(f32), "mp", scatter_dimension=2, tiled=True
        )
        total_in = sum_dp(total_in.astype(bf16).reshape(-1, narrow)).astype(f32)
        total_out = lax.psum_scatter(
            grad_out.astype(f32), "mp", scatter_dimension=0, tiled=True
        )
        total_out = sum_dp(total_out.astype(bf16)).astype(f32)
        gains = lax.psum(jnp.stack([gain_one_term, gain_two_term]), ("dp", "mp"))
        terms = lax.psum_scatter(conv_terms, "mp", scatter_dimension=1, tiled=True)
        terms = jnp.pad(lax.psum(terms, "dp"), ((0, 0), (0, width - narrow)))
        tail = jnp.concatenate([gains, terms], axis=0)
    total_taps = tail[2:taps_end, :narrow]
    return (
        block_out,
        tokens_grad,
        tail[0],
        total_in.reshape(in_weight.shape),
        total_taps,
        total_out,
        tail[1],
        total_gate,
        total_up,
        total_down,
    )


def solution(mesh):
    in_specs = (
        P("dp", "mp"),
        P("dp", "mp"),
        P("dp"),
        P("dp", None),
        P(),
        P(None, None, "mp"),
        P(None, "mp"),
        P("mp", None),
        P(),
        P(None, "mp"),
        P(None, "mp"),
        P("mp", None),
    )
    out_specs = (
        P("dp", "mp"),
        P("dp", "mp"),
        P(),
        P(None, None, "mp"),
        P(None, "mp"),
        P("mp", None),
        P(),
        P(None, "mp"),
        P(None, "mp"),
        P("mp", None),
    )
    return jax.shard_map(
        on_device, mesh=mesh, in_specs=in_specs, out_specs=out_specs, check_vma=False
    )
```

```python
import jax
import jax.numpy as jnp
from jax import lax
from jax.experimental import pallas as pl
from jax.experimental.pallas import tpu as pltpu
from jax.sharding import PartitionSpec as P

epsilon = 1e-05
f32 = jnp.float32
bf16 = jnp.bfloat16
halo = 8
spare = 8
big_vmem = pltpu.CompilerParams(vmem_limit_bytes=58 << 20)


def cost(flops, moved, transcendentals=0):
    return pl.CostEstimate(
        flops=int(flops), bytes_accessed=int(moved), transcendentals=int(transcendentals)
    )


def lag_rows(values, shift):
    return jnp.concatenate(
        [jnp.zeros((shift, values.shape[1]), values.dtype), values[:-shift]], axis=0
    )


def lead_rows(values, shift):
    return jnp.concatenate(
        [values[shift:], jnp.zeros((shift, values.shape[1]), values.dtype)], axis=0
    )


def seq_masks(lengths, positions, row_count):
    count = lengths.shape[0]
    before = jnp.arange(count)[:, None] < jnp.arange(count)[None, :]
    starts = jnp.sum(jnp.where(before, lengths[:, None], 0), axis=0, dtype=jnp.int32)
    started = positions[:, None] >= starts[None, :]
    seq_first = jnp.max(jnp.where(started, starts[None, :], 0), axis=1)
    offset = positions - seq_first
    inside = (positions >= 0) & (positions < row_count)
    return (
        ((offset >= 1) & inside).astype(f32)[:, None],
        ((offset >= 2) & inside).astype(f32)[:, None],
    )


def nt_dot(left, right):
    return lax.dot_general(
        left, right, (((1,), (1,)), ((), ())), preferred_element_type=f32
    )


def tn_dot(left, right):
    return lax.dot_general(
        left, right, (((0,), (0,)), ((), ())), preferred_element_type=f32
    )


def rank_kernel(rows, members, slots, route_ref, slot_ref):
    target = route_ref[...] // rows
    width = min(rows, 512)
    owner = lax.broadcasted_iota(jnp.int32, (members, rows), 0)
    one_hot = jnp.where(owner == target, 1.0, 0.0)
    left = one_hot.astype(bf16)
    for start in range(0, rows, width):
        first = lax.broadcasted_iota(jnp.int32, (rows, width), 0)
        second = lax.broadcasted_iota(jnp.int32, (rows, width), 1) + start
        earlier = jnp.where(first < second, 1.0, 0.0).astype(bf16)
        rank = jnp.dot(left, earlier, preferred_element_type=f32)
        piece = one_hot[:, start : start + width]
        mine = jnp.sum(rank * piece, axis=0, keepdims=True).astype(jnp.int32)
        slot_ref[:, start : start + width] = (
            target[:, start : start + width] * slots + mine
        )


def pack_kernel(rows, members, slots, route_ref, x_ref, sx_ref, digit_ref, slot_ref):
    step = pl.program_id(0)
    group = sx_ref.shape[0]

    @pl.when(step == 0)
    def _():
        rank_kernel(rows, members, slots, route_ref, slot_ref)

    place = route_ref[...] % rows
    row = lax.broadcasted_iota(jnp.int32, (8, rows), 0)
    digits = jnp.where(
        row == 0,
        (place // 64).astype(f32),
        jnp.where(row == 1, (place % 64).astype(f32), 1.0),
    ).astype(bf16)
    ids = lax.broadcasted_iota(jnp.int32, (group * slots, rows), 0)
    pick = jnp.where(slot_ref[...] == ids + step * group * slots, 1.0, 0.0).astype(bf16)
    sent = jnp.dot(pick, x_ref[...], preferred_element_type=f32).astype(bf16)
    for k in range(group):
        here = slice(k * slots, (k + 1) * slots)
        sx_ref[k, 0:slots] = sent[here]
        coded = nt_dot(digits, pick[here]).astype(bf16)
        if sx_ref.shape[1] > slots:
            sx_ref[k, slots : slots + spare] = jnp.zeros((spare, sx_ref.shape[2]), bf16)
            sx_ref[k, slots : slots + spare, 0:slots] = coded
        else:
            digit_ref[k] = jnp.zeros(digit_ref.shape[1:], bf16)
            digit_ref[k, :, 0:slots] = coded


def pack(route, tokens, members, slots):
    rows, width = tokens.shape
    group = min(members, 4)
    inside = slots <= width
    span = slots + spare if inside else slots
    whole = lambda j: (0, 0)
    block = lambda *tail: pl.BlockSpec((group, *tail), lambda j: (j, 0, 0))
    lanes = 8 if inside else 256
    return pl.pallas_call(
        lambda *refs: pack_kernel(rows, members, slots, *refs),
        grid=(members // group,),
        in_specs=[pl.BlockSpec((1, rows), whole), pl.BlockSpec((rows, width), whole)],
        out_specs=[block(span, width), block(8, lanes), pl.BlockSpec((1, rows), whole)],
        out_shape=[
            jax.ShapeDtypeStruct((members, span, width), bf16),
            jax.ShapeDtypeStruct((members, 8, lanes), bf16),
            jax.ShapeDtypeStruct((1, rows), jnp.int32),
        ],
        compiler_params=big_vmem,
        cost_estimate=cost(2 * members * slots * rows * width, 5 * rows * width),
        name="pack",
    )(route.reshape(1, rows), tokens)


def send_kernel(slots, slot_ref, x_ref, out_ref):
    group = out_ref.shape[0]
    count = group * slots
    ids = lax.broadcasted_iota(jnp.int32, (count, x_ref.shape[0]), 0)
    pick = jnp.where(slot_ref[...] == ids + pl.program_id(0) * count, 1.0, 0.0)
    sent = jnp.dot(pick.astype(bf16), x_ref[...], preferred_element_type=f32)
    for k in range(group):
        out_ref[k] = sent[k * slots : (k + 1) * slots].astype(bf16)


def send_rows(slot_of, source, members, slots):
    rows, width = source.shape
    group = min(members, 8)
    return pl.pallas_call(
        lambda *refs: send_kernel(slots, *refs),
        grid=(members // group,),
        in_specs=[
            pl.BlockSpec((1, rows), lambda j: (0, 0)),
            pl.BlockSpec((rows, width), lambda j: (0, 0)),
        ],
        out_specs=pl.BlockSpec((group, slots, width), lambda j: (j, 0, 0)),
        out_shape=jax.ShapeDtypeStruct((members, slots, width), bf16),
        compiler_params=big_vmem,
        cost_estimate=cost(2 * members * slots * rows * width, 5 * rows * width),
        name="send_rows",
    )(slot_of, source)


def place_kernel(rows, bases_ref, digit_ref, got_ref, out_ref, place_ref, src, pick):
    members, slots = got_ref.shape[0], got_ref.shape[1]
    count = out_ref.shape[0]
    span = src.shape[0] // members
    base = bases_ref[pl.program_id(0)]
    ids = lax.broadcasted_iota(jnp.int32, (count, span), 0) + base

    @pl.when(pl.program_id(0) == 0)
    def _():
        for j in range(members):
            src[j * span : j * span + slots] = got_ref[j]
            if span > slots:
                src[j * span + slots : (j + 1) * span] = jnp.zeros(
                    (span - slots, src.shape[1]), bf16
                )

    for j in range(members):
        coded = digit_ref[j].astype(f32)[:, 0:span]
        value = coded[0:1] * 64.0 + coded[1:2]
        places = jnp.where(coded[2:3] > 0.5, value, 4.0 * rows).astype(jnp.int32)
        pick[:, j * span : (j + 1) * span] = jnp.where(places == ids, 1.0, 0.0).astype(bf16)
        place_ref[j : j + 1, :] = places[:, 0:slots]
    out_ref[...] = jnp.dot(pick[...], src[...], preferred_element_type=f32).astype(bf16)


def place_rows(bases, digits, got, slots, rows, count):
    members, width = got.shape[0], got.shape[2]
    at = digits.shape[1] // 8 - 1
    span = -(-slots // 128) * 128
    return pl.pallas_call(
        lambda *refs: place_kernel(rows, *refs),
        grid_spec=pltpu.PrefetchScalarGridSpec(
            num_scalar_prefetch=1,
            grid=(bases.shape[0],),
            in_specs=[
                pl.BlockSpec((members, 8, digits.shape[2]), lambda i, b: (0, at, 0)),
                pl.BlockSpec((members, slots, width), lambda i, b: (0, 0, 0)),
            ],
            out_specs=[
                pl.BlockSpec((None, count, width), lambda i, b: (i, 0, 0)),
                pl.BlockSpec((members, slots), lambda i, b: (0, 0)),
            ],
            scratch_shapes=[
                pltpu.VMEM((members * span, width), bf16),
                pltpu.VMEM((count, members * span), bf16),
            ],
        ),
        out_shape=[
            jax.ShapeDtypeStruct((bases.shape[0], count, width), bf16),
            jax.ShapeDtypeStruct((members, slots), jnp.int32),
        ],
        compiler_params=big_vmem,
        cost_estimate=cost(0, (bases.shape[0] * count + members * slots) * width // 8),
        name="place_rows",
    )(bases, digits, got)


def take_kernel(ids_ref, from_ref, out_ref):
    cols = lax.broadcasted_iota(jnp.int32, (out_ref.shape[0], from_ref.shape[0]), 1)
    pick = jnp.where(ids_ref[...] == cols, 1.0, 0.0).astype(bf16)
    out_ref[...] = jnp.dot(pick, from_ref[...], preferred_element_type=f32).astype(
        out_ref.dtype
    )


def take_rows(ids, source, block, dtype):
    count = ids.shape[0]
    total, width = source.shape
    return pl.pallas_call(
        take_kernel,
        grid=(count // block,),
        in_specs=[
            pl.BlockSpec((block, 1), lambda i: (i, 0)),
            pl.BlockSpec((total, width), lambda i: (0, 0)),
        ],
        out_specs=pl.BlockSpec((block, width), lambda i: (i, 0)),
        out_shape=jax.ShapeDtypeStruct((count, width), dtype),
        compiler_params=big_vmem,
        cost_estimate=cost(2 * count * total * width, 2 * (count + total) * width),
        name="take_rows",
    )(ids, source)


def swap_mp(value):
    return lax.ppermute(value, "mp", [(0, 1), (1, 0)])


def side_by_side(mine, other, index):
    return jnp.where(
        index == 0,
        jnp.concatenate([mine, other], axis=1),
        jnp.concatenate([other, mine], axis=1),
    )


def rolled(full, shift):
    return jnp.roll(full, shift, axis=0)


def flip(value, bit):
    size = lax.axis_size("dp")
    return lax.ppermute(value, "dp", [(i, i ^ bit) for i in range(size)])


def dp_bits():
    return [1 << k for k in range(lax.axis_size("dp").bit_length() - 1)]


def halve(value, bit):
    half = value.shape[0] // 2
    side = (lax.axis_index("dp") // bit) % 2
    sent = lax.dynamic_slice_in_dim(value, (1 - side) * half, half, 0)
    kept = lax.dynamic_slice_in_dim(value, side * half, half, 0)
    return (kept.astype(f32) + flip(sent, bit).astype(f32)).astype(bf16)


def double(value, bit):
    side = (lax.axis_index("dp") // bit) % 2
    other = flip(value, bit)
    return jnp.where(
        side == 0,
        jnp.concatenate([value, other], axis=0),
        jnp.concatenate([other, value], axis=0),
    )


def sum_dp(value):
    bits = dp_bits()
    for bit in bits:
        value = halve(value, bit)
    for bit in reversed(bits):
        value = double(value, bit)
    return value


def after(value, *others):
    return lax.optimization_barrier((value, *others))[0]


class Ring:
    def __init__(self, parts):
        self.parts = parts
        self.nodes = nodes = lax.axis_size("dp") // 2
        chip = lax.axis_index("dp") // 2
        self.here = jnp.where(chip % 2 == 0, chip // 2, nodes - 1 - chip // 2)
        top = nodes // 2
        self.chips = [2 * p if p < top else 2 * (nodes - 1 - p) + 1 for p in range(nodes)]
        self.half = parts[0].shape[1] // 2
        self.held = {way: self.terms(self.here, way).astype(bf16) for way in (1, -1)}
        self.pieces = {1: [], -1: []}
        self.steps = 0

    def send(self, value, way):
        pairs = [
            (2 * self.chips[p] + c, 2 * self.chips[(p + way) % self.nodes] + c)
            for p in range(self.nodes)
            for c in range(2)
        ]
        return lax.ppermute(value, "dp", pairs)

    def terms(self, block, way):
        at = (block % self.nodes, 0 if way == 1 else self.half, 0)
        size = (1, self.half, self.parts[0].shape[2])
        pieces = [lax.dynamic_slice(v, at, size) for v in self.parts]
        return sum(piece.astype(f32) for piece in pieces)

    def step(self, *gates):
        count = self.steps
        if count == 2 * self.nodes - 2:
            return
        self.steps += 1
        adding = count < self.nodes - 1
        if gates:
            both = lax.optimization_barrier((self.held[1], self.held[-1], *gates))
            self.held = {1: both[0], -1: both[1]}
        for way in (1, -1):
            if count == self.nodes - 1:
                self.pieces[way].append(self.held[way])
            came = self.send(self.held[way], way)
            if adding:
                own = self.terms(self.here - way * (count + 1) + self.nodes, way)
                came = (came.astype(f32) + own).astype(bf16)
            else:
                self.pieces[way].append(came)
            self.held[way] = came

    def first(self, value):
        return after(value, *self.held.values())

    def total(self):
        return gather_pieces([p[0] for way in (1, -1) for p in self.pieces[way]])

    def order(self):
        block = jnp.arange(self.nodes, dtype=jnp.int32)
        up = (self.here + 1 - block + self.nodes) % self.nodes
        down = (block - self.here + 1 + self.nodes) % self.nodes + self.nodes
        core = lax.axis_index("dp")[None] % 2
        return jnp.concatenate([up, down, core]).astype(jnp.int32)


def gather_kernel(*refs):
    *sources, out_ref = refs
    for k, ref in enumerate(sources):
        out_ref[k] = ref[...]


def gather_pieces(pieces):
    count = len(pieces)
    vmem = pl.BlockSpec(memory_space=pltpu.VMEM)
    return pl.pallas_call(
        gather_kernel,
        in_specs=[vmem] * count,
        out_specs=vmem,
        out_shape=jax.ShapeDtypeStruct((count, *pieces[0].shape), bf16),
        compiler_params=big_vmem,
        cost_estimate=cost(0, 4 * count * pieces[0].size),
        name="gather_pieces",
    )(*pieces)


def ff_kernel(sub, x_ref, g_ref, wg_ref, wu_ref, wd_ref, gx_ref, y_ref, h_ref, gg_ref, gu_ref):
    step = pl.program_id(0)
    for at in range(0, wg_ref.shape[1], sub):
        c = slice(at, at + sub)
        gate = jnp.dot(x_ref[...], wg_ref[:, c], preferred_element_type=f32)
        up = jnp.dot(x_ref[...], wu_ref[:, c], preferred_element_type=f32)
        grad = nt_dot(g_ref[...], wd_ref[c])
        sig = 1.0 / (1.0 + jnp.exp(-gate))
        silu = gate * sig
        h_ref[:, c] = (silu * up).astype(bf16)
        gg_ref[:, c] = (grad * up * (sig + silu * (1.0 - sig))).astype(bf16)
        gu_ref[:, c] = (grad * silu).astype(bf16)
    def back(first):
        w = 256
        for at in range(0, gx_ref.shape[1], w):
            c = slice(at, at + w)
            gx = nt_dot(gg_ref[...], wg_ref[c, :]) + nt_dot(gu_ref[...], wu_ref[c, :])
            y = jnp.dot(h_ref[...], wd_ref[:, c], preferred_element_type=f32)
            if first:
                gx_ref[:, c] = gx
                y_ref[:, c] = y
            else:
                gx_ref[:, c] += gx
                y_ref[:, c] += y
    pl.when(step == 0)(lambda: back(True))
    pl.when(step > 0)(lambda: back(False))

def feed_forward(x, g, wg, wu, wd, sub=384):
    r, d = x.shape
    hid = wg.shape[1]
    chunk = hid // 3
    whole = pl.BlockSpec((r, d), lambda i: (0, 0))
    tall = pl.BlockSpec((d, chunk), lambda i: (0, i))
    wide = pl.BlockSpec((r, chunk), lambda i: (0, i))
    return pl.pallas_call(
        lambda *refs: ff_kernel(sub, *refs),
        grid=(hid // chunk,),
        in_specs=[
            whole,
            whole,
            tall,
            tall,
            pl.BlockSpec((chunk, d), lambda i: (i, 0)),
        ],
        out_specs=[whole, whole, wide, wide, wide],
        out_shape=[jax.ShapeDtypeStruct((r, d), f32)] * 2 + [jax.ShapeDtypeStruct((r, hid), bf16)] * 3,
        compiler_params=big_vmem,
        cost_estimate=cost(24 * r * d * hid, 6 * (d + r) * hid + 12 * r * d, 2 * r * hid),
        name="feed_forward",
    )(x, g, wg, wu, wd)

def grads_kernel(x0, x1, gg0, gg1, gu0, gu1, h0, h1, g0, g1, out_ref, xt, ht):
    step = pl.program_id(0)
    nodes, count, lanes = out_ref.shape
    rows = x0.shape[1] // nodes
    deep = h0.shape[1] // nodes
    r = x0.shape[0]
    @pl.when(step == 0)
    def _():
        xt[:, :r] = x0[...].T
        xt[:, r:] = x1[...].T
    @pl.when(step == 5)
    def _():
        ht[:, :r] = h0[...].T
        ht[:, r:] = h1[...].T
    def put(c, d, at):
        v = jnp.dot(xt[:, :r], c[...], preferred_element_type=f32) + jnp.dot(xt[:, r:], d[...], preferred_element_type=f32)
        out_ref[:, pl.ds(pl.multiple_of(at, 64), rows)] = v.astype(bf16).reshape(nodes, rows, lanes)
    @pl.when(step < 3)
    def _(): put(gg0, gg1, step * rows)
    @pl.when((step >= 3) & (step < 6))
    def _(): put(gu0, gu1, step * rows)
    @pl.when(step == 6)
    def _():
        v = jnp.dot(ht[:, :r], g0[:, :lanes], preferred_element_type=f32) + jnp.dot(ht[:, r:], g1[:, :lanes], preferred_element_type=f32)
        out_ref[:, 6 * rows : 6 * rows + deep] = v.astype(bf16).reshape(nodes, deep, lanes)
        v = jnp.dot(ht[:, :r], g0[:, lanes:], preferred_element_type=f32) + jnp.dot(ht[:, r:], g1[:, lanes:], preferred_element_type=f32)
        v = v.astype(bf16).reshape(nodes, deep, v.shape[1])
        short, rest = deep // 3, v.shape[2]
        for k in range(3):
            out_ref[:, 6 * rows + deep :, k * rest : (k + 1) * rest] = v[:, k * short : (k + 1) * short]

def ff_grads(side, nodes, x0, x1, gg0, gg1, gu0, gu1, h0, h1, g0, g1):
    r, d = x0.shape
    hid = gg0.shape[1]
    lanes = hid // 3
    rows, deep = d // (2 * nodes), hid // (2 * nodes)
    count = 6 * rows + deep + deep // 3
    half = lambda n: pl.BlockSpec((r, n), lambda i, s: (0, s[0]))
    first = pl.BlockSpec((r, lanes), lambda i, s: (0, jnp.minimum(i, 2)))
    second = pl.BlockSpec((r, lanes), lambda i, s: (0, jnp.clip(i - 3, 0, 2)))
    whole = pl.BlockSpec((r, d), lambda i, s: (0, 0))
    return pl.pallas_call(
        lambda s, *refs: grads_kernel(*refs),
        grid_spec=pltpu.PrefetchScalarGridSpec(
            num_scalar_prefetch=1, grid=(7,),
            in_specs=[half(d // 2)] * 2 + [first] * 2 + [second] * 2 + [half(hid // 2)] * 2 + [whole] * 2,
            out_specs=pl.BlockSpec((nodes, count, lanes), lambda i, s: (0, 0, 0)),
            scratch_shapes=[pltpu.VMEM((d // 2, 2 * r), bf16), pltpu.VMEM((hid // 2, 2 * r), bf16)],
        ),
        out_shape=jax.ShapeDtypeStruct((nodes, count, lanes), bf16),
        compiler_params=big_vmem,
        cost_estimate=cost(12 * r * d * hid, 6 * r * hid + 5 * d * hid),
        name="ff_grads",
    )(side.astype(jnp.int32).reshape(1), x0, x1, gg0, gg1, gu0, gu1, h0, h1, g0, g1)


def open_specs(nodes, group, half, lanes, first=0):
    specs = []
    for _ in range(2):
        for b in range(group):
            for at in (0, nodes):
                specs.append(
                    pl.BlockSpec(
                        (None, half, lanes),
                        lambda j, h, order, b=b, at=at: (
                            order[at + (first + j) * group + b],
                            0,
                            0,
                        ),
                    )
                )
    return specs


def open_blocks(group, order_ref, refs, write):
    core = order_ref[order_ref.shape[0] - 1]
    half = refs[0].shape[0]

    def reader(first, second):
        def read(start, stop):
            if stop <= half:
                return first[start:stop].astype(f32)
            if start >= half:
                return second[start - half : stop - half].astype(f32)
            pieces = [first[start:half], second[0 : stop - half]]
            return jnp.concatenate([p.astype(f32) for p in pieces], axis=0)

        return read

    def hand(refs):
        for b in range(group):
            write(b, reader(refs[2 * b], refs[2 * b + 1]))

    own = pl.program_id(1) == core
    pl.when(own)(lambda: hand(refs[: 2 * group]))
    pl.when(jnp.logical_not(own))(lambda: hand(refs[2 * group :]))


def open_ff_kernel(group, order_ref, *refs):
    *pieces, gate_ref, up_ref, down_ref = refs
    lanes = pieces[0].shape[1]
    rows, deep = gate_ref.shape[0] // group, down_ref.shape[0] // group
    rest = down_ref.shape[1] - lanes
    short = deep // 3

    def write(b, read):
        here = slice(b * rows, (b + 1) * rows)
        for k, out in enumerate((gate_ref, up_ref)):
            for c in range(3):
                part = read((3 * k + c) * rows, (3 * k + c + 1) * rows)
                out[here, c * lanes : (c + 1) * lanes] = part
        low, at = b * deep, 6 * rows
        down_ref[low : low + deep, :lanes] = read(at, at + deep)
        for c in range(3):
            part = read(at + deep, at + deep + short)[:, c * rest : (c + 1) * rest]
            down_ref[low + c * short : low + (c + 1) * short, lanes:] = part

    open_blocks(group, order_ref, pieces, write)


def open_ff(pieces, order, at, so_far, width, hidden):
    mine, other = pieces
    half, lanes = mine.shape[1:]
    nodes, group = mine.shape[0] // 2, 2
    steps = nodes // group
    rows, deep = width // (2 * nodes), hidden // (2 * nodes)
    out = lambda tall, wide: pl.BlockSpec(
        (group * tall, wide), lambda j, h, order: (h * steps + at, 0)
    )
    specs = open_specs(nodes, group, half, lanes, at)
    shapes = [(width, hidden), (width, hidden), (hidden, width)]
    kernel = lambda order, *refs: open_ff_kernel(
        group, order, *refs[: 4 * group], *refs[4 * group + len(so_far) :]
    )
    return pl.pallas_call(
        kernel,
        grid_spec=pltpu.PrefetchScalarGridSpec(
            num_scalar_prefetch=1,
            grid=(1, 2),
            in_specs=specs + [pl.BlockSpec(memory_space=pl.ANY)] * len(so_far),
            out_specs=[out(rows, hidden), out(rows, hidden), out(deep, width)],
        ),
        out_shape=[jax.ShapeDtypeStruct(shape, f32) for shape in shapes],
        input_output_aliases={1 + 4 * group + k: k for k in range(len(so_far))},
        compiler_params=big_vmem,
        cost_estimate=cost(0, 24 * width * hidden // steps),
        name="open_ff",
    )(order, *[mine] * (2 * group), *[other] * (2 * group), *so_far)


def pack_conv_kernel(core_ref, in_ref, out_w_ref, tail_ref, away_ref, own_ref):
    blocks, _, width = own_ref.shape
    rows = in_ref.shape[0] // (2 * blocks)
    deep = out_w_ref.shape[0] // blocks
    lanes = width // 2

    def write(ref):
        for k in range(blocks):
            ref[k, 0:rows, 0:lanes] = in_ref[2 * k * rows : (2 * k + 1) * rows]
            ref[k, 0:rows, lanes:] = in_ref[(2 * k + 1) * rows : (2 * k + 2) * rows]
            ref[k, rows : rows + deep] = out_w_ref[k * deep : (k + 1) * deep]
            ref[k, rows + deep :] = tail_ref[...]

    pl.when(pl.program_id(0) == 0)(lambda: write(away_ref))
    pl.when(pl.program_id(0) == 1)(lambda: write(own_ref))


def pack_conv(grad_in, grad_out, tail, part, nodes):
    total, width = grad_in.shape
    half_in, half_out = total // 2, grad_out.shape[0] // 4
    spared = tail.shape[0]
    count = half_in // (2 * nodes) + half_out // nodes + spared
    core = (lax.axis_index("dp") % 2).astype(jnp.int32).reshape(1)
    side = lambda i, c: jnp.where(i == 0, 1 - c[0], c[0])
    out = pl.BlockSpec((nodes, count, width), lambda i, c: (0, 0, 0))
    return pl.pallas_call(
        pack_conv_kernel,
        grid_spec=pltpu.PrefetchScalarGridSpec(
            num_scalar_prefetch=1,
            grid=(2,),
            in_specs=[
                pl.BlockSpec((half_in, width // 2), lambda i, c: (side(i, c), part)),
                pl.BlockSpec((half_out, width), lambda i, c: (2 * part + side(i, c), 0)),
                pl.BlockSpec((spared, width), lambda i, c: (0, 0)),
            ],
            out_specs=[out, out],
        ),
        out_shape=[jax.ShapeDtypeStruct((nodes, count, width), bf16)] * 2,
        compiler_params=big_vmem,
        cost_estimate=cost(0, 2 * (grad_in.size + grad_out.size)),
        name="pack_conv",
    )(core, grad_in, grad_out, tail)


def open_conv_kernel(group, order_ref, *refs):
    *pieces, in_ref, out_w_ref, tail_ref = refs
    rows, lanes = in_ref.shape[0] // (2 * group), in_ref.shape[1]
    deep = out_w_ref.shape[0] // group

    def write(b, read):
        low = 2 * b * rows
        in_ref[low : low + rows] = read(0, rows)[:, :lanes]
        in_ref[low + rows : low + 2 * rows] = read(0, rows)[:, lanes:]
        out_w_ref[b * deep : (b + 1) * deep] = read(rows, rows + deep)
        tail_ref[b] = read(rows + deep, rows + deep + tail_ref.shape[1])

    open_blocks(group, order_ref, pieces, write)


def open_conv(ring, gate, total, deep_total):
    mine = after(ring.total(), gate)
    other = flip(mine, 1)
    _, half, width = mine.shape
    nodes, group = ring.nodes, ring.nodes // 2
    blocks = 2 * nodes
    steps = nodes // group
    rows, deep = total // blocks, deep_total // blocks
    spared = 2 * half - rows // 2 - deep
    at = lambda j, h, order: (h * steps + j, 0)
    return pl.pallas_call(
        lambda *refs: open_conv_kernel(group, *refs),
        grid_spec=pltpu.PrefetchScalarGridSpec(
            num_scalar_prefetch=1,
            grid=(steps, 2),
            in_specs=open_specs(nodes, group, half, width),
            out_specs=[
                pl.BlockSpec((group * rows, width // 2), at),
                pl.BlockSpec((group * deep, width), at),
                pl.BlockSpec(
                    (group, spared, width), lambda j, h, order: (h * steps + j, 0, 0)
                ),
            ],
        ),
        out_shape=[
            jax.ShapeDtypeStruct((total, width // 2), f32),
            jax.ShapeDtypeStruct((deep_total, width), f32),
            jax.ShapeDtypeStruct((blocks, spared, width), f32),
        ],
        compiler_params=big_vmem,
        cost_estimate=cost(0, 8 * (total + deep_total) * width),
        name="open_conv",
    )(ring.order(), *[mine] * (2 * group), *[other] * (2 * group))


def on_device(
    tokens,
    cotangent,
    route,
    seq_lengths,
    norm1_gain,
    in_weight,
    conv_weight,
    out_weight,
    norm2_gain,
    gate_weight,
    up_weight,
    down_weight,
):
    dp_size = lax.axis_size("dp")
    mp_size = lax.axis_size("mp")
    dp_index = lax.axis_index("dp")
    mp_index = lax.axis_index("mp")
    rows = tokens.shape[0]
    narrow = tokens.shape[1]
    width = norm1_gain.shape[0]
    own = rows // mp_size
    start = mp_index * own
    column = mp_index * narrow
    pair_share = rows // dp_size
    slots = pair_share + pair_share // 2
    paired = mp_size == 2

    if paired:
        core = dp_index % 2
        deep = width // 2
        part_in = lax.dynamic_slice_in_dim(in_weight, core * deep, deep, 1)
        part_out = lax.dynamic_slice_in_dim(out_weight, core * deep, deep, 1)
        part = jnp.concatenate([part_in, part_out.reshape(1, deep, deep)], axis=0)
        there = swap_mp(part)
        route = after(route, part)
        taps = jnp.concatenate([conv_weight, swap_mp(conv_weight)], axis=1)
    else:
        full_in = lax.all_gather(in_weight, "mp", axis=2, tiled=True)
        full_out = lax.all_gather(out_weight, "mp", axis=0, tiled=True)
        taps = lax.all_gather(conv_weight, "mp", axis=1, tiled=True)

    sent_rows, digits, slot_of = pack(route, tokens, dp_size, slots)
    sent_seeds = send_rows(after(slot_of, sent_rows), cotangent, dp_size, slots)
    over = dict(split_axis=0, concat_axis=0, tiled=True)
    got_rows = lax.all_to_all(sent_rows, "dp", **over)
    digits = got_rows if slots <= narrow else lax.all_to_all(digits, "dp", **over)
    got_rows, sent_seeds = lax.optimization_barrier((got_rows, sent_seeds))
    got_seeds = lax.all_to_all(sent_seeds, "dp", **over)
    slot_of = slot_of.reshape(rows, 1)
    window = own + 2 * halo
    if paired:
        bases = jnp.stack([start, own - start]).astype(jnp.int32)
        digits = got_rows if slots <= narrow else digits
        pieces, places = place_rows(bases - halo, digits, got_rows, slots, rows, window)
        there, _ = lax.optimization_barrier((there, pieces))
        here = flip(there, 1)
        both = [jnp.where(core == k, there, here) for k in range(2)]
        other_in = jnp.concatenate([v[:3] for v in both], axis=1)
        other_out = jnp.concatenate([v[3] for v in both], axis=1)
        full_in = jnp.concatenate([in_weight, other_in], axis=2)
        full_out = jnp.concatenate([out_weight, other_out], axis=0)
        input_rows = side_by_side(pieces[0], swap_mp(pieces[1]), mp_index)
        pieces, _ = place_rows(bases, digits, got_seeds, slots, rows, own)
        input_rows = after(input_rows, pieces)
        came = swap_mp(pieces[1])
        seeds_here = came
        seeds_own = side_by_side(pieces[0], came, mp_index)
        seeds_other = side_by_side(pieces[1], swap_mp(after(pieces[0], came)), mp_index)
        place_ids = ((places - start) % rows).reshape(-1, 1)
    else:
        bases = (jnp.arange(mp_size) * own).astype(jnp.int32)
        pieces, places = place_rows(bases, digits, got_rows, slots, rows, own)
        full = lax.all_gather(pieces.reshape(rows, narrow), "mp", axis=1, tiled=True)
        full = jnp.pad(full, ((halo, halo), (0, 0)))
        input_rows = lax.dynamic_slice_in_dim(full, start, window, 0)
        pieces, _ = place_rows(bases, digits, got_seeds, slots, rows, own)
        full = lax.all_gather(pieces.reshape(rows, narrow), "mp", axis=1, tiled=True)
        seeds = rolled(full, -start)
        seeds_own, seeds_other = seeds[:own], seeds[own:]
        seeds_here = seeds_own
        place_ids = places.reshape(-1, 1)

    positions = start - halo + jnp.arange(window, dtype=jnp.int32)
    first_mask, second_mask = seq_masks(seq_lengths[0], positions, rows)
    residual = input_rows.astype(f32)
    scale_one = lax.rsqrt(jnp.mean(residual * residual, axis=1) + epsilon)[:, None]
    normed_one = (residual * scale_one * norm1_gain).astype(bf16)
    projected = jnp.einsum("rd,kdc->krc", normed_one, full_in, preferred_element_type=f32)
    projected = after(projected, seeds_here)
    in_gate, out_gate, value_part = (projected[0], projected[1], projected[2])
    mixed = in_gate * value_part
    lag_one = lag_rows(mixed, 1) * first_mask
    lag_two = lag_rows(mixed, 2) * second_mask
    convolved = taps[2] * mixed + taps[1] * lag_one + taps[0] * lag_two
    gated = (out_gate * convolved).astype(bf16)
    middle = (residual + jnp.dot(gated, full_out, preferred_element_type=f32))[halo:]
    scale_two = lax.rsqrt(jnp.mean(middle * middle, axis=1) + epsilon)[:, None]
    normed_own = (middle[:own] * scale_two[:own] * norm2_gain).astype(bf16)

    weights = (gate_weight, up_weight, down_weight)
    if paired:
        normed_other = swap_mp(normed_own)
        first = feed_forward(normed_own, seeds_own, *weights)
        second = feed_forward(normed_other, seeds_other, *weights)
        sent = jnp.concatenate([second[0], first[0][:halo]], axis=0).astype(bf16)
        came = swap_mp(sent)
        saved = (normed_other, first[3], second[3], first[4], second[4])
        saved += (first[2], second[2], seeds_own, seeds_other)
        away = ff_grads(1 - core, dp_size // 2, after(normed_own, sent), *saved)
        kept = ff_grads(core, dp_size // 2, after(normed_own, away), *saved)
        away = flip(away, 1)
        came, _ = lax.optimization_barrier((came, kept))
        grad_normed_two = jnp.concatenate([first[0], second[0][:halo]], axis=0)
        grad_normed_two = grad_normed_two + came.astype(f32)
        down_came = swap_mp(after(second[1].astype(bf16), came))
        ring = Ring((kept, away))
        grad_normed_two = ring.first(grad_normed_two)
        ring.step()
    else:
        normed_two = rolled(lax.all_gather(normed_own, "mp", axis=0, tiled=True), -start)
        gate_val = jnp.dot(normed_two, gate_weight, preferred_element_type=f32)
        up_val = jnp.dot(normed_two, up_weight, preferred_element_type=f32)
        sigmoid_val = jax.nn.sigmoid(gate_val)
        silu_val = gate_val * sigmoid_val
        hidden = (silu_val * up_val).astype(bf16)
        grad_hidden = nt_dot(seeds, down_weight)
        grad_gate_val = (
            grad_hidden * up_val * sigmoid_val * (1.0 + gate_val * (1.0 - sigmoid_val))
        ).astype(bf16)
        grad_up_val = (grad_hidden * silu_val).astype(bf16)
        normed_terms = nt_dot(grad_gate_val, gate_weight) + nt_dot(grad_up_val, up_weight)
        down_terms = jnp.dot(hidden, down_weight, preferred_element_type=f32)
        full = rolled(lax.psum(rolled(normed_terms, start), "mp"), -start)
        grad_normed_two = full[: own + halo]
        down_sum = rolled(lax.psum(rolled(down_terms, start), "mp"), -start)[:own]
        total_gate = sum_dp(tn_dot(normed_two, grad_gate_val).astype(bf16)).astype(f32)
        total_up = sum_dp(tn_dot(normed_two, grad_up_val).astype(bf16)).astype(f32)
        total_down = sum_dp(tn_dot(hidden, seeds).astype(bf16)).astype(f32)
        block_own = (middle[:own] + down_sum).astype(bf16)

    def to_features(mine):
        if not paired:
            full = lax.all_gather(mine, "mp", axis=0, tiled=True)
            return lax.dynamic_slice_in_dim(full, column, narrow, 1)
        low, high = mine[:, :narrow], mine[:, narrow:]
        other = swap_mp(jnp.where(mp_index == 0, high, low))
        return jnp.concatenate([jnp.where(mp_index == 0, low, high), other], axis=0)

    shape = (dp_size, slots, narrow)
    back_block = min(8 * slots, slots * dp_size)
    home_block = min(rows, 512)

    def leave(piece):
        return take_rows(place_ids, piece, back_block, bf16).reshape(shape)

    def to_home(back):
        return lax.all_to_all(back, "dp", **over)

    def arrive(home, dtype):
        return take_rows(slot_of, home.reshape(-1, narrow), home_block, dtype)

    gain_two_term = jnp.sum((grad_normed_two * middle * scale_two)[:own], axis=0)
    dot_two = jnp.sum(norm2_gain * grad_normed_two * middle, axis=1, keepdims=True)
    grad_middle = (
        jnp.concatenate([seeds_own, seeds_other[:halo]], axis=0).astype(f32)
        + scale_two * norm2_gain * grad_normed_two
        - middle * (scale_two * scale_two * scale_two * dot_two / width)
    )
    grad_mix = grad_middle.astype(bf16)
    grad_gated = jnp.einsum("rd,cd->rc", grad_mix, full_out, preferred_element_type=f32)
    if paired:
        grad_gated = ring.first(grad_gated)
        ring.step()
    grad_conv = grad_gated * out_gate[halo:]
    inner = slice(halo, halo + own)
    conv_terms = jnp.stack(
        [
            jnp.sum(grad_conv[:own] * lag_two[inner], axis=0),
            jnp.sum(grad_conv[:own] * lag_one[inner], axis=0),
            jnp.sum(grad_conv[:own] * mixed[inner], axis=0),
        ],
        axis=0,
    )
    grad_mixed = (
        taps[2] * grad_conv
        + taps[1] * lead_rows(grad_conv * first_mask[halo:], 1)
        + taps[0] * lead_rows(grad_conv * second_mask[halo:], 2)
    )[:own]
    grad_parts = jnp.stack(
        [
            grad_mixed * value_part[inner],
            grad_gated[:own] * convolved[inner],
            grad_mixed * in_gate[inner],
        ],
        axis=0,
    ).astype(bf16)
    grad_in = jnp.einsum(
        "rd,krc->kdc", normed_one[inner], grad_parts, preferred_element_type=f32
    ).astype(bf16)
    grad_out = jnp.einsum(
        "rc,rd->cd", gated[inner], grad_mix[:own], preferred_element_type=f32
    ).astype(bf16)
    taps_end = 2 + conv_weight.shape[0]

    parts_late = grad_parts
    if paired:
        ring.step()
        parts_late = ring.first(grad_parts)
    grad_normed_one = jnp.einsum("krc,kdc->rd", parts_late, full_in, preferred_element_type=f32)
    residual_own = residual[inner]
    scale_own = scale_one[inner]
    gain_one_term = jnp.sum(grad_normed_one * residual_own * scale_own, axis=0)
    dot_one = jnp.sum(norm1_gain * grad_normed_one * residual_own, axis=1, keepdims=True)
    input_own = (
        grad_middle[:own]
        + scale_own * norm1_gain * grad_normed_one
        - residual_own * (scale_own * scale_own * scale_own * dot_one / width)
    ).astype(bf16)

    def packed_half(k, *gates):
        lanes = slice(k * narrow, (k + 1) * narrow)
        terms = jnp.pad(conv_terms[:, lanes], ((0, 16 - taps_end), (0, width - narrow)))
        gains = jnp.stack([gain_one_term, gain_two_term], axis=0)
        ends = after(jnp.concatenate([gains, terms], axis=0).astype(bf16), *gates)
        return pack_conv(grad_in.reshape(-1, width), grad_out, ends, k, dp_size // 2)

    if paired:
        away, other = packed_half(1)
        passed = (other.astype(f32) + flip(away, 1).astype(f32)).astype(bf16)
        down_came = after(down_came, grad_parts)
        block_own = (middle[:own] + (first[1] + down_came.astype(f32))).astype(bf16)
        block_piece = to_features(block_own)
        block_back = leave(block_piece)
        out_home = to_home(block_back)
        ring.step(block_piece)
        ring.step(passed)
        away, own_half = packed_half(0, passed)
        passed = swap_mp(passed)
        input_piece = to_features(input_own)
        ring.step(input_piece)
        input_back = leave(after(input_piece, out_home))
        grad_home = to_home(input_back)
        second = Ring((own_half, flip(away, 1), passed))
        ring.step(*second.held.values(), out_home)
        second.step()
        block_out = arrive(out_home, bf16)
        ring.step(*second.held.values(), grad_home)
        second.step(block_out)
        tokens_grad = arrive(grad_home, f32)
        ring.step(*second.held.values())
        second.step()
        ring.step(*second.held.values(), tokens_grad)
        second.step()
        while ring.steps < 2 * ring.nodes - 2:
            ring.step(*second.held.values())
            second.step()
        mine = ring.total()
        pieces = (mine, flip(mine, 1))
        second.step(mine)
        totals = ()
        for at in range(ring.nodes // 2):
            totals = open_ff(pieces, ring.order(), at, totals, width, gate_weight.shape[1])
            second.step(*totals)
        while second.steps < 2 * second.nodes - 2:
            second.step()
        total_gate, total_up, total_down = totals
        total_in, total_out, ends = open_conv(
            second, total_gate, grad_in.size // (2 * narrow), narrow
        )
        tail = ends[0]
    else:
        block_out = arrive(to_home(leave(to_features(block_own))), bf16)
        tokens_grad = arrive(to_home(leave(to_features(input_own))), f32)
        total_in = lax.psum_scatter(
            grad_in.astype(f32), "mp", scatter_dimension=2, tiled=True
        )
        total_in = sum_dp(total_in.astype(bf16).reshape(-1, narrow)).astype(f32)
        total_out = lax.psum_scatter(
            grad_out.astype(f32), "mp", scatter_dimension=0, tiled=True
        )
        total_out = sum_dp(total_out.astype(bf16)).astype(f32)
        gains = lax.psum(jnp.stack([gain_one_term, gain_two_term]), ("dp", "mp"))
        terms = lax.psum_scatter(conv_terms, "mp", scatter_dimension=1, tiled=True)
        terms = jnp.pad(lax.psum(terms, "dp"), ((0, 0), (0, width - narrow)))
        tail = jnp.concatenate([gains, terms], axis=0)
    total_taps = tail[2:taps_end, :narrow]
    return (
        block_out,
        tokens_grad,
        tail[0],
        total_in.reshape(in_weight.shape),
        total_taps,
        total_out,
        tail[1],
        total_gate,
        total_up,
        total_down,
    )


def solution(mesh):
    in_specs = (
        P("dp", "mp"),
        P("dp", "mp"),
        P("dp"),
        P("dp", None),
        P(),
        P(None, None, "mp"),
        P(None, "mp"),
        P("mp", None),
        P(),
        P(None, "mp"),
        P(None, "mp"),
        P("mp", None),
    )
    out_specs = (
        P("dp", "mp"),
        P("dp", "mp"),
        P(),
        P(None, None, "mp"),
        P(None, "mp"),
        P("mp", None),
        P(),
        P(None, "mp"),
        P(None, "mp"),
        P("mp", None),
    )
    return jax.shard_map(
        on_device, mesh=mesh, in_specs=in_specs, out_specs=out_specs, check_vma=False
    )
```

```python
import jax
import jax.numpy as jnp
from jax import lax
from jax.experimental import pallas as pl
from jax.experimental.pallas import tpu as pltpu
from jax.sharding import PartitionSpec as P

epsilon = 1e-05
f32 = jnp.float32
bf16 = jnp.bfloat16
halo = 8
spare = 8
small_vmem = pltpu.CompilerParams(vmem_limit_bytes=26 << 20)
forward_vmem = pltpu.CompilerParams(vmem_limit_bytes=40 << 20)
big_vmem = pltpu.CompilerParams(vmem_limit_bytes=48 << 20)


def cost(flops, moved, transcendentals=0):
    return pl.CostEstimate(
        flops=int(flops), bytes_accessed=int(moved), transcendentals=int(transcendentals)
    )


def lag_rows(values, shift):
    return jnp.concatenate(
        [jnp.zeros((shift, values.shape[1]), values.dtype), values[:-shift]], axis=0
    )


def lead_rows(values, shift):
    return jnp.concatenate(
        [values[shift:], jnp.zeros((shift, values.shape[1]), values.dtype)], axis=0
    )


def seq_masks(lengths, positions, row_count):
    count = lengths.shape[0]
    before = jnp.arange(count)[:, None] < jnp.arange(count)[None, :]
    starts = jnp.sum(jnp.where(before, lengths[:, None], 0), axis=0, dtype=jnp.int32)
    started = positions[:, None] >= starts[None, :]
    seq_first = jnp.max(jnp.where(started, starts[None, :], 0), axis=1)
    offset = positions - seq_first
    inside = (positions >= 0) & (positions < row_count)
    return (
        ((offset >= 1) & inside).astype(f32)[:, None],
        ((offset >= 2) & inside).astype(f32)[:, None],
    )


def nt_dot(left, right):
    return lax.dot_general(
        left, right, (((1,), (1,)), ((), ())), preferred_element_type=f32
    )


def tn_dot(left, right):
    return lax.dot_general(
        left, right, (((0,), (0,)), ((), ())), preferred_element_type=f32
    )


def rank_kernel(rows, members, slots, route_ref, slot_ref):
    target = route_ref[...] // rows
    width = min(rows, 512)
    owner = lax.broadcasted_iota(jnp.int32, (members, rows), 0)
    one_hot = jnp.where(owner == target, 1.0, 0.0)
    left = one_hot.astype(bf16)
    for start in range(0, rows, width):
        first = lax.broadcasted_iota(jnp.int32, (rows, width), 0)
        second = lax.broadcasted_iota(jnp.int32, (rows, width), 1) + start
        earlier = jnp.where(first < second, 1.0, 0.0).astype(bf16)
        rank = jnp.dot(left, earlier, preferred_element_type=f32)
        piece = one_hot[:, start : start + width]
        mine = jnp.sum(rank * piece, axis=0, keepdims=True).astype(jnp.int32)
        slot_ref[:, start : start + width] = (
            target[:, start : start + width] * slots + mine
        )


def pack_kernel(rows, members, slots, route_ref, x_ref, sx_ref, digit_ref, slot_ref):
    step = pl.program_id(0)
    group = sx_ref.shape[0]

    @pl.when(step == 0)
    def _():
        rank_kernel(rows, members, slots, route_ref, slot_ref)

    place = route_ref[...] % rows
    row = lax.broadcasted_iota(jnp.int32, (8, rows), 0)
    digits = jnp.where(
        row == 0,
        (place // 64).astype(f32),
        jnp.where(row == 1, (place % 64).astype(f32), 1.0),
    ).astype(bf16)
    ids = lax.broadcasted_iota(jnp.int32, (group * slots, rows), 0)
    pick = jnp.where(slot_ref[...] == ids + step * group * slots, 1.0, 0.0).astype(bf16)
    sent = jnp.dot(pick, x_ref[...], preferred_element_type=f32).astype(bf16)
    for k in range(group):
        here = slice(k * slots, (k + 1) * slots)
        sx_ref[k, 0:slots] = sent[here]
        coded = nt_dot(digits, pick[here]).astype(bf16)
        if sx_ref.shape[1] > slots:
            sx_ref[k, slots : slots + spare] = jnp.zeros((spare, sx_ref.shape[2]), bf16)
            sx_ref[k, slots : slots + spare, 0:slots] = coded
        else:
            digit_ref[k] = jnp.zeros(digit_ref.shape[1:], bf16)
            digit_ref[k, :, 0:slots] = coded


def pack(route, tokens, members, slots):
    rows, width = tokens.shape
    group = min(members, 4)
    inside = slots <= width
    span = slots + spare if inside else slots
    whole = lambda j: (0, 0)
    block = lambda *tail: pl.BlockSpec((group, *tail), lambda j: (j, 0, 0))
    lanes = 8 if inside else 256
    return pl.pallas_call(
        lambda *refs: pack_kernel(rows, members, slots, *refs),
        grid=(members // group,),
        in_specs=[pl.BlockSpec((1, rows), whole), pl.BlockSpec((rows, width), whole)],
        out_specs=[block(span, width), block(8, lanes), pl.BlockSpec((1, rows), whole)],
        out_shape=[
            jax.ShapeDtypeStruct((members, span, width), bf16),
            jax.ShapeDtypeStruct((members, 8, lanes), bf16),
            jax.ShapeDtypeStruct((1, rows), jnp.int32),
        ],
        compiler_params=small_vmem,
        cost_estimate=cost(2 * members * slots * rows * width, 5 * rows * width),
        name="pack",
    )(route.reshape(1, rows), tokens)


def send_kernel(slots, slot_ref, x_ref, out_ref):
    group = out_ref.shape[0]
    count = group * slots
    ids = lax.broadcasted_iota(jnp.int32, (count, x_ref.shape[0]), 0)
    pick = jnp.where(slot_ref[...] == ids + pl.program_id(0) * count, 1.0, 0.0)
    sent = jnp.dot(pick.astype(bf16), x_ref[...], preferred_element_type=f32)
    for k in range(group):
        out_ref[k] = sent[k * slots : (k + 1) * slots].astype(bf16)


def send_rows(slot_of, source, members, slots):
    rows, width = source.shape
    group = min(members, 8)
    return pl.pallas_call(
        lambda *refs: send_kernel(slots, *refs),
        grid=(members // group,),
        in_specs=[
            pl.BlockSpec((1, rows), lambda j: (0, 0)),
            pl.BlockSpec((rows, width), lambda j: (0, 0)),
        ],
        out_specs=pl.BlockSpec((group, slots, width), lambda j: (j, 0, 0)),
        out_shape=jax.ShapeDtypeStruct((members, slots, width), bf16),
        compiler_params=small_vmem,
        cost_estimate=cost(2 * members * slots * rows * width, 5 * rows * width),
        name="send_rows",
    )(slot_of, source)


def place_kernel(rows, bases_ref, digit_ref, got_ref, out_ref, place_ref, src, pick):
    members, slots = got_ref.shape[0], got_ref.shape[1]
    count = out_ref.shape[0]
    span = src.shape[0] // members
    base = bases_ref[pl.program_id(0)]
    ids = lax.broadcasted_iota(jnp.int32, (count, span), 0) + base

    @pl.when(pl.program_id(0) == 0)
    def _():
        for j in range(members):
            src[j * span : j * span + slots] = got_ref[j]
            if span > slots:
                src[j * span + slots : (j + 1) * span] = jnp.zeros(
                    (span - slots, src.shape[1]), bf16
                )

    for j in range(members):
        coded = digit_ref[j].astype(f32)[:, 0:span]
        value = coded[0:1] * 64.0 + coded[1:2]
        places = jnp.where(coded[2:3] > 0.5, value, 4.0 * rows).astype(jnp.int32)
        pick[:, j * span : (j + 1) * span] = jnp.where(places == ids, 1.0, 0.0).astype(bf16)
        place_ref[j : j + 1, :] = places[:, 0:slots]
    out_ref[...] = jnp.dot(pick[...], src[...], preferred_element_type=f32).astype(bf16)


def place_rows(bases, digits, got, slots, rows, count):
    members, width = got.shape[0], got.shape[2]
    at = digits.shape[1] // 8 - 1
    span = -(-slots // 128) * 128
    return pl.pallas_call(
        lambda *refs: place_kernel(rows, *refs),
        grid_spec=pltpu.PrefetchScalarGridSpec(
            num_scalar_prefetch=1,
            grid=(bases.shape[0],),
            in_specs=[
                pl.BlockSpec((members, 8, digits.shape[2]), lambda i, b: (0, at, 0)),
                pl.BlockSpec((members, slots, width), lambda i, b: (0, 0, 0)),
            ],
            out_specs=[
                pl.BlockSpec((None, count, width), lambda i, b: (i, 0, 0)),
                pl.BlockSpec((members, slots), lambda i, b: (0, 0)),
            ],
            scratch_shapes=[
                pltpu.VMEM((members * span, width), bf16),
                pltpu.VMEM((count, members * span), bf16),
            ],
        ),
        out_shape=[
            jax.ShapeDtypeStruct((bases.shape[0], count, width), bf16),
            jax.ShapeDtypeStruct((members, slots), jnp.int32),
        ],
        compiler_params=small_vmem,
        cost_estimate=cost(0, (bases.shape[0] * count + members * slots) * width // 8),
        name="place_rows",
    )(bases, digits, got)


def take_kernel(ids_ref, from_ref, out_ref):
    cols = lax.broadcasted_iota(jnp.int32, (out_ref.shape[0], from_ref.shape[0]), 1)
    pick = jnp.where(ids_ref[...] == cols, 1.0, 0.0).astype(bf16)
    out_ref[...] = jnp.dot(pick, from_ref[...], preferred_element_type=f32).astype(
        out_ref.dtype
    )


def take_rows(ids, source, block, dtype):
    count = ids.shape[0]
    total, width = source.shape
    return pl.pallas_call(
        take_kernel,
        grid=(count // block,),
        in_specs=[
            pl.BlockSpec((block, 1), lambda i: (i, 0)),
            pl.BlockSpec((total, width), lambda i: (0, 0)),
        ],
        out_specs=pl.BlockSpec((block, width), lambda i: (i, 0)),
        out_shape=jax.ShapeDtypeStruct((count, width), dtype),
        compiler_params=small_vmem,
        cost_estimate=cost(2 * count * total * width, 2 * (count + total) * width),
        name="take_rows",
    )(ids, source)


def swap_mp(value):
    return lax.ppermute(value, "mp", [(0, 1), (1, 0)])


def side_by_side(mine, other, index):
    return jnp.where(
        index == 0,
        jnp.concatenate([mine, other], axis=1),
        jnp.concatenate([other, mine], axis=1),
    )


def rolled(full, shift):
    return jnp.roll(full, shift, axis=0)


def flip(value, bit):
    size = lax.axis_size("dp")
    return lax.ppermute(value, "dp", [(i, i ^ bit) for i in range(size)])


def dp_bits():
    return [1 << k for k in range(lax.axis_size("dp").bit_length() - 1)]


def halve(value, bit):
    half = value.shape[0] // 2
    side = (lax.axis_index("dp") // bit) % 2
    sent = lax.dynamic_slice_in_dim(value, (1 - side) * half, half, 0)
    kept = lax.dynamic_slice_in_dim(value, side * half, half, 0)
    return (kept.astype(f32) + flip(sent, bit).astype(f32)).astype(bf16)


def double(value, bit):
    side = (lax.axis_index("dp") // bit) % 2
    other = flip(value, bit)
    return jnp.where(
        side == 0,
        jnp.concatenate([value, other], axis=0),
        jnp.concatenate([other, value], axis=0),
    )


def sum_dp(value):
    bits = dp_bits()
    for bit in bits:
        value = halve(value, bit)
    for bit in reversed(bits):
        value = double(value, bit)
    return value


def after(value, *others):
    return lax.optimization_barrier((value, *others))[0]


class Ring:
    def __init__(self, parts):
        self.parts = parts
        self.nodes = nodes = lax.axis_size("dp") // 2
        chip = lax.axis_index("dp") // 2
        self.here = jnp.where(chip % 2 == 0, chip // 2, nodes - 1 - chip // 2)
        top = nodes // 2
        self.chips = [2 * p if p < top else 2 * (nodes - 1 - p) + 1 for p in range(nodes)]
        self.half = parts[0].shape[1] // 2
        self.held = {way: self.terms(self.here, way).astype(bf16) for way in (1, -1)}
        self.pieces = {1: [], -1: []}
        self.steps = 0

    def send(self, value, way):
        pairs = [
            (2 * self.chips[p] + c, 2 * self.chips[(p + way) % self.nodes] + c)
            for p in range(self.nodes)
            for c in range(2)
        ]
        return lax.ppermute(value, "dp", pairs)

    def terms(self, block, way):
        at = (block % self.nodes, 0 if way == 1 else self.half, 0)
        size = (1, self.half, self.parts[0].shape[2])
        pieces = [lax.dynamic_slice(v, at, size) for v in self.parts]
        return sum(piece.astype(f32) for piece in pieces)

    def step(self, *gates):
        count = self.steps
        if count == 2 * self.nodes - 2:
            return
        self.steps += 1
        adding = count < self.nodes - 1
        if gates:
            both = lax.optimization_barrier((self.held[1], self.held[-1], *gates))
            self.held = {1: both[0], -1: both[1]}
        for way in (1, -1):
            if count == self.nodes - 1:
                self.pieces[way].append(self.held[way])
            came = self.send(self.held[way], way)
            if adding:
                own = self.terms(self.here - way * (count + 1) + self.nodes, way)
                came = (came.astype(f32) + own).astype(bf16)
            else:
                self.pieces[way].append(came)
            self.held[way] = came

    def first(self, value):
        return after(value, *self.held.values())

    def total(self):
        return gather_pieces([p[0] for way in (1, -1) for p in self.pieces[way]])

    def order(self):
        block = jnp.arange(self.nodes, dtype=jnp.int32)
        up = (self.here + 1 - block + self.nodes) % self.nodes
        down = (block - self.here + 1 + self.nodes) % self.nodes + self.nodes
        core = lax.axis_index("dp")[None] % 2
        return jnp.concatenate([up, down, core]).astype(jnp.int32)


def gather_kernel(*refs):
    *sources, out_ref = refs
    for k, ref in enumerate(sources):
        out_ref[k] = ref[...]


def gather_pieces(pieces):
    count = len(pieces)
    vmem = pl.BlockSpec(memory_space=pltpu.VMEM)
    return pl.pallas_call(
        gather_kernel,
        in_specs=[vmem] * count,
        out_specs=vmem,
        out_shape=jax.ShapeDtypeStruct((count, *pieces[0].shape), bf16),
        compiler_params=small_vmem,
        cost_estimate=cost(0, 4 * count * pieces[0].size),
        name="gather_pieces",
    )(*pieces)


def ff_kernel(sub, x_ref, g_ref, wg_ref, wu_ref, wd_ref, gx_ref, y_ref, h_ref, gg_ref, gu_ref):
    step = pl.program_id(0)
    for at in range(0, wg_ref.shape[1], sub):
        c = slice(at, at + sub)
        gate = jnp.dot(x_ref[...], wg_ref[:, c], preferred_element_type=f32)
        up = jnp.dot(x_ref[...], wu_ref[:, c], preferred_element_type=f32)
        grad = nt_dot(g_ref[...], wd_ref[c])
        sig = 1.0 / (1.0 + jnp.exp(-gate))
        silu = gate * sig
        h_ref[:, c] = (silu * up).astype(bf16)
        gg_ref[:, c] = (grad * up * (sig + silu * (1.0 - sig))).astype(bf16)
        gu_ref[:, c] = (grad * silu).astype(bf16)
    def back(first):
        w = 256
        for at in range(0, gx_ref.shape[1], w):
            c = slice(at, at + w)
            gx = nt_dot(gg_ref[...], wg_ref[c, :]) + nt_dot(gu_ref[...], wu_ref[c, :])
            y = jnp.dot(h_ref[...], wd_ref[:, c], preferred_element_type=f32)
            if first:
                gx_ref[:, c] = gx
                y_ref[:, c] = y
            else:
                gx_ref[:, c] += gx
                y_ref[:, c] += y
    pl.when(step == 0)(lambda: back(True))
    pl.when(step > 0)(lambda: back(False))

def feed_forward(x, g, wg, wu, wd, sub=384):
    r, d = x.shape
    hid = wg.shape[1]
    chunk = hid // 3
    whole = pl.BlockSpec((r, d), lambda i: (0, 0))
    tall = pl.BlockSpec((d, chunk), lambda i: (0, i))
    wide = pl.BlockSpec((r, chunk), lambda i: (0, i))
    return pl.pallas_call(
        lambda *refs: ff_kernel(sub, *refs),
        grid=(hid // chunk,),
        in_specs=[
            whole,
            whole,
            tall,
            tall,
            pl.BlockSpec((chunk, d), lambda i: (i, 0)),
        ],
        out_specs=[whole, whole, wide, wide, wide],
        out_shape=[jax.ShapeDtypeStruct((r, d), f32)] * 2 + [jax.ShapeDtypeStruct((r, hid), bf16)] * 3,
        compiler_params=forward_vmem,
        cost_estimate=cost(24 * r * d * hid, 6 * (d + r) * hid + 12 * r * d, 2 * r * hid),
        name="feed_forward",
    )(x, g, wg, wu, wd)

def grads_kernel(x0, x1, gg0, gg1, gu0, gu1, h0, h1, g0, g1, out_ref, xt, ht):
    step = pl.program_id(0)
    nodes, count, lanes = out_ref.shape
    rows = x0.shape[1] // nodes
    deep = h0.shape[1] // nodes
    r = x0.shape[0]
    @pl.when(step == 0)
    def _():
        xt[:, :r] = x0[...].T
        xt[:, r:] = x1[...].T
    @pl.when(step == 5)
    def _():
        ht[:, :r] = h0[...].T
        ht[:, r:] = h1[...].T
    def put(c, d, at):
        v = jnp.dot(xt[:, :r], c[...], preferred_element_type=f32) + jnp.dot(xt[:, r:], d[...], preferred_element_type=f32)
        out_ref[:, pl.ds(pl.multiple_of(at, 64), rows)] = v.astype(bf16).reshape(nodes, rows, lanes)
    @pl.when(step < 3)
    def _(): put(gg0, gg1, step * rows)
    @pl.when((step >= 3) & (step < 6))
    def _(): put(gu0, gu1, step * rows)
    @pl.when(step == 6)
    def _():
        v = jnp.dot(ht[:, :r], g0[:, :lanes], preferred_element_type=f32) + jnp.dot(ht[:, r:], g1[:, :lanes], preferred_element_type=f32)
        out_ref[:, 6 * rows : 6 * rows + deep] = v.astype(bf16).reshape(nodes, deep, lanes)
        v = jnp.dot(ht[:, :r], g0[:, lanes:], preferred_element_type=f32) + jnp.dot(ht[:, r:], g1[:, lanes:], preferred_element_type=f32)
        v = v.astype(bf16).reshape(nodes, deep, v.shape[1])
        short, rest = deep // 3, v.shape[2]
        for k in range(3):
            out_ref[:, 6 * rows + deep :, k * rest : (k + 1) * rest] = v[:, k * short : (k + 1) * short]

def ff_grads(side, nodes, x0, x1, gg0, gg1, gu0, gu1, h0, h1, g0, g1):
    r, d = x0.shape
    hid = gg0.shape[1]
    lanes = hid // 3
    rows, deep = d // (2 * nodes), hid // (2 * nodes)
    count = 6 * rows + deep + deep // 3
    half = lambda n: pl.BlockSpec((r, n), lambda i, s: (0, s[0]))
    first = pl.BlockSpec((r, lanes), lambda i, s: (0, jnp.minimum(i, 2)))
    second = pl.BlockSpec((r, lanes), lambda i, s: (0, jnp.clip(i - 3, 0, 2)))
    whole = pl.BlockSpec((r, d), lambda i, s: (0, 0))
    return pl.pallas_call(
        lambda s, *refs: grads_kernel(*refs),
        grid_spec=pltpu.PrefetchScalarGridSpec(
            num_scalar_prefetch=1, grid=(7,),
            in_specs=[half(d // 2)] * 2 + [first] * 2 + [second] * 2 + [half(hid // 2)] * 2 + [whole] * 2,
            out_specs=pl.BlockSpec((nodes, count, lanes), lambda i, s: (0, 0, 0)),
            scratch_shapes=[pltpu.VMEM((d // 2, 2 * r), bf16), pltpu.VMEM((hid // 2, 2 * r), bf16)],
        ),
        out_shape=jax.ShapeDtypeStruct((nodes, count, lanes), bf16),
        compiler_params=big_vmem,
        cost_estimate=cost(12 * r * d * hid, 6 * r * hid + 5 * d * hid),
        name="ff_grads",
    )(side.astype(jnp.int32).reshape(1), x0, x1, gg0, gg1, gu0, gu1, h0, h1, g0, g1)


def open_specs(nodes, group, half, lanes, first=0):
    specs = []
    for _ in range(2):
        for b in range(group):
            for at in (0, nodes):
                specs.append(
                    pl.BlockSpec(
                        (None, half, lanes),
                        lambda j, h, order, b=b, at=at: (
                            order[at + (first + j) * group + b],
                            0,
                            0,
                        ),
                    )
                )
    return specs


def open_blocks(group, order_ref, refs, write):
    core = order_ref[order_ref.shape[0] - 1]
    half = refs[0].shape[0]

    def reader(first, second):
        def read(start, stop):
            if stop <= half:
                return first[start:stop].astype(f32)
            if start >= half:
                return second[start - half : stop - half].astype(f32)
            pieces = [first[start:half], second[0 : stop - half]]
            return jnp.concatenate([p.astype(f32) for p in pieces], axis=0)

        return read

    def hand(refs):
        for b in range(group):
            write(b, reader(refs[2 * b], refs[2 * b + 1]))

    own = pl.program_id(1) == core
    pl.when(own)(lambda: hand(refs[: 2 * group]))
    pl.when(jnp.logical_not(own))(lambda: hand(refs[2 * group :]))


def open_ff_kernel(group, order_ref, *refs):
    *pieces, gate_ref, up_ref, down_ref = refs
    lanes = pieces[0].shape[1]
    rows, deep = gate_ref.shape[0] // group, down_ref.shape[0] // group
    rest = down_ref.shape[1] - lanes
    short = deep // 3

    def write(b, read):
        here = slice(b * rows, (b + 1) * rows)
        for k, out in enumerate((gate_ref, up_ref)):
            for c in range(3):
                part = read((3 * k + c) * rows, (3 * k + c + 1) * rows)
                out[here, c * lanes : (c + 1) * lanes] = part
        low, at = b * deep, 6 * rows
        down_ref[low : low + deep, :lanes] = read(at, at + deep)
        for c in range(3):
            part = read(at + deep, at + deep + short)[:, c * rest : (c + 1) * rest]
            down_ref[low + c * short : low + (c + 1) * short, lanes:] = part

    open_blocks(group, order_ref, pieces, write)


def open_ff(pieces, order, at, so_far, width, hidden):
    mine, other = pieces
    half, lanes = mine.shape[1:]
    nodes, group = mine.shape[0] // 2, 2
    steps = nodes // group
    rows, deep = width // (2 * nodes), hidden // (2 * nodes)
    out = lambda tall, wide: pl.BlockSpec(
        (group * tall, wide), lambda j, h, order: (h * steps + at, 0)
    )
    specs = open_specs(nodes, group, half, lanes, at)
    shapes = [(width, hidden), (width, hidden), (hidden, width)]
    kernel = lambda order, *refs: open_ff_kernel(
        group, order, *refs[: 4 * group], *refs[4 * group + len(so_far) :]
    )
    return pl.pallas_call(
        kernel,
        grid_spec=pltpu.PrefetchScalarGridSpec(
            num_scalar_prefetch=1,
            grid=(1, 2),
            in_specs=specs + [pl.BlockSpec(memory_space=pl.ANY)] * len(so_far),
            out_specs=[out(rows, hidden), out(rows, hidden), out(deep, width)],
        ),
        out_shape=[jax.ShapeDtypeStruct(shape, f32) for shape in shapes],
        input_output_aliases={1 + 4 * group + k: k for k in range(len(so_far))},
        compiler_params=small_vmem,
        cost_estimate=cost(0, 24 * width * hidden // steps),
        name="open_ff",
    )(order, *[mine] * (2 * group), *[other] * (2 * group), *so_far)


def pack_conv_kernel(core_ref, in_ref, out_w_ref, tail_ref, away_ref, own_ref):
    blocks, _, width = own_ref.shape
    rows = in_ref.shape[0] // (2 * blocks)
    deep = out_w_ref.shape[0] // blocks
    lanes = width // 2

    def write(ref):
        for k in range(blocks):
            ref[k, 0:rows, 0:lanes] = in_ref[2 * k * rows : (2 * k + 1) * rows]
            ref[k, 0:rows, lanes:] = in_ref[(2 * k + 1) * rows : (2 * k + 2) * rows]
            ref[k, rows : rows + deep] = out_w_ref[k * deep : (k + 1) * deep]
            ref[k, rows + deep :] = tail_ref[...]

    pl.when(pl.program_id(0) == 0)(lambda: write(away_ref))
    pl.when(pl.program_id(0) == 1)(lambda: write(own_ref))


def pack_conv(grad_in, grad_out, tail, part, nodes):
    total, width = grad_in.shape
    half_in, half_out = total // 2, grad_out.shape[0] // 4
    spared = tail.shape[0]
    count = half_in // (2 * nodes) + half_out // nodes + spared
    core = (lax.axis_index("dp") % 2).astype(jnp.int32).reshape(1)
    side = lambda i, c: jnp.where(i == 0, 1 - c[0], c[0])
    out = pl.BlockSpec((nodes, count, width), lambda i, c: (0, 0, 0))
    return pl.pallas_call(
        pack_conv_kernel,
        grid_spec=pltpu.PrefetchScalarGridSpec(
            num_scalar_prefetch=1,
            grid=(2,),
            in_specs=[
                pl.BlockSpec((half_in, width // 2), lambda i, c: (side(i, c), part)),
                pl.BlockSpec((half_out, width), lambda i, c: (2 * part + side(i, c), 0)),
                pl.BlockSpec((spared, width), lambda i, c: (0, 0)),
            ],
            out_specs=[out, out],
        ),
        out_shape=[jax.ShapeDtypeStruct((nodes, count, width), bf16)] * 2,
        compiler_params=small_vmem,
        cost_estimate=cost(0, 2 * (grad_in.size + grad_out.size)),
        name="pack_conv",
    )(core, grad_in, grad_out, tail)


def open_conv_kernel(group, order_ref, *refs):
    *pieces, in_ref, out_w_ref, tail_ref = refs
    rows, lanes = in_ref.shape[0] // (2 * group), in_ref.shape[1]
    deep = out_w_ref.shape[0] // group

    def write(b, read):
        low = 2 * b * rows
        in_ref[low : low + rows] = read(0, rows)[:, :lanes]
        in_ref[low + rows : low + 2 * rows] = read(0, rows)[:, lanes:]
        out_w_ref[b * deep : (b + 1) * deep] = read(rows, rows + deep)
        tail_ref[b] = read(rows + deep, rows + deep + tail_ref.shape[1])

    open_blocks(group, order_ref, pieces, write)


def open_conv(ring, gate, total, deep_total):
    mine = after(ring.total(), gate)
    other = flip(mine, 1)
    _, half, width = mine.shape
    nodes, group = ring.nodes, ring.nodes // 2
    blocks = 2 * nodes
    steps = nodes // group
    rows, deep = total // blocks, deep_total // blocks
    spared = 2 * half - rows // 2 - deep
    at = lambda j, h, order: (h * steps + j, 0)
    return pl.pallas_call(
        lambda *refs: open_conv_kernel(group, *refs),
        grid_spec=pltpu.PrefetchScalarGridSpec(
            num_scalar_prefetch=1,
            grid=(steps, 2),
            in_specs=open_specs(nodes, group, half, width),
            out_specs=[
                pl.BlockSpec((group * rows, width // 2), at),
                pl.BlockSpec((group * deep, width), at),
                pl.BlockSpec(
                    (group, spared, width), lambda j, h, order: (h * steps + j, 0, 0)
                ),
            ],
        ),
        out_shape=[
            jax.ShapeDtypeStruct((total, width // 2), f32),
            jax.ShapeDtypeStruct((deep_total, width), f32),
            jax.ShapeDtypeStruct((blocks, spared, width), f32),
        ],
        compiler_params=small_vmem,
        cost_estimate=cost(0, 8 * (total + deep_total) * width),
        name="open_conv",
    )(ring.order(), *[mine] * (2 * group), *[other] * (2 * group))


def on_device(
    tokens,
    cotangent,
    route,
    seq_lengths,
    norm1_gain,
    in_weight,
    conv_weight,
    out_weight,
    norm2_gain,
    gate_weight,
    up_weight,
    down_weight,
):
    dp_size = lax.axis_size("dp")
    mp_size = lax.axis_size("mp")
    dp_index = lax.axis_index("dp")
    mp_index = lax.axis_index("mp")
    rows = tokens.shape[0]
    narrow = tokens.shape[1]
    width = norm1_gain.shape[0]
    own = rows // mp_size
    start = mp_index * own
    column = mp_index * narrow
    pair_share = rows // dp_size
    slots = pair_share + pair_share // 2
    paired = mp_size == 2

    if paired:
        core = dp_index % 2
        deep = width // 2
        part_in = lax.dynamic_slice_in_dim(in_weight, core * deep, deep, 1)
        part_out = lax.dynamic_slice_in_dim(out_weight, core * deep, deep, 1)
        part = jnp.concatenate([part_in, part_out.reshape(1, deep, deep)], axis=0)
        there = swap_mp(part)
        route = after(route, part)
        taps = jnp.concatenate([conv_weight, swap_mp(conv_weight)], axis=1)
    else:
        full_in = lax.all_gather(in_weight, "mp", axis=2, tiled=True)
        full_out = lax.all_gather(out_weight, "mp", axis=0, tiled=True)
        taps = lax.all_gather(conv_weight, "mp", axis=1, tiled=True)

    sent_rows, digits, slot_of = pack(route, tokens, dp_size, slots)
    sent_seeds = send_rows(after(slot_of, sent_rows), cotangent, dp_size, slots)
    over = dict(split_axis=0, concat_axis=0, tiled=True)
    got_rows = lax.all_to_all(sent_rows, "dp", **over)
    digits = got_rows if slots <= narrow else lax.all_to_all(digits, "dp", **over)
    got_rows, sent_seeds = lax.optimization_barrier((got_rows, sent_seeds))
    got_seeds = lax.all_to_all(sent_seeds, "dp", **over)
    slot_of = slot_of.reshape(rows, 1)
    window = own + 2 * halo
    if paired:
        bases = jnp.stack([start, own - start]).astype(jnp.int32)
        digits = got_rows if slots <= narrow else digits
        pieces, places = place_rows(bases - halo, digits, got_rows, slots, rows, window)
        there, _ = lax.optimization_barrier((there, pieces))
        here = flip(there, 1)
        both = [jnp.where(core == k, there, here) for k in range(2)]
        other_in = jnp.concatenate([v[:3] for v in both], axis=1)
        other_out = jnp.concatenate([v[3] for v in both], axis=1)
        full_in = jnp.concatenate([in_weight, other_in], axis=2)
        full_out = jnp.concatenate([out_weight, other_out], axis=0)
        input_rows = side_by_side(pieces[0], swap_mp(pieces[1]), mp_index)
        pieces, _ = place_rows(bases, digits, got_seeds, slots, rows, own)
        input_rows = after(input_rows, pieces)
        came = swap_mp(pieces[1])
        seeds_here = came
        seeds_own = side_by_side(pieces[0], came, mp_index)
        seeds_other = side_by_side(pieces[1], swap_mp(after(pieces[0], came)), mp_index)
        place_ids = ((places - start) % rows).reshape(-1, 1)
    else:
        bases = (jnp.arange(mp_size) * own).astype(jnp.int32)
        pieces, places = place_rows(bases, digits, got_rows, slots, rows, own)
        full = lax.all_gather(pieces.reshape(rows, narrow), "mp", axis=1, tiled=True)
        full = jnp.pad(full, ((halo, halo), (0, 0)))
        input_rows = lax.dynamic_slice_in_dim(full, start, window, 0)
        pieces, _ = place_rows(bases, digits, got_seeds, slots, rows, own)
        full = lax.all_gather(pieces.reshape(rows, narrow), "mp", axis=1, tiled=True)
        seeds = rolled(full, -start)
        seeds_own, seeds_other = seeds[:own], seeds[own:]
        seeds_here = seeds_own
        place_ids = places.reshape(-1, 1)

    positions = start - halo + jnp.arange(window, dtype=jnp.int32)
    first_mask, second_mask = seq_masks(seq_lengths[0], positions, rows)
    residual = input_rows.astype(f32)
    scale_one = lax.rsqrt(jnp.mean(residual * residual, axis=1) + epsilon)[:, None]
    normed_one = (residual * scale_one * norm1_gain).astype(bf16)
    projected = jnp.einsum("rd,kdc->krc", normed_one, full_in, preferred_element_type=f32)
    projected = after(projected, seeds_here)
    in_gate, out_gate, value_part = (projected[0], projected[1], projected[2])
    mixed = in_gate * value_part
    lag_one = lag_rows(mixed, 1) * first_mask
    lag_two = lag_rows(mixed, 2) * second_mask
    convolved = taps[2] * mixed + taps[1] * lag_one + taps[0] * lag_two
    gated = (out_gate * convolved).astype(bf16)
    middle = (residual + jnp.dot(gated, full_out, preferred_element_type=f32))[halo:]
    scale_two = lax.rsqrt(jnp.mean(middle * middle, axis=1) + epsilon)[:, None]
    normed_own = (middle[:own] * scale_two[:own] * norm2_gain).astype(bf16)

    weights = (gate_weight, up_weight, down_weight)
    if paired:
        normed_other = swap_mp(normed_own)
        first = feed_forward(normed_own, seeds_own, *weights)
        second = feed_forward(normed_other, seeds_other, *weights)
        sent = jnp.concatenate([second[0], first[0][:halo]], axis=0).astype(bf16)
        came = swap_mp(sent)
        saved = (normed_other, first[3], second[3], first[4], second[4])
        saved += (first[2], second[2], seeds_own, seeds_other)
        away = ff_grads(1 - core, dp_size // 2, after(normed_own, sent), *saved)
        kept = ff_grads(core, dp_size // 2, after(normed_own, away), *saved)
        away = flip(away, 1)
        came, _ = lax.optimization_barrier((came, kept))
        grad_normed_two = jnp.concatenate([first[0], second[0][:halo]], axis=0)
        grad_normed_two = grad_normed_two + came.astype(f32)
        down_came = swap_mp(after(second[1].astype(bf16), came))
        ring = Ring((kept, away))
        grad_normed_two = ring.first(grad_normed_two)
        ring.step()
    else:
        normed_two = rolled(lax.all_gather(normed_own, "mp", axis=0, tiled=True), -start)
        gate_val = jnp.dot(normed_two, gate_weight, preferred_element_type=f32)
        up_val = jnp.dot(normed_two, up_weight, preferred_element_type=f32)
        sigmoid_val = jax.nn.sigmoid(gate_val)
        silu_val = gate_val * sigmoid_val
        hidden = (silu_val * up_val).astype(bf16)
        grad_hidden = nt_dot(seeds, down_weight)
        grad_gate_val = (
            grad_hidden * up_val * sigmoid_val * (1.0 + gate_val * (1.0 - sigmoid_val))
        ).astype(bf16)
        grad_up_val = (grad_hidden * silu_val).astype(bf16)
        normed_terms = nt_dot(grad_gate_val, gate_weight) + nt_dot(grad_up_val, up_weight)
        down_terms = jnp.dot(hidden, down_weight, preferred_element_type=f32)
        full = rolled(lax.psum(rolled(normed_terms, start), "mp"), -start)
        grad_normed_two = full[: own + halo]
        down_sum = rolled(lax.psum(rolled(down_terms, start), "mp"), -start)[:own]
        total_gate = sum_dp(tn_dot(normed_two, grad_gate_val).astype(bf16)).astype(f32)
        total_up = sum_dp(tn_dot(normed_two, grad_up_val).astype(bf16)).astype(f32)
        total_down = sum_dp(tn_dot(hidden, seeds).astype(bf16)).astype(f32)
        block_own = (middle[:own] + down_sum).astype(bf16)

    def to_features(mine):
        if not paired:
            full = lax.all_gather(mine, "mp", axis=0, tiled=True)
            return lax.dynamic_slice_in_dim(full, column, narrow, 1)
        low, high = mine[:, :narrow], mine[:, narrow:]
        other = swap_mp(jnp.where(mp_index == 0, high, low))
        return jnp.concatenate([jnp.where(mp_index == 0, low, high), other], axis=0)

    shape = (dp_size, slots, narrow)
    back_block = min(8 * slots, slots * dp_size)
    home_block = min(rows, 512)

    def leave(piece):
        return take_rows(place_ids, piece, back_block, bf16).reshape(shape)

    def to_home(back):
        return lax.all_to_all(back, "dp", **over)

    def arrive(home, dtype):
        return take_rows(slot_of, home.reshape(-1, narrow), home_block, dtype)

    gain_two_term = jnp.sum((grad_normed_two * middle * scale_two)[:own], axis=0)
    dot_two = jnp.sum(norm2_gain * grad_normed_two * middle, axis=1, keepdims=True)
    grad_middle = (
        jnp.concatenate([seeds_own, seeds_other[:halo]], axis=0).astype(f32)
        + scale_two * norm2_gain * grad_normed_two
        - middle * (scale_two * scale_two * scale_two * dot_two / width)
    )
    grad_mix = grad_middle.astype(bf16)
    grad_gated = jnp.einsum("rd,cd->rc", grad_mix, full_out, preferred_element_type=f32)
    if paired:
        grad_gated = ring.first(grad_gated)
        ring.step()
    grad_conv = grad_gated * out_gate[halo:]
    inner = slice(halo, halo + own)
    conv_terms = jnp.stack(
        [
            jnp.sum(grad_conv[:own] * lag_two[inner], axis=0),
            jnp.sum(grad_conv[:own] * lag_one[inner], axis=0),
            jnp.sum(grad_conv[:own] * mixed[inner], axis=0),
        ],
        axis=0,
    )
    grad_mixed = (
        taps[2] * grad_conv
        + taps[1] * lead_rows(grad_conv * first_mask[halo:], 1)
        + taps[0] * lead_rows(grad_conv * second_mask[halo:], 2)
    )[:own]
    grad_parts = jnp.stack(
        [
            grad_mixed * value_part[inner],
            grad_gated[:own] * convolved[inner],
            grad_mixed * in_gate[inner],
        ],
        axis=0,
    ).astype(bf16)
    grad_in = jnp.einsum(
        "rd,krc->kdc", normed_one[inner], grad_parts, preferred_element_type=f32
    ).astype(bf16)
    grad_out = jnp.einsum(
        "rc,rd->cd", gated[inner], grad_mix[:own], preferred_element_type=f32
    ).astype(bf16)
    taps_end = 2 + conv_weight.shape[0]

    parts_late = grad_parts
    if paired:
        ring.step()
        parts_late = ring.first(grad_parts)
    grad_normed_one = jnp.einsum("krc,kdc->rd", parts_late, full_in, preferred_element_type=f32)
    residual_own = residual[inner]
    scale_own = scale_one[inner]
    gain_one_term = jnp.sum(grad_normed_one * residual_own * scale_own, axis=0)
    dot_one = jnp.sum(norm1_gain * grad_normed_one * residual_own, axis=1, keepdims=True)
    input_own = (
        grad_middle[:own]
        + scale_own * norm1_gain * grad_normed_one
        - residual_own * (scale_own * scale_own * scale_own * dot_one / width)
    ).astype(bf16)

    def packed_half(k, *gates):
        lanes = slice(k * narrow, (k + 1) * narrow)
        terms = jnp.pad(conv_terms[:, lanes], ((0, 16 - taps_end), (0, width - narrow)))
        gains = jnp.stack([gain_one_term, gain_two_term], axis=0)
        ends = after(jnp.concatenate([gains, terms], axis=0).astype(bf16), *gates)
        return pack_conv(grad_in.reshape(-1, width), grad_out, ends, k, dp_size // 2)

    if paired:
        away, other = packed_half(1)
        passed = (other.astype(f32) + flip(away, 1).astype(f32)).astype(bf16)
        down_came = after(down_came, grad_parts)
        block_own = (middle[:own] + (first[1] + down_came.astype(f32))).astype(bf16)
        block_piece = to_features(block_own)
        block_back = leave(block_piece)
        out_home = to_home(block_back)
        ring.step(block_piece)
        ring.step(passed)
        away, own_half = packed_half(0, passed)
        passed = swap_mp(passed)
        input_piece = to_features(input_own)
        ring.step(input_piece)
        input_back = leave(after(input_piece, out_home))
        grad_home = to_home(input_back)
        second = Ring((own_half, flip(away, 1), passed))
        ring.step(*second.held.values(), out_home)
        second.step()
        block_out = arrive(out_home, bf16)
        ring.step(*second.held.values(), grad_home)
        second.step(block_out)
        tokens_grad = arrive(grad_home, f32)
        ring.step(*second.held.values())
        second.step()
        ring.step(*second.held.values(), tokens_grad)
        second.step()
        while ring.steps < 2 * ring.nodes - 2:
            ring.step(*second.held.values())
            second.step()
        mine = ring.total()
        pieces = (mine, flip(mine, 1))
        second.step(mine)
        totals = ()
        for at in range(ring.nodes // 2):
            totals = open_ff(pieces, ring.order(), at, totals, width, gate_weight.shape[1])
            second.step(*totals)
        while second.steps < 2 * second.nodes - 2:
            second.step()
        total_gate, total_up, total_down = totals
        total_in, total_out, ends = open_conv(
            second, total_gate, grad_in.size // (2 * narrow), narrow
        )
        tail = ends[0]
    else:
        block_out = arrive(to_home(leave(to_features(block_own))), bf16)
        tokens_grad = arrive(to_home(leave(to_features(input_own))), f32)
        total_in = lax.psum_scatter(
            grad_in.astype(f32), "mp", scatter_dimension=2, tiled=True
        )
        total_in = sum_dp(total_in.astype(bf16).reshape(-1, narrow)).astype(f32)
        total_out = lax.psum_scatter(
            grad_out.astype(f32), "mp", scatter_dimension=0, tiled=True
        )
        total_out = sum_dp(total_out.astype(bf16)).astype(f32)
        gains = lax.psum(jnp.stack([gain_one_term, gain_two_term]), ("dp", "mp"))
        terms = lax.psum_scatter(conv_terms, "mp", scatter_dimension=1, tiled=True)
        terms = jnp.pad(lax.psum(terms, "dp"), ((0, 0), (0, width - narrow)))
        tail = jnp.concatenate([gains, terms], axis=0)
    total_taps = tail[2:taps_end, :narrow]
    return (
        block_out,
        tokens_grad,
        tail[0],
        total_in.reshape(in_weight.shape),
        total_taps,
        total_out,
        tail[1],
        total_gate,
        total_up,
        total_down,
    )


def solution(mesh):
    in_specs = (
        P("dp", "mp"),
        P("dp", "mp"),
        P("dp"),
        P("dp", None),
        P(),
        P(None, None, "mp"),
        P(None, "mp"),
        P("mp", None),
        P(),
        P(None, "mp"),
        P(None, "mp"),
        P("mp", None),
    )
    out_specs = (
        P("dp", "mp"),
        P("dp", "mp"),
        P(),
        P(None, None, "mp"),
        P(None, "mp"),
        P("mp", None),
        P(),
        P(None, "mp"),
        P(None, "mp"),
        P("mp", None),
    )
    return jax.shard_map(
        on_device, mesh=mesh, in_specs=in_specs, out_specs=out_specs, check_vma=False
    )
```

```python
import jax
import jax.numpy as jnp
from jax import lax
from jax.experimental import pallas as pl
from jax.experimental.pallas import tpu as pltpu
from jax.sharding import PartitionSpec as P

epsilon = 1e-05
f32 = jnp.float32
bf16 = jnp.bfloat16
halo = 8
spare = 8
small_vmem = pltpu.CompilerParams(vmem_limit_bytes=26 << 20)
forward_vmem = pltpu.CompilerParams(vmem_limit_bytes=46 << 20)
tight_vmem = pltpu.CompilerParams(vmem_limit_bytes=20 << 20)
big_vmem = pltpu.CompilerParams(vmem_limit_bytes=52 << 20)


def cost(flops, moved, transcendentals=0):
    return pl.CostEstimate(
        flops=int(flops), bytes_accessed=int(moved), transcendentals=int(transcendentals)
    )


def lag_rows(values, shift):
    return jnp.concatenate(
        [jnp.zeros((shift, values.shape[1]), values.dtype), values[:-shift]], axis=0
    )


def lead_rows(values, shift):
    return jnp.concatenate(
        [values[shift:], jnp.zeros((shift, values.shape[1]), values.dtype)], axis=0
    )


def seq_masks(lengths, positions, row_count):
    count = lengths.shape[0]
    before = jnp.arange(count)[:, None] < jnp.arange(count)[None, :]
    starts = jnp.sum(jnp.where(before, lengths[:, None], 0), axis=0, dtype=jnp.int32)
    started = positions[:, None] >= starts[None, :]
    seq_first = jnp.max(jnp.where(started, starts[None, :], 0), axis=1)
    offset = positions - seq_first
    inside = (positions >= 0) & (positions < row_count)
    return (
        ((offset >= 1) & inside).astype(f32)[:, None],
        ((offset >= 2) & inside).astype(f32)[:, None],
    )


def nt_dot(left, right):
    return lax.dot_general(
        left, right, (((1,), (1,)), ((), ())), preferred_element_type=f32
    )


def tn_dot(left, right):
    return lax.dot_general(
        left, right, (((0,), (0,)), ((), ())), preferred_element_type=f32
    )


def rank_kernel(rows, members, slots, route_ref, slot_ref):
    target = route_ref[...] // rows
    width = min(rows, 512)
    owner = lax.broadcasted_iota(jnp.int32, (members, rows), 0)
    one_hot = jnp.where(owner == target, 1.0, 0.0)
    left = one_hot.astype(bf16)
    for start in range(0, rows, width):
        first = lax.broadcasted_iota(jnp.int32, (rows, width), 0)
        second = lax.broadcasted_iota(jnp.int32, (rows, width), 1) + start
        earlier = jnp.where(first < second, 1.0, 0.0).astype(bf16)
        rank = jnp.dot(left, earlier, preferred_element_type=f32)
        piece = one_hot[:, start : start + width]
        mine = jnp.sum(rank * piece, axis=0, keepdims=True).astype(jnp.int32)
        slot_ref[:, start : start + width] = (
            target[:, start : start + width] * slots + mine
        )


def pack_kernel(rows, members, slots, route_ref, x_ref, sx_ref, digit_ref, slot_ref):
    step = pl.program_id(0)
    group = sx_ref.shape[0]

    @pl.when(step == 0)
    def _():
        rank_kernel(rows, members, slots, route_ref, slot_ref)

    place = route_ref[...] % rows
    row = lax.broadcasted_iota(jnp.int32, (8, rows), 0)
    digits = jnp.where(
        row == 0,
        (place // 64).astype(f32),
        jnp.where(row == 1, (place % 64).astype(f32), 1.0),
    ).astype(bf16)
    ids = lax.broadcasted_iota(jnp.int32, (group * slots, rows), 0)
    pick = jnp.where(slot_ref[...] == ids + step * group * slots, 1.0, 0.0).astype(bf16)
    sent = jnp.dot(pick, x_ref[...], preferred_element_type=f32).astype(bf16)
    for k in range(group):
        here = slice(k * slots, (k + 1) * slots)
        sx_ref[k, 0:slots] = sent[here]
        coded = nt_dot(digits, pick[here]).astype(bf16)
        if sx_ref.shape[1] > slots:
            sx_ref[k, slots : slots + spare] = jnp.zeros((spare, sx_ref.shape[2]), bf16)
            sx_ref[k, slots : slots + spare, 0:slots] = coded
        else:
            digit_ref[k] = jnp.zeros(digit_ref.shape[1:], bf16)
            digit_ref[k, :, 0:slots] = coded


def pack(route, tokens, members, slots):
    rows, width = tokens.shape
    group = min(members, 4)
    inside = slots <= width
    span = slots + spare if inside else slots
    whole = lambda j: (0, 0)
    block = lambda *tail: pl.BlockSpec((group, *tail), lambda j: (j, 0, 0))
    lanes = 8 if inside else 256
    return pl.pallas_call(
        lambda *refs: pack_kernel(rows, members, slots, *refs),
        grid=(members // group,),
        in_specs=[pl.BlockSpec((1, rows), whole), pl.BlockSpec((rows, width), whole)],
        out_specs=[block(span, width), block(8, lanes), pl.BlockSpec((1, rows), whole)],
        out_shape=[
            jax.ShapeDtypeStruct((members, span, width), bf16),
            jax.ShapeDtypeStruct((members, 8, lanes), bf16),
            jax.ShapeDtypeStruct((1, rows), jnp.int32),
        ],
        compiler_params=small_vmem,
        cost_estimate=cost(2 * members * slots * rows * width, 5 * rows * width),
        name="pack",
    )(route.reshape(1, rows), tokens)


def send_kernel(slots, slot_ref, x_ref, out_ref):
    group = out_ref.shape[0]
    count = group * slots
    ids = lax.broadcasted_iota(jnp.int32, (count, x_ref.shape[0]), 0)
    pick = jnp.where(slot_ref[...] == ids + pl.program_id(0) * count, 1.0, 0.0)
    sent = jnp.dot(pick.astype(bf16), x_ref[...], preferred_element_type=f32)
    for k in range(group):
        out_ref[k] = sent[k * slots : (k + 1) * slots].astype(bf16)


def send_rows(slot_of, source, members, slots):
    rows, width = source.shape
    group = min(members, 8)
    return pl.pallas_call(
        lambda *refs: send_kernel(slots, *refs),
        grid=(members // group,),
        in_specs=[
            pl.BlockSpec((1, rows), lambda j: (0, 0)),
            pl.BlockSpec((rows, width), lambda j: (0, 0)),
        ],
        out_specs=pl.BlockSpec((group, slots, width), lambda j: (j, 0, 0)),
        out_shape=jax.ShapeDtypeStruct((members, slots, width), bf16),
        compiler_params=small_vmem,
        cost_estimate=cost(2 * members * slots * rows * width, 5 * rows * width),
        name="send_rows",
    )(slot_of, source)


def place_kernel(rows, bases_ref, digit_ref, got_ref, out_ref, place_ref, src, pick):
    members, slots = got_ref.shape[0], got_ref.shape[1]
    count = out_ref.shape[0]
    span = src.shape[0] // members
    base = bases_ref[pl.program_id(0)]
    ids = lax.broadcasted_iota(jnp.int32, (count, span), 0) + base

    @pl.when(pl.program_id(0) == 0)
    def _():
        for j in range(members):
            src[j * span : j * span + slots] = got_ref[j]
            if span > slots:
                src[j * span + slots : (j + 1) * span] = jnp.zeros(
                    (span - slots, src.shape[1]), bf16
                )

    for j in range(members):
        coded = digit_ref[j].astype(f32)[:, 0:span]
        value = coded[0:1] * 64.0 + coded[1:2]
        places = jnp.where(coded[2:3] > 0.5, value, 4.0 * rows).astype(jnp.int32)
        pick[:, j * span : (j + 1) * span] = jnp.where(places == ids, 1.0, 0.0).astype(bf16)
        place_ref[j : j + 1, :] = places[:, 0:slots]
    out_ref[...] = jnp.dot(pick[...], src[...], preferred_element_type=f32).astype(bf16)


def place_rows(bases, digits, got, slots, rows, count):
    members, width = got.shape[0], got.shape[2]
    at = digits.shape[1] // 8 - 1
    span = -(-slots // 128) * 128
    return pl.pallas_call(
        lambda *refs: place_kernel(rows, *refs),
        grid_spec=pltpu.PrefetchScalarGridSpec(
            num_scalar_prefetch=1,
            grid=(bases.shape[0],),
            in_specs=[
                pl.BlockSpec((members, 8, digits.shape[2]), lambda i, b: (0, at, 0)),
                pl.BlockSpec((members, slots, width), lambda i, b: (0, 0, 0)),
            ],
            out_specs=[
                pl.BlockSpec((None, count, width), lambda i, b: (i, 0, 0)),
                pl.BlockSpec((members, slots), lambda i, b: (0, 0)),
            ],
            scratch_shapes=[
                pltpu.VMEM((members * span, width), bf16),
                pltpu.VMEM((count, members * span), bf16),
            ],
        ),
        out_shape=[
            jax.ShapeDtypeStruct((bases.shape[0], count, width), bf16),
            jax.ShapeDtypeStruct((members, slots), jnp.int32),
        ],
        compiler_params=small_vmem,
        cost_estimate=cost(0, (bases.shape[0] * count + members * slots) * width // 8),
        name="place_rows",
    )(bases, digits, got)


def take_kernel(ids_ref, from_ref, out_ref):
    cols = lax.broadcasted_iota(jnp.int32, (out_ref.shape[0], from_ref.shape[0]), 1)
    pick = jnp.where(ids_ref[...] == cols, 1.0, 0.0).astype(bf16)
    out_ref[...] = jnp.dot(pick, from_ref[...], preferred_element_type=f32).astype(
        out_ref.dtype
    )


def take_rows(ids, source, block, dtype):
    count = ids.shape[0]
    total, width = source.shape
    return pl.pallas_call(
        take_kernel,
        grid=(count // block,),
        in_specs=[
            pl.BlockSpec((block, 1), lambda i: (i, 0)),
            pl.BlockSpec((total, width), lambda i: (0, 0)),
        ],
        out_specs=pl.BlockSpec((block, width), lambda i: (i, 0)),
        out_shape=jax.ShapeDtypeStruct((count, width), dtype),
        compiler_params=small_vmem,
        cost_estimate=cost(2 * count * total * width, 2 * (count + total) * width),
        name="take_rows",
    )(ids, source)


def swap_mp(value):
    return lax.ppermute(value, "mp", [(0, 1), (1, 0)])


def side_by_side(mine, other, index):
    return jnp.where(
        index == 0,
        jnp.concatenate([mine, other], axis=1),
        jnp.concatenate([other, mine], axis=1),
    )


def rolled(full, shift):
    return jnp.roll(full, shift, axis=0)


def flip(value, bit):
    size = lax.axis_size("dp")
    return lax.ppermute(value, "dp", [(i, i ^ bit) for i in range(size)])


def dp_bits():
    return [1 << k for k in range(lax.axis_size("dp").bit_length() - 1)]


def halve(value, bit):
    half = value.shape[0] // 2
    side = (lax.axis_index("dp") // bit) % 2
    sent = lax.dynamic_slice_in_dim(value, (1 - side) * half, half, 0)
    kept = lax.dynamic_slice_in_dim(value, side * half, half, 0)
    return (kept.astype(f32) + flip(sent, bit).astype(f32)).astype(bf16)


def double(value, bit):
    side = (lax.axis_index("dp") // bit) % 2
    other = flip(value, bit)
    return jnp.where(
        side == 0,
        jnp.concatenate([value, other], axis=0),
        jnp.concatenate([other, value], axis=0),
    )


def sum_dp(value):
    bits = dp_bits()
    for bit in bits:
        value = halve(value, bit)
    for bit in reversed(bits):
        value = double(value, bit)
    return value


def after(value, *others):
    return lax.optimization_barrier((value, *others))[0]


class Ring:
    def __init__(self, parts):
        self.parts = parts
        self.nodes = nodes = lax.axis_size("dp") // 2
        chip = lax.axis_index("dp") // 2
        self.here = jnp.where(chip % 2 == 0, chip // 2, nodes - 1 - chip // 2)
        top = nodes // 2
        self.chips = [2 * p if p < top else 2 * (nodes - 1 - p) + 1 for p in range(nodes)]
        self.half = parts[0].shape[1] // 2
        self.held = {way: self.terms(self.here, way).astype(bf16) for way in (1, -1)}
        self.pieces = {1: [], -1: []}
        self.steps = 0

    def send(self, value, way):
        pairs = [
            (2 * self.chips[p] + c, 2 * self.chips[(p + way) % self.nodes] + c)
            for p in range(self.nodes)
            for c in range(2)
        ]
        return lax.ppermute(value, "dp", pairs)

    def terms(self, block, way):
        at = (block % self.nodes, 0 if way == 1 else self.half, 0)
        size = (1, self.half, self.parts[0].shape[2])
        pieces = [lax.dynamic_slice(v, at, size) for v in self.parts]
        return sum(piece.astype(f32) for piece in pieces)

    def step(self, *gates):
        count = self.steps
        if count == 2 * self.nodes - 2:
            return
        self.steps += 1
        adding = count < self.nodes - 1
        if gates:
            both = lax.optimization_barrier((self.held[1], self.held[-1], *gates))
            self.held = {1: both[0], -1: both[1]}
        for way in (1, -1):
            if count == self.nodes - 1:
                self.pieces[way].append(self.held[way])
            came = self.send(self.held[way], way)
            if adding:
                own = self.terms(self.here - way * (count + 1) + self.nodes, way)
                came = (came.astype(f32) + own).astype(bf16)
            else:
                self.pieces[way].append(came)
            self.held[way] = came

    def first(self, value):
        return after(value, *self.held.values())

    def total(self):
        return gather_pieces([p[0] for way in (1, -1) for p in self.pieces[way]])

    def order(self):
        block = jnp.arange(self.nodes, dtype=jnp.int32)
        up = (self.here + 1 - block + self.nodes) % self.nodes
        down = (block - self.here + 1 + self.nodes) % self.nodes + self.nodes
        core = lax.axis_index("dp")[None] % 2
        return jnp.concatenate([up, down, core]).astype(jnp.int32)


def gather_kernel(*refs):
    *sources, out_ref = refs
    for k, ref in enumerate(sources):
        out_ref[k] = ref[...]


def gather_pieces(pieces):
    count = len(pieces)
    vmem = pl.BlockSpec(memory_space=pltpu.VMEM)
    return pl.pallas_call(
        gather_kernel,
        in_specs=[vmem] * count,
        out_specs=vmem,
        out_shape=jax.ShapeDtypeStruct((count, *pieces[0].shape), bf16),
        compiler_params=tight_vmem,
        cost_estimate=cost(0, 4 * count * pieces[0].size),
        name="gather_pieces",
    )(*pieces)


def ff_kernel(sub, x_ref, g_ref, wg_ref, wu_ref, wd_ref, gx_ref, y_ref, h_ref, gg_ref, gu_ref):
    step = pl.program_id(0)
    for at in range(0, wg_ref.shape[1], sub):
        c = slice(at, at + sub)
        gate = jnp.dot(x_ref[...], wg_ref[:, c], preferred_element_type=f32)
        up = jnp.dot(x_ref[...], wu_ref[:, c], preferred_element_type=f32)
        grad = nt_dot(g_ref[...], wd_ref[c])
        sig = 1.0 / (1.0 + jnp.exp(-gate))
        silu = gate * sig
        h_ref[:, c] = (silu * up).astype(bf16)
        gg_ref[:, c] = (grad * up * (sig + silu * (1.0 - sig))).astype(bf16)
        gu_ref[:, c] = (grad * silu).astype(bf16)
    def back(first):
        w = 256
        for at in range(0, gx_ref.shape[1], w):
            c = slice(at, at + w)
            gx = nt_dot(gg_ref[...], wg_ref[c, :]) + nt_dot(gu_ref[...], wu_ref[c, :])
            y = jnp.dot(h_ref[...], wd_ref[:, c], preferred_element_type=f32)
            if first:
                gx_ref[:, c] = gx
                y_ref[:, c] = y
            else:
                gx_ref[:, c] += gx
                y_ref[:, c] += y
    pl.when(step == 0)(lambda: back(True))
    pl.when(step > 0)(lambda: back(False))

def feed_forward(x, g, wg, wu, wd, sub=384):
    r, d = x.shape
    hid = wg.shape[1]
    chunk = hid // 3
    whole = pl.BlockSpec((r, d), lambda i: (0, 0))
    tall = pl.BlockSpec((d, chunk), lambda i: (0, i))
    wide = pl.BlockSpec((r, chunk), lambda i: (0, i))
    return pl.pallas_call(
        lambda *refs: ff_kernel(sub, *refs),
        grid=(hid // chunk,),
        in_specs=[
            whole,
            whole,
            tall,
            tall,
            pl.BlockSpec((chunk, d), lambda i: (i, 0)),
        ],
        out_specs=[whole, whole, wide, wide, wide],
        out_shape=[jax.ShapeDtypeStruct((r, d), f32)] * 2 + [jax.ShapeDtypeStruct((r, hid), bf16)] * 3,
        compiler_params=forward_vmem,
        cost_estimate=cost(24 * r * d * hid, 6 * (d + r) * hid + 12 * r * d, 2 * r * hid),
        name="feed_forward",
    )(x, g, wg, wu, wd)

def grads_kernel(x0, x1, gg0, gg1, gu0, gu1, h0, h1, g0, g1, out_ref, xt, ht):
    step = pl.program_id(0)
    nodes, count, lanes = out_ref.shape
    rows = x0.shape[1] // nodes
    deep = h0.shape[1] // nodes
    r = x0.shape[0]
    @pl.when(step == 0)
    def _():
        xt[:, :r] = x0[...].T
        xt[:, r:] = x1[...].T
    @pl.when(step == 5)
    def _():
        ht[:, :r] = h0[...].T
        ht[:, r:] = h1[...].T
    def put(c, d, at):
        v = jnp.dot(xt[:, :r], c[...], preferred_element_type=f32) + jnp.dot(xt[:, r:], d[...], preferred_element_type=f32)
        out_ref[:, pl.ds(pl.multiple_of(at, 64), rows)] = v.astype(bf16).reshape(nodes, rows, lanes)
    @pl.when(step < 3)
    def _(): put(gg0, gg1, step * rows)
    @pl.when((step >= 3) & (step < 6))
    def _(): put(gu0, gu1, step * rows)
    @pl.when(step == 6)
    def _():
        v = jnp.dot(ht[:, :r], g0[:, :lanes], preferred_element_type=f32) + jnp.dot(ht[:, r:], g1[:, :lanes], preferred_element_type=f32)
        out_ref[:, 6 * rows : 6 * rows + deep] = v.astype(bf16).reshape(nodes, deep, lanes)
        v = jnp.dot(ht[:, :r], g0[:, lanes:], preferred_element_type=f32) + jnp.dot(ht[:, r:], g1[:, lanes:], preferred_element_type=f32)
        v = v.astype(bf16).reshape(nodes, deep, v.shape[1])
        short, rest = deep // 3, v.shape[2]
        for k in range(3):
            out_ref[:, 6 * rows + deep :, k * rest : (k + 1) * rest] = v[:, k * short : (k + 1) * short]

def ff_grads(side, nodes, x0, x1, gg0, gg1, gu0, gu1, h0, h1, g0, g1):
    r, d = x0.shape
    hid = gg0.shape[1]
    lanes = hid // 3
    rows, deep = d // (2 * nodes), hid // (2 * nodes)
    count = 6 * rows + deep + deep // 3
    half = lambda n: pl.BlockSpec((r, n), lambda i, s: (0, s[0]))
    first = pl.BlockSpec((r, lanes), lambda i, s: (0, jnp.minimum(i, 2)))
    second = pl.BlockSpec((r, lanes), lambda i, s: (0, jnp.clip(i - 3, 0, 2)))
    whole = pl.BlockSpec((r, d), lambda i, s: (0, 0))
    return pl.pallas_call(
        lambda s, *refs: grads_kernel(*refs),
        grid_spec=pltpu.PrefetchScalarGridSpec(
            num_scalar_prefetch=1, grid=(7,),
            in_specs=[half(d // 2)] * 2 + [first] * 2 + [second] * 2 + [half(hid // 2)] * 2 + [whole] * 2,
            out_specs=pl.BlockSpec((nodes, count, lanes), lambda i, s: (0, 0, 0)),
            scratch_shapes=[pltpu.VMEM((d // 2, 2 * r), bf16), pltpu.VMEM((hid // 2, 2 * r), bf16)],
        ),
        out_shape=jax.ShapeDtypeStruct((nodes, count, lanes), bf16),
        compiler_params=big_vmem,
        cost_estimate=cost(12 * r * d * hid, 6 * r * hid + 5 * d * hid),
        name="ff_grads",
    )(side.astype(jnp.int32).reshape(1), x0, x1, gg0, gg1, gu0, gu1, h0, h1, g0, g1)


def open_specs(nodes, group, half, lanes, first=0):
    specs = []
    for _ in range(2):
        for b in range(group):
            for at in (0, nodes):
                specs.append(
                    pl.BlockSpec(
                        (None, half, lanes),
                        lambda j, h, order, b=b, at=at: (
                            order[at + (first + j) * group + b],
                            0,
                            0,
                        ),
                    )
                )
    return specs


def open_blocks(group, order_ref, refs, write):
    core = order_ref[order_ref.shape[0] - 1]
    half = refs[0].shape[0]

    def reader(first, second):
        def read(start, stop):
            if stop <= half:
                return first[start:stop].astype(f32)
            if start >= half:
                return second[start - half : stop - half].astype(f32)
            pieces = [first[start:half], second[0 : stop - half]]
            return jnp.concatenate([p.astype(f32) for p in pieces], axis=0)

        return read

    def hand(refs):
        for b in range(group):
            write(b, reader(refs[2 * b], refs[2 * b + 1]))

    own = pl.program_id(1) == core
    pl.when(own)(lambda: hand(refs[: 2 * group]))
    pl.when(jnp.logical_not(own))(lambda: hand(refs[2 * group :]))


def open_ff_kernel(group, order_ref, *refs):
    *pieces, gate_ref, up_ref, down_ref = refs
    lanes = pieces[0].shape[1]
    rows, deep = gate_ref.shape[0] // group, down_ref.shape[0] // group
    rest = down_ref.shape[1] - lanes
    short = deep // 3

    def write(b, read):
        here = slice(b * rows, (b + 1) * rows)
        for k, out in enumerate((gate_ref, up_ref)):
            for c in range(3):
                part = read((3 * k + c) * rows, (3 * k + c + 1) * rows)
                out[here, c * lanes : (c + 1) * lanes] = part
        low, at = b * deep, 6 * rows
        down_ref[low : low + deep, :lanes] = read(at, at + deep)
        for c in range(3):
            part = read(at + deep, at + deep + short)[:, c * rest : (c + 1) * rest]
            down_ref[low + c * short : low + (c + 1) * short, lanes:] = part

    open_blocks(group, order_ref, pieces, write)


def open_ff(pieces, order, at, so_far, width, hidden):
    mine, other = pieces
    half, lanes = mine.shape[1:]
    nodes, group = mine.shape[0] // 2, 2
    steps = nodes // group
    rows, deep = width // (2 * nodes), hidden // (2 * nodes)
    out = lambda tall, wide: pl.BlockSpec(
        (group * tall, wide), lambda j, h, order: (h * steps + at, 0)
    )
    specs = open_specs(nodes, group, half, lanes, at)
    shapes = [(width, hidden), (width, hidden), (hidden, width)]
    kernel = lambda order, *refs: open_ff_kernel(
        group, order, *refs[: 4 * group], *refs[4 * group + len(so_far) :]
    )
    return pl.pallas_call(
        kernel,
        grid_spec=pltpu.PrefetchScalarGridSpec(
            num_scalar_prefetch=1,
            grid=(1, 2),
            in_specs=specs + [pl.BlockSpec(memory_space=pl.ANY)] * len(so_far),
            out_specs=[out(rows, hidden), out(rows, hidden), out(deep, width)],
        ),
        out_shape=[jax.ShapeDtypeStruct(shape, f32) for shape in shapes],
        input_output_aliases={1 + 4 * group + k: k for k in range(len(so_far))},
        compiler_params=tight_vmem,
        cost_estimate=cost(0, 24 * width * hidden // steps),
        name="open_ff",
    )(order, *[mine] * (2 * group), *[other] * (2 * group), *so_far)


def pack_conv_kernel(core_ref, in_ref, out_w_ref, tail_ref, away_ref, own_ref):
    blocks, _, width = own_ref.shape
    rows = in_ref.shape[0] // (2 * blocks)
    deep = out_w_ref.shape[0] // blocks
    lanes = width // 2

    def write(ref):
        for k in range(blocks):
            ref[k, 0:rows, 0:lanes] = in_ref[2 * k * rows : (2 * k + 1) * rows]
            ref[k, 0:rows, lanes:] = in_ref[(2 * k + 1) * rows : (2 * k + 2) * rows]
            ref[k, rows : rows + deep] = out_w_ref[k * deep : (k + 1) * deep]
            ref[k, rows + deep :] = tail_ref[...]

    pl.when(pl.program_id(0) == 0)(lambda: write(away_ref))
    pl.when(pl.program_id(0) == 1)(lambda: write(own_ref))


def pack_conv(grad_in, grad_out, tail, part, nodes):
    total, width = grad_in.shape
    half_in, half_out = total // 2, grad_out.shape[0] // 4
    spared = tail.shape[0]
    count = half_in // (2 * nodes) + half_out // nodes + spared
    core = (lax.axis_index("dp") % 2).astype(jnp.int32).reshape(1)
    side = lambda i, c: jnp.where(i == 0, 1 - c[0], c[0])
    out = pl.BlockSpec((nodes, count, width), lambda i, c: (0, 0, 0))
    return pl.pallas_call(
        pack_conv_kernel,
        grid_spec=pltpu.PrefetchScalarGridSpec(
            num_scalar_prefetch=1,
            grid=(2,),
            in_specs=[
                pl.BlockSpec((half_in, width // 2), lambda i, c: (side(i, c), part)),
                pl.BlockSpec((half_out, width), lambda i, c: (2 * part + side(i, c), 0)),
                pl.BlockSpec((spared, width), lambda i, c: (0, 0)),
            ],
            out_specs=[out, out],
        ),
        out_shape=[jax.ShapeDtypeStruct((nodes, count, width), bf16)] * 2,
        compiler_params=tight_vmem,
        cost_estimate=cost(0, 2 * (grad_in.size + grad_out.size)),
        name="pack_conv",
    )(core, grad_in, grad_out, tail)


def open_conv_kernel(group, order_ref, *refs):
    *pieces, in_ref, out_w_ref, tail_ref = refs
    rows, lanes = in_ref.shape[0] // (2 * group), in_ref.shape[1]
    deep = out_w_ref.shape[0] // group

    def write(b, read):
        low = 2 * b * rows
        in_ref[low : low + rows] = read(0, rows)[:, :lanes]
        in_ref[low + rows : low + 2 * rows] = read(0, rows)[:, lanes:]
        out_w_ref[b * deep : (b + 1) * deep] = read(rows, rows + deep)
        tail_ref[b] = read(rows + deep, rows + deep + tail_ref.shape[1])

    open_blocks(group, order_ref, pieces, write)


def open_conv(ring, gate, total, deep_total):
    mine = after(ring.total(), gate)
    other = flip(mine, 1)
    _, half, width = mine.shape
    nodes, group = ring.nodes, ring.nodes // 2
    blocks = 2 * nodes
    steps = nodes // group
    rows, deep = total // blocks, deep_total // blocks
    spared = 2 * half - rows // 2 - deep
    at = lambda j, h, order: (h * steps + j, 0)
    return pl.pallas_call(
        lambda *refs: open_conv_kernel(group, *refs),
        grid_spec=pltpu.PrefetchScalarGridSpec(
            num_scalar_prefetch=1,
            grid=(steps, 2),
            in_specs=open_specs(nodes, group, half, width),
            out_specs=[
                pl.BlockSpec((group * rows, width // 2), at),
                pl.BlockSpec((group * deep, width), at),
                pl.BlockSpec(
                    (group, spared, width), lambda j, h, order: (h * steps + j, 0, 0)
                ),
            ],
        ),
        out_shape=[
            jax.ShapeDtypeStruct((total, width // 2), f32),
            jax.ShapeDtypeStruct((deep_total, width), f32),
            jax.ShapeDtypeStruct((blocks, spared, width), f32),
        ],
        compiler_params=tight_vmem,
        cost_estimate=cost(0, 8 * (total + deep_total) * width),
        name="open_conv",
    )(ring.order(), *[mine] * (2 * group), *[other] * (2 * group))


def on_device(
    tokens,
    cotangent,
    route,
    seq_lengths,
    norm1_gain,
    in_weight,
    conv_weight,
    out_weight,
    norm2_gain,
    gate_weight,
    up_weight,
    down_weight,
):
    dp_size = lax.axis_size("dp")
    mp_size = lax.axis_size("mp")
    dp_index = lax.axis_index("dp")
    mp_index = lax.axis_index("mp")
    rows = tokens.shape[0]
    narrow = tokens.shape[1]
    width = norm1_gain.shape[0]
    own = rows // mp_size
    start = mp_index * own
    column = mp_index * narrow
    pair_share = rows // dp_size
    slots = pair_share + pair_share // 2
    paired = mp_size == 2

    if paired:
        core = dp_index % 2
        deep = width // 2
        part_in = lax.dynamic_slice_in_dim(in_weight, core * deep, deep, 1)
        part_out = lax.dynamic_slice_in_dim(out_weight, core * deep, deep, 1)
        part = jnp.concatenate([part_in, part_out.reshape(1, deep, deep)], axis=0)
        there = swap_mp(part)
        route = after(route, part)
        taps = jnp.concatenate([conv_weight, swap_mp(conv_weight)], axis=1)
    else:
        full_in = lax.all_gather(in_weight, "mp", axis=2, tiled=True)
        full_out = lax.all_gather(out_weight, "mp", axis=0, tiled=True)
        taps = lax.all_gather(conv_weight, "mp", axis=1, tiled=True)

    sent_rows, digits, slot_of = pack(route, tokens, dp_size, slots)
    sent_seeds = send_rows(after(slot_of, sent_rows), cotangent, dp_size, slots)
    over = dict(split_axis=0, concat_axis=0, tiled=True)
    got_rows = lax.all_to_all(sent_rows, "dp", **over)
    digits = got_rows if slots <= narrow else lax.all_to_all(digits, "dp", **over)
    got_rows, sent_seeds = lax.optimization_barrier((got_rows, sent_seeds))
    got_seeds = lax.all_to_all(sent_seeds, "dp", **over)
    slot_of = slot_of.reshape(rows, 1)
    window = own + 2 * halo
    if paired:
        bases = jnp.stack([start, own - start]).astype(jnp.int32)
        digits = got_rows if slots <= narrow else digits
        pieces, places = place_rows(bases - halo, digits, got_rows, slots, rows, window)
        there, _ = lax.optimization_barrier((there, pieces))
        here = flip(there, 1)
        both = [jnp.where(core == k, there, here) for k in range(2)]
        other_in = jnp.concatenate([v[:3] for v in both], axis=1)
        other_out = jnp.concatenate([v[3] for v in both], axis=1)
        full_in = jnp.concatenate([in_weight, other_in], axis=2)
        full_out = jnp.concatenate([out_weight, other_out], axis=0)
        input_rows = side_by_side(pieces[0], swap_mp(pieces[1]), mp_index)
        pieces, _ = place_rows(bases, digits, got_seeds, slots, rows, own)
        input_rows = after(input_rows, pieces)
        came = swap_mp(pieces[1])
        seeds_here = came
        seeds_own = side_by_side(pieces[0], came, mp_index)
        seeds_other = side_by_side(pieces[1], swap_mp(after(pieces[0], came)), mp_index)
        place_ids = ((places - start) % rows).reshape(-1, 1)
    else:
        bases = (jnp.arange(mp_size) * own).astype(jnp.int32)
        pieces, places = place_rows(bases, digits, got_rows, slots, rows, own)
        full = lax.all_gather(pieces.reshape(rows, narrow), "mp", axis=1, tiled=True)
        full = jnp.pad(full, ((halo, halo), (0, 0)))
        input_rows = lax.dynamic_slice_in_dim(full, start, window, 0)
        pieces, _ = place_rows(bases, digits, got_seeds, slots, rows, own)
        full = lax.all_gather(pieces.reshape(rows, narrow), "mp", axis=1, tiled=True)
        seeds = rolled(full, -start)
        seeds_own, seeds_other = seeds[:own], seeds[own:]
        seeds_here = seeds_own
        place_ids = places.reshape(-1, 1)

    positions = start - halo + jnp.arange(window, dtype=jnp.int32)
    first_mask, second_mask = seq_masks(seq_lengths[0], positions, rows)
    residual = input_rows.astype(f32)
    scale_one = lax.rsqrt(jnp.mean(residual * residual, axis=1) + epsilon)[:, None]
    normed_one = (residual * scale_one * norm1_gain).astype(bf16)
    projected = jnp.einsum("rd,kdc->krc", normed_one, full_in, preferred_element_type=f32)
    projected = after(projected, seeds_here)
    in_gate, out_gate, value_part = (projected[0], projected[1], projected[2])
    mixed = in_gate * value_part
    lag_one = lag_rows(mixed, 1) * first_mask
    lag_two = lag_rows(mixed, 2) * second_mask
    convolved = taps[2] * mixed + taps[1] * lag_one + taps[0] * lag_two
    gated = (out_gate * convolved).astype(bf16)
    middle = (residual + jnp.dot(gated, full_out, preferred_element_type=f32))[halo:]
    scale_two = lax.rsqrt(jnp.mean(middle * middle, axis=1) + epsilon)[:, None]
    normed_own = (middle[:own] * scale_two[:own] * norm2_gain).astype(bf16)

    weights = (gate_weight, up_weight, down_weight)
    if paired:
        normed_other = swap_mp(normed_own)
        first = feed_forward(normed_own, seeds_own, *weights)
        second = feed_forward(normed_other, seeds_other, *weights)
        sent = jnp.concatenate([second[0], first[0][:halo]], axis=0).astype(bf16)
        came = swap_mp(sent)
        saved = (normed_other, first[3], second[3], first[4], second[4])
        saved += (first[2], second[2], seeds_own, seeds_other)
        away = ff_grads(1 - core, dp_size // 2, after(normed_own, sent), *saved)
        kept = ff_grads(core, dp_size // 2, after(normed_own, away), *saved)
        away = flip(away, 1)
        came, _ = lax.optimization_barrier((came, kept))
        grad_normed_two = jnp.concatenate([first[0], second[0][:halo]], axis=0)
        grad_normed_two = grad_normed_two + came.astype(f32)
        down_came = swap_mp(after(second[1].astype(bf16), came))
        ring = Ring((kept, away))
        grad_normed_two = ring.first(grad_normed_two)
        ring.step()
    else:
        normed_two = rolled(lax.all_gather(normed_own, "mp", axis=0, tiled=True), -start)
        gate_val = jnp.dot(normed_two, gate_weight, preferred_element_type=f32)
        up_val = jnp.dot(normed_two, up_weight, preferred_element_type=f32)
        sigmoid_val = jax.nn.sigmoid(gate_val)
        silu_val = gate_val * sigmoid_val
        hidden = (silu_val * up_val).astype(bf16)
        grad_hidden = nt_dot(seeds, down_weight)
        grad_gate_val = (
            grad_hidden * up_val * sigmoid_val * (1.0 + gate_val * (1.0 - sigmoid_val))
        ).astype(bf16)
        grad_up_val = (grad_hidden * silu_val).astype(bf16)
        normed_terms = nt_dot(grad_gate_val, gate_weight) + nt_dot(grad_up_val, up_weight)
        down_terms = jnp.dot(hidden, down_weight, preferred_element_type=f32)
        full = rolled(lax.psum(rolled(normed_terms, start), "mp"), -start)
        grad_normed_two = full[: own + halo]
        down_sum = rolled(lax.psum(rolled(down_terms, start), "mp"), -start)[:own]
        total_gate = sum_dp(tn_dot(normed_two, grad_gate_val).astype(bf16)).astype(f32)
        total_up = sum_dp(tn_dot(normed_two, grad_up_val).astype(bf16)).astype(f32)
        total_down = sum_dp(tn_dot(hidden, seeds).astype(bf16)).astype(f32)
        block_own = (middle[:own] + down_sum).astype(bf16)

    def to_features(mine):
        if not paired:
            full = lax.all_gather(mine, "mp", axis=0, tiled=True)
            return lax.dynamic_slice_in_dim(full, column, narrow, 1)
        low, high = mine[:, :narrow], mine[:, narrow:]
        other = swap_mp(jnp.where(mp_index == 0, high, low))
        return jnp.concatenate([jnp.where(mp_index == 0, low, high), other], axis=0)

    shape = (dp_size, slots, narrow)
    back_block = min(8 * slots, slots * dp_size)
    home_block = min(rows, 512)

    def leave(piece):
        return take_rows(place_ids, piece, back_block, bf16).reshape(shape)

    def to_home(back):
        return lax.all_to_all(back, "dp", **over)

    def arrive(home, dtype):
        return take_rows(slot_of, home.reshape(-1, narrow), home_block, dtype)

    gain_two_term = jnp.sum((grad_normed_two * middle * scale_two)[:own], axis=0)
    dot_two = jnp.sum(norm2_gain * grad_normed_two * middle, axis=1, keepdims=True)
    grad_middle = (
        jnp.concatenate([seeds_own, seeds_other[:halo]], axis=0).astype(f32)
        + scale_two * norm2_gain * grad_normed_two
        - middle * (scale_two * scale_two * scale_two * dot_two / width)
    )
    grad_mix = grad_middle.astype(bf16)
    grad_gated = jnp.einsum("rd,cd->rc", grad_mix, full_out, preferred_element_type=f32)
    if paired:
        grad_gated = ring.first(grad_gated)
        ring.step()
    grad_conv = grad_gated * out_gate[halo:]
    inner = slice(halo, halo + own)
    conv_terms = jnp.stack(
        [
            jnp.sum(grad_conv[:own] * lag_two[inner], axis=0),
            jnp.sum(grad_conv[:own] * lag_one[inner], axis=0),
            jnp.sum(grad_conv[:own] * mixed[inner], axis=0),
        ],
        axis=0,
    )
    grad_mixed = (
        taps[2] * grad_conv
        + taps[1] * lead_rows(grad_conv * first_mask[halo:], 1)
        + taps[0] * lead_rows(grad_conv * second_mask[halo:], 2)
    )[:own]
    grad_parts = jnp.stack(
        [
            grad_mixed * value_part[inner],
            grad_gated[:own] * convolved[inner],
            grad_mixed * in_gate[inner],
        ],
        axis=0,
    ).astype(bf16)
    grad_in = jnp.einsum(
        "rd,krc->kdc", normed_one[inner], grad_parts, preferred_element_type=f32
    ).astype(bf16)
    grad_out = jnp.einsum(
        "rc,rd->cd", gated[inner], grad_mix[:own], preferred_element_type=f32
    ).astype(bf16)
    taps_end = 2 + conv_weight.shape[0]

    parts_late = grad_parts
    if paired:
        ring.step()
        parts_late = ring.first(grad_parts)
    grad_normed_one = jnp.einsum("krc,kdc->rd", parts_late, full_in, preferred_element_type=f32)
    residual_own = residual[inner]
    scale_own = scale_one[inner]
    gain_one_term = jnp.sum(grad_normed_one * residual_own * scale_own, axis=0)
    dot_one = jnp.sum(norm1_gain * grad_normed_one * residual_own, axis=1, keepdims=True)
    input_own = (
        grad_middle[:own]
        + scale_own * norm1_gain * grad_normed_one
        - residual_own * (scale_own * scale_own * scale_own * dot_one / width)
    ).astype(bf16)

    def packed_half(k, *gates):
        lanes = slice(k * narrow, (k + 1) * narrow)
        terms = jnp.pad(conv_terms[:, lanes], ((0, 16 - taps_end), (0, width - narrow)))
        gains = jnp.stack([gain_one_term, gain_two_term], axis=0)
        ends = after(jnp.concatenate([gains, terms], axis=0).astype(bf16), *gates)
        return pack_conv(grad_in.reshape(-1, width), grad_out, ends, k, dp_size // 2)

    if paired:
        away, other = packed_half(1)
        passed = (other.astype(f32) + flip(away, 1).astype(f32)).astype(bf16)
        down_came = after(down_came, grad_parts)
        block_own = (middle[:own] + (first[1] + down_came.astype(f32))).astype(bf16)
        block_piece = to_features(block_own)
        block_back = leave(block_piece)
        out_home = to_home(block_back)
        ring.step(block_piece)
        ring.step(passed)
        away, own_half = packed_half(0, passed)
        passed = swap_mp(passed)
        input_piece = to_features(input_own)
        ring.step(input_piece)
        input_back = leave(after(input_piece, out_home))
        grad_home = to_home(input_back)
        second = Ring((own_half, flip(away, 1), passed))
        ring.step(*second.held.values(), out_home)
        second.step()
        block_out = arrive(out_home, bf16)
        ring.step(*second.held.values(), grad_home)
        second.step(block_out)
        tokens_grad = arrive(grad_home, f32)
        ring.step(*second.held.values())
        second.step()
        ring.step(*second.held.values(), tokens_grad)
        second.step()
        while ring.steps < 2 * ring.nodes - 2:
            ring.step(*second.held.values())
            second.step()
        mine = ring.total()
        pieces = (mine, flip(mine, 1))
        second.step(mine)
        totals = ()
        for at in range(ring.nodes // 2):
            totals = open_ff(pieces, ring.order(), at, totals, width, gate_weight.shape[1])
            second.step(*totals)
        while second.steps < 2 * second.nodes - 2:
            second.step()
        total_gate, total_up, total_down = totals
        total_in, total_out, ends = open_conv(
            second, total_gate, grad_in.size // (2 * narrow), narrow
        )
        tail = ends[0]
    else:
        block_out = arrive(to_home(leave(to_features(block_own))), bf16)
        tokens_grad = arrive(to_home(leave(to_features(input_own))), f32)
        total_in = lax.psum_scatter(
            grad_in.astype(f32), "mp", scatter_dimension=2, tiled=True
        )
        total_in = sum_dp(total_in.astype(bf16).reshape(-1, narrow)).astype(f32)
        total_out = lax.psum_scatter(
            grad_out.astype(f32), "mp", scatter_dimension=0, tiled=True
        )
        total_out = sum_dp(total_out.astype(bf16)).astype(f32)
        gains = lax.psum(jnp.stack([gain_one_term, gain_two_term]), ("dp", "mp"))
        terms = lax.psum_scatter(conv_terms, "mp", scatter_dimension=1, tiled=True)
        terms = jnp.pad(lax.psum(terms, "dp"), ((0, 0), (0, width - narrow)))
        tail = jnp.concatenate([gains, terms], axis=0)
    total_taps = tail[2:taps_end, :narrow]
    return (
        block_out,
        tokens_grad,
        tail[0],
        total_in.reshape(in_weight.shape),
        total_taps,
        total_out,
        tail[1],
        total_gate,
        total_up,
        total_down,
    )


def solution(mesh):
    in_specs = (
        P("dp", "mp"),
        P("dp", "mp"),
        P("dp"),
        P("dp", None),
        P(),
        P(None, None, "mp"),
        P(None, "mp"),
        P("mp", None),
        P(),
        P(None, "mp"),
        P(None, "mp"),
        P("mp", None),
    )
    out_specs = (
        P("dp", "mp"),
        P("dp", "mp"),
        P(),
        P(None, None, "mp"),
        P(None, "mp"),
        P("mp", None),
        P(),
        P(None, "mp"),
        P(None, "mp"),
        P("mp", None),
    )
    return jax.shard_map(
        on_device, mesh=mesh, in_specs=in_specs, out_specs=out_specs, check_vma=False
    )
```

```python
import jax
import jax.numpy as jnp
from jax import lax
from jax.experimental import pallas as pl
from jax.experimental.pallas import tpu as pltpu
from jax.sharding import PartitionSpec as P

epsilon = 1e-05
f32 = jnp.float32
bf16 = jnp.bfloat16
halo = 8
spare = 8
small_vmem = pltpu.CompilerParams(vmem_limit_bytes=26 << 20)
forward_vmem = pltpu.CompilerParams(vmem_limit_bytes=43 << 20)
tight_vmem = pltpu.CompilerParams(vmem_limit_bytes=20 << 20)
big_vmem = pltpu.CompilerParams(vmem_limit_bytes=52 << 20)


def cost(flops, moved, transcendentals=0):
    return pl.CostEstimate(
        flops=int(flops), bytes_accessed=int(moved), transcendentals=int(transcendentals)
    )


def lag_rows(values, shift):
    return jnp.concatenate(
        [jnp.zeros((shift, values.shape[1]), values.dtype), values[:-shift]], axis=0
    )


def lead_rows(values, shift):
    return jnp.concatenate(
        [values[shift:], jnp.zeros((shift, values.shape[1]), values.dtype)], axis=0
    )


def seq_masks(lengths, positions, row_count):
    count = lengths.shape[0]
    before = jnp.arange(count)[:, None] < jnp.arange(count)[None, :]
    starts = jnp.sum(jnp.where(before, lengths[:, None], 0), axis=0, dtype=jnp.int32)
    started = positions[:, None] >= starts[None, :]
    seq_first = jnp.max(jnp.where(started, starts[None, :], 0), axis=1)
    offset = positions - seq_first
    inside = (positions >= 0) & (positions < row_count)
    return (
        ((offset >= 1) & inside).astype(f32)[:, None],
        ((offset >= 2) & inside).astype(f32)[:, None],
    )


def nt_dot(left, right):
    return lax.dot_general(
        left, right, (((1,), (1,)), ((), ())), preferred_element_type=f32
    )


def tn_dot(left, right):
    return lax.dot_general(
        left, right, (((0,), (0,)), ((), ())), preferred_element_type=f32
    )


def rank_kernel(rows, members, slots, route_ref, slot_ref):
    target = route_ref[...] // rows
    width = min(rows, 512)
    owner = lax.broadcasted_iota(jnp.int32, (members, rows), 0)
    one_hot = jnp.where(owner == target, 1.0, 0.0)
    left = one_hot.astype(bf16)
    for start in range(0, rows, width):
        first = lax.broadcasted_iota(jnp.int32, (rows, width), 0)
        second = lax.broadcasted_iota(jnp.int32, (rows, width), 1) + start
        earlier = jnp.where(first < second, 1.0, 0.0).astype(bf16)
        rank = jnp.dot(left, earlier, preferred_element_type=f32)
        piece = one_hot[:, start : start + width]
        mine = jnp.sum(rank * piece, axis=0, keepdims=True).astype(jnp.int32)
        slot_ref[:, start : start + width] = (
            target[:, start : start + width] * slots + mine
        )


def pack_kernel(rows, members, slots, route_ref, x_ref, sx_ref, digit_ref, slot_ref):
    step = pl.program_id(0)
    group = sx_ref.shape[0]

    @pl.when(step == 0)
    def _():
        rank_kernel(rows, members, slots, route_ref, slot_ref)

    place = route_ref[...] % rows
    row = lax.broadcasted_iota(jnp.int32, (8, rows), 0)
    digits = jnp.where(
        row == 0,
        (place // 64).astype(f32),
        jnp.where(row == 1, (place % 64).astype(f32), 1.0),
    ).astype(bf16)
    ids = lax.broadcasted_iota(jnp.int32, (group * slots, rows), 0)
    pick = jnp.where(slot_ref[...] == ids + step * group * slots, 1.0, 0.0).astype(bf16)
    sent = jnp.dot(pick, x_ref[...], preferred_element_type=f32).astype(bf16)
    for k in range(group):
        here = slice(k * slots, (k + 1) * slots)
        sx_ref[k, 0:slots] = sent[here]
        coded = nt_dot(digits, pick[here]).astype(bf16)
        if sx_ref.shape[1] > slots:
            sx_ref[k, slots : slots + spare] = jnp.zeros((spare, sx_ref.shape[2]), bf16)
            sx_ref[k, slots : slots + spare, 0:slots] = coded
        else:
            digit_ref[k] = jnp.zeros(digit_ref.shape[1:], bf16)
            digit_ref[k, :, 0:slots] = coded


def pack(route, tokens, members, slots):
    rows, width = tokens.shape
    group = min(members, 4)
    inside = slots <= width
    span = slots + spare if inside else slots
    whole = lambda j: (0, 0)
    block = lambda *tail: pl.BlockSpec((group, *tail), lambda j: (j, 0, 0))
    lanes = 8 if inside else 256
    return pl.pallas_call(
        lambda *refs: pack_kernel(rows, members, slots, *refs),
        grid=(members // group,),
        in_specs=[pl.BlockSpec((1, rows), whole), pl.BlockSpec((rows, width), whole)],
        out_specs=[block(span, width), block(8, lanes), pl.BlockSpec((1, rows), whole)],
        out_shape=[
            jax.ShapeDtypeStruct((members, span, width), bf16),
            jax.ShapeDtypeStruct((members, 8, lanes), bf16),
            jax.ShapeDtypeStruct((1, rows), jnp.int32),
        ],
        compiler_params=small_vmem,
        cost_estimate=cost(2 * members * slots * rows * width, 5 * rows * width),
        name="pack",
    )(route.reshape(1, rows), tokens)


def send_kernel(slots, slot_ref, x_ref, out_ref):
    group = out_ref.shape[0]
    count = group * slots
    ids = lax.broadcasted_iota(jnp.int32, (count, x_ref.shape[0]), 0)
    pick = jnp.where(slot_ref[...] == ids + pl.program_id(0) * count, 1.0, 0.0)
    sent = jnp.dot(pick.astype(bf16), x_ref[...], preferred_element_type=f32)
    for k in range(group):
        out_ref[k] = sent[k * slots : (k + 1) * slots].astype(bf16)


def send_rows(slot_of, source, members, slots):
    rows, width = source.shape
    group = min(members, 8)
    return pl.pallas_call(
        lambda *refs: send_kernel(slots, *refs),
        grid=(members // group,),
        in_specs=[
            pl.BlockSpec((1, rows), lambda j: (0, 0)),
            pl.BlockSpec((rows, width), lambda j: (0, 0)),
        ],
        out_specs=pl.BlockSpec((group, slots, width), lambda j: (j, 0, 0)),
        out_shape=jax.ShapeDtypeStruct((members, slots, width), bf16),
        compiler_params=small_vmem,
        cost_estimate=cost(2 * members * slots * rows * width, 5 * rows * width),
        name="send_rows",
    )(slot_of, source)


def place_kernel(rows, bases_ref, digit_ref, got_ref, out_ref, place_ref, src, pick):
    members, slots = got_ref.shape[0], got_ref.shape[1]
    count = out_ref.shape[0]
    span = src.shape[0] // members
    base = bases_ref[pl.program_id(0)]
    ids = lax.broadcasted_iota(jnp.int32, (count, span), 0) + base

    @pl.when(pl.program_id(0) == 0)
    def _():
        for j in range(members):
            src[j * span : j * span + slots] = got_ref[j]
            if span > slots:
                src[j * span + slots : (j + 1) * span] = jnp.zeros(
                    (span - slots, src.shape[1]), bf16
                )

    for j in range(members):
        coded = digit_ref[j].astype(f32)[:, 0:span]
        value = coded[0:1] * 64.0 + coded[1:2]
        places = jnp.where(coded[2:3] > 0.5, value, 4.0 * rows).astype(jnp.int32)
        pick[:, j * span : (j + 1) * span] = jnp.where(places == ids, 1.0, 0.0).astype(bf16)
        place_ref[j : j + 1, :] = places[:, 0:slots]
    out_ref[...] = jnp.dot(pick[...], src[...], preferred_element_type=f32).astype(bf16)


def place_rows(bases, digits, got, slots, rows, count):
    members, width = got.shape[0], got.shape[2]
    at = digits.shape[1] // 8 - 1
    span = -(-slots // 128) * 128
    return pl.pallas_call(
        lambda *refs: place_kernel(rows, *refs),
        grid_spec=pltpu.PrefetchScalarGridSpec(
            num_scalar_prefetch=1,
            grid=(bases.shape[0],),
            in_specs=[
                pl.BlockSpec((members, 8, digits.shape[2]), lambda i, b: (0, at, 0)),
                pl.BlockSpec((members, slots, width), lambda i, b: (0, 0, 0)),
            ],
            out_specs=[
                pl.BlockSpec((None, count, width), lambda i, b: (i, 0, 0)),
                pl.BlockSpec((members, slots), lambda i, b: (0, 0)),
            ],
            scratch_shapes=[
                pltpu.VMEM((members * span, width), bf16),
                pltpu.VMEM((count, members * span), bf16),
            ],
        ),
        out_shape=[
            jax.ShapeDtypeStruct((bases.shape[0], count, width), bf16),
            jax.ShapeDtypeStruct((members, slots), jnp.int32),
        ],
        compiler_params=small_vmem,
        cost_estimate=cost(0, (bases.shape[0] * count + members * slots) * width // 8),
        name="place_rows",
    )(bases, digits, got)


def take_kernel(ids_ref, from_ref, out_ref):
    cols = lax.broadcasted_iota(jnp.int32, (out_ref.shape[0], from_ref.shape[0]), 1)
    pick = jnp.where(ids_ref[...] == cols, 1.0, 0.0).astype(bf16)
    out_ref[...] = jnp.dot(pick, from_ref[...], preferred_element_type=f32).astype(
        out_ref.dtype
    )


def take_rows(ids, source, block, dtype):
    count = ids.shape[0]
    total, width = source.shape
    return pl.pallas_call(
        take_kernel,
        grid=(count // block,),
        in_specs=[
            pl.BlockSpec((block, 1), lambda i: (i, 0)),
            pl.BlockSpec((total, width), lambda i: (0, 0)),
        ],
        out_specs=pl.BlockSpec((block, width), lambda i: (i, 0)),
        out_shape=jax.ShapeDtypeStruct((count, width), dtype),
        compiler_params=small_vmem,
        cost_estimate=cost(2 * count * total * width, 2 * (count + total) * width),
        name="take_rows",
    )(ids, source)


def swap_mp(value):
    return lax.ppermute(value, "mp", [(0, 1), (1, 0)])


def side_by_side(mine, other, index):
    return jnp.where(
        index == 0,
        jnp.concatenate([mine, other], axis=1),
        jnp.concatenate([other, mine], axis=1),
    )


def rolled(full, shift):
    return jnp.roll(full, shift, axis=0)


def flip(value, bit):
    size = lax.axis_size("dp")
    return lax.ppermute(value, "dp", [(i, i ^ bit) for i in range(size)])


def dp_bits():
    return [1 << k for k in range(lax.axis_size("dp").bit_length() - 1)]


def halve(value, bit):
    half = value.shape[0] // 2
    side = (lax.axis_index("dp") // bit) % 2
    sent = lax.dynamic_slice_in_dim(value, (1 - side) * half, half, 0)
    kept = lax.dynamic_slice_in_dim(value, side * half, half, 0)
    return (kept.astype(f32) + flip(sent, bit).astype(f32)).astype(bf16)


def double(value, bit):
    side = (lax.axis_index("dp") // bit) % 2
    other = flip(value, bit)
    return jnp.where(
        side == 0,
        jnp.concatenate([value, other], axis=0),
        jnp.concatenate([other, value], axis=0),
    )


def sum_dp(value):
    bits = dp_bits()
    for bit in bits:
        value = halve(value, bit)
    for bit in reversed(bits):
        value = double(value, bit)
    return value


def after(value, *others):
    return lax.optimization_barrier((value, *others))[0]


class Ring:
    def __init__(self, parts):
        self.parts = parts
        self.nodes = nodes = lax.axis_size("dp") // 2
        chip = lax.axis_index("dp") // 2
        self.here = jnp.where(chip % 2 == 0, chip // 2, nodes - 1 - chip // 2)
        top = nodes // 2
        self.chips = [2 * p if p < top else 2 * (nodes - 1 - p) + 1 for p in range(nodes)]
        self.half = parts[0].shape[1] // 2
        self.held = {way: self.terms(self.here, way).astype(bf16) for way in (1, -1)}
        self.pieces = {1: [], -1: []}
        self.steps = 0

    def send(self, value, way):
        pairs = [
            (2 * self.chips[p] + c, 2 * self.chips[(p + way) % self.nodes] + c)
            for p in range(self.nodes)
            for c in range(2)
        ]
        return lax.ppermute(value, "dp", pairs)

    def terms(self, block, way):
        at = (block % self.nodes, 0 if way == 1 else self.half, 0)
        size = (1, self.half, self.parts[0].shape[2])
        pieces = [lax.dynamic_slice(v, at, size) for v in self.parts]
        return sum(piece.astype(f32) for piece in pieces)

    def step(self, *gates):
        count = self.steps
        if count == 2 * self.nodes - 2:
            return
        self.steps += 1
        adding = count < self.nodes - 1
        if gates:
            both = lax.optimization_barrier((self.held[1], self.held[-1], *gates))
            self.held = {1: both[0], -1: both[1]}
        for way in (1, -1):
            if count == self.nodes - 1:
                self.pieces[way].append(self.held[way])
            came = self.send(self.held[way], way)
            if adding:
                own = self.terms(self.here - way * (count + 1) + self.nodes, way)
                came = (came.astype(f32) + own).astype(bf16)
            else:
                self.pieces[way].append(came)
            self.held[way] = came

    def first(self, value):
        return after(value, *self.held.values())

    def total(self):
        return gather_pieces([p[0] for way in (1, -1) for p in self.pieces[way]])

    def order(self):
        block = jnp.arange(self.nodes, dtype=jnp.int32)
        up = (self.here + 1 - block + self.nodes) % self.nodes
        down = (block - self.here + 1 + self.nodes) % self.nodes + self.nodes
        core = lax.axis_index("dp")[None] % 2
        return jnp.concatenate([up, down, core]).astype(jnp.int32)


def gather_kernel(*refs):
    *sources, out_ref = refs
    for k, ref in enumerate(sources):
        out_ref[k] = ref[...]


def gather_pieces(pieces):
    count = len(pieces)
    vmem = pl.BlockSpec(memory_space=pltpu.VMEM)
    return pl.pallas_call(
        gather_kernel,
        in_specs=[vmem] * count,
        out_specs=vmem,
        out_shape=jax.ShapeDtypeStruct((count, *pieces[0].shape), bf16),
        compiler_params=tight_vmem,
        cost_estimate=cost(0, 4 * count * pieces[0].size),
        name="gather_pieces",
    )(*pieces)


def ff_kernel(sub, x_ref, g_ref, wg_ref, wu_ref, wd_ref, gx_ref, y_ref, h_ref, gg_ref, gu_ref):
    step = pl.program_id(0)
    for at in range(0, wg_ref.shape[1], sub):
        c = slice(at, at + sub)
        gate = jnp.dot(x_ref[...], wg_ref[:, c], preferred_element_type=f32)
        up = jnp.dot(x_ref[...], wu_ref[:, c], preferred_element_type=f32)
        grad = nt_dot(g_ref[...], wd_ref[c])
        sig = 1.0 / (1.0 + jnp.exp(-gate))
        silu = gate * sig
        h_ref[:, c] = (silu * up).astype(bf16)
        gg_ref[:, c] = (grad * up * (sig + silu * (1.0 - sig))).astype(bf16)
        gu_ref[:, c] = (grad * silu).astype(bf16)
    def back(first):
        w = 256
        for at in range(0, gx_ref.shape[1], w):
            c = slice(at, at + w)
            gx = nt_dot(gg_ref[...], wg_ref[c, :]) + nt_dot(gu_ref[...], wu_ref[c, :])
            y = jnp.dot(h_ref[...], wd_ref[:, c], preferred_element_type=f32)
            if first:
                gx_ref[:, c] = gx
                y_ref[:, c] = y
            else:
                gx_ref[:, c] += gx
                y_ref[:, c] += y
    pl.when(step == 0)(lambda: back(True))
    pl.when(step > 0)(lambda: back(False))

def feed_forward(x, g, wg, wu, wd, sub=384):
    r, d = x.shape
    hid = wg.shape[1]
    chunk = hid // 3
    whole = pl.BlockSpec((r, d), lambda i: (0, 0))
    tall = pl.BlockSpec((d, chunk), lambda i: (0, i))
    wide = pl.BlockSpec((r, chunk), lambda i: (0, i))
    return pl.pallas_call(
        lambda *refs: ff_kernel(sub, *refs),
        grid=(hid // chunk,),
        in_specs=[
            whole,
            whole,
            tall,
            tall,
            pl.BlockSpec((chunk, d), lambda i: (i, 0)),
        ],
        out_specs=[whole, whole, wide, wide, wide],
        out_shape=[jax.ShapeDtypeStruct((r, d), f32)] * 2 + [jax.ShapeDtypeStruct((r, hid), bf16)] * 3,
        compiler_params=forward_vmem,
        cost_estimate=cost(24 * r * d * hid, 6 * (d + r) * hid + 12 * r * d, 2 * r * hid),
        name="feed_forward",
    )(x, g, wg, wu, wd)

def grads_kernel(x0, x1, gg0, gg1, gu0, gu1, h0, h1, g0, g1, out_ref, xt, ht):
    step = pl.program_id(0)
    nodes, count, lanes = out_ref.shape
    rows = x0.shape[1] // nodes
    deep = h0.shape[1] // nodes
    r = x0.shape[0]
    @pl.when(step == 0)
    def _():
        xt[:, :r] = x0[...].T
        xt[:, r:] = x1[...].T
    @pl.when(step == 5)
    def _():
        ht[:, :r] = h0[...].T
        ht[:, r:] = h1[...].T
    def put(c, d, at):
        v = jnp.dot(xt[:, :r], c[...], preferred_element_type=f32) + jnp.dot(xt[:, r:], d[...], preferred_element_type=f32)
        out_ref[:, pl.ds(pl.multiple_of(at, 64), rows)] = v.astype(bf16).reshape(nodes, rows, lanes)
    @pl.when(step < 3)
    def _(): put(gg0, gg1, step * rows)
    @pl.when((step >= 3) & (step < 6))
    def _(): put(gu0, gu1, step * rows)
    @pl.when(step == 6)
    def _():
        v = jnp.dot(ht[:, :r], g0[:, :lanes], preferred_element_type=f32) + jnp.dot(ht[:, r:], g1[:, :lanes], preferred_element_type=f32)
        out_ref[:, 6 * rows : 6 * rows + deep] = v.astype(bf16).reshape(nodes, deep, lanes)
        v = jnp.dot(ht[:, :r], g0[:, lanes:], preferred_element_type=f32) + jnp.dot(ht[:, r:], g1[:, lanes:], preferred_element_type=f32)
        v = v.astype(bf16).reshape(nodes, deep, v.shape[1])
        short, rest = deep // 3, v.shape[2]
        for k in range(3):
            out_ref[:, 6 * rows + deep :, k * rest : (k + 1) * rest] = v[:, k * short : (k + 1) * short]

def ff_grads(side, nodes, x0, x1, gg0, gg1, gu0, gu1, h0, h1, g0, g1):
    r, d = x0.shape
    hid = gg0.shape[1]
    lanes = hid // 3
    rows, deep = d // (2 * nodes), hid // (2 * nodes)
    count = 6 * rows + deep + deep // 3
    half = lambda n: pl.BlockSpec((r, n), lambda i, s: (0, s[0]))
    first = pl.BlockSpec((r, lanes), lambda i, s: (0, jnp.minimum(i, 2)))
    second = pl.BlockSpec((r, lanes), lambda i, s: (0, jnp.clip(i - 3, 0, 2)))
    whole = pl.BlockSpec((r, d), lambda i, s: (0, 0))
    return pl.pallas_call(
        lambda s, *refs: grads_kernel(*refs),
        grid_spec=pltpu.PrefetchScalarGridSpec(
            num_scalar_prefetch=1, grid=(7,),
            in_specs=[half(d // 2)] * 2 + [first] * 2 + [second] * 2 + [half(hid // 2)] * 2 + [whole] * 2,
            out_specs=pl.BlockSpec((nodes, count, lanes), lambda i, s: (0, 0, 0)),
            scratch_shapes=[pltpu.VMEM((d // 2, 2 * r), bf16), pltpu.VMEM((hid // 2, 2 * r), bf16)],
        ),
        out_shape=jax.ShapeDtypeStruct((nodes, count, lanes), bf16),
        compiler_params=big_vmem,
        cost_estimate=cost(12 * r * d * hid, 6 * r * hid + 5 * d * hid),
        name="ff_grads",
    )(side.astype(jnp.int32).reshape(1), x0, x1, gg0, gg1, gu0, gu1, h0, h1, g0, g1)


def open_specs(nodes, group, half, lanes, first=0):
    specs = []
    for _ in range(2):
        for b in range(group):
            for at in (0, nodes):
                specs.append(
                    pl.BlockSpec(
                        (None, half, lanes),
                        lambda j, h, order, b=b, at=at: (
                            order[at + (first + j) * group + b],
                            0,
                            0,
                        ),
                    )
                )
    return specs


def open_blocks(group, order_ref, refs, write):
    core = order_ref[order_ref.shape[0] - 1]
    half = refs[0].shape[0]

    def reader(first, second):
        def read(start, stop):
            if stop <= half:
                return first[start:stop].astype(f32)
            if start >= half:
                return second[start - half : stop - half].astype(f32)
            pieces = [first[start:half], second[0 : stop - half]]
            return jnp.concatenate([p.astype(f32) for p in pieces], axis=0)

        return read

    def hand(refs):
        for b in range(group):
            write(b, reader(refs[2 * b], refs[2 * b + 1]))

    own = pl.program_id(1) == core
    pl.when(own)(lambda: hand(refs[: 2 * group]))
    pl.when(jnp.logical_not(own))(lambda: hand(refs[2 * group :]))


def open_ff_kernel(group, order_ref, *refs):
    *pieces, gate_ref, up_ref, down_ref = refs
    lanes = pieces[0].shape[1]
    rows, deep = gate_ref.shape[0] // group, down_ref.shape[0] // group
    rest = down_ref.shape[1] - lanes
    short = deep // 3

    def write(b, read):
        here = slice(b * rows, (b + 1) * rows)
        for k, out in enumerate((gate_ref, up_ref)):
            for c in range(3):
                part = read((3 * k + c) * rows, (3 * k + c + 1) * rows)
                out[here, c * lanes : (c + 1) * lanes] = part
        low, at = b * deep, 6 * rows
        down_ref[low : low + deep, :lanes] = read(at, at + deep)
        for c in range(3):
            part = read(at + deep, at + deep + short)[:, c * rest : (c + 1) * rest]
            down_ref[low + c * short : low + (c + 1) * short, lanes:] = part

    open_blocks(group, order_ref, pieces, write)


def open_ff(pieces, order, at, so_far, width, hidden):
    mine, other = pieces
    half, lanes = mine.shape[1:]
    nodes, group = mine.shape[0] // 2, 2
    steps = nodes // group
    rows, deep = width // (2 * nodes), hidden // (2 * nodes)
    out = lambda tall, wide: pl.BlockSpec(
        (group * tall, wide), lambda j, h, order: (h * steps + at, 0)
    )
    specs = open_specs(nodes, group, half, lanes, at)
    shapes = [(width, hidden), (width, hidden), (hidden, width)]
    kernel = lambda order, *refs: open_ff_kernel(
        group, order, *refs[: 4 * group], *refs[4 * group + len(so_far) :]
    )
    return pl.pallas_call(
        kernel,
        grid_spec=pltpu.PrefetchScalarGridSpec(
            num_scalar_prefetch=1,
            grid=(1, 2),
            in_specs=specs + [pl.BlockSpec(memory_space=pl.ANY)] * len(so_far),
            out_specs=[out(rows, hidden), out(rows, hidden), out(deep, width)],
        ),
        out_shape=[jax.ShapeDtypeStruct(shape, f32) for shape in shapes],
        input_output_aliases={1 + 4 * group + k: k for k in range(len(so_far))},
        compiler_params=tight_vmem,
        cost_estimate=cost(0, 24 * width * hidden // steps),
        name="open_ff",
    )(order, *[mine] * (2 * group), *[other] * (2 * group), *so_far)


def pack_conv_kernel(core_ref, in_ref, out_w_ref, tail_ref, away_ref, own_ref):
    blocks, _, width = own_ref.shape
    rows = in_ref.shape[0] // (2 * blocks)
    deep = out_w_ref.shape[0] // blocks
    lanes = width // 2

    def write(ref):
        for k in range(blocks):
            ref[k, 0:rows, 0:lanes] = in_ref[2 * k * rows : (2 * k + 1) * rows]
            ref[k, 0:rows, lanes:] = in_ref[(2 * k + 1) * rows : (2 * k + 2) * rows]
            ref[k, rows : rows + deep] = out_w_ref[k * deep : (k + 1) * deep]
            ref[k, rows + deep :] = tail_ref[...]

    pl.when(pl.program_id(0) == 0)(lambda: write(away_ref))
    pl.when(pl.program_id(0) == 1)(lambda: write(own_ref))


def pack_conv(grad_in, grad_out, tail, part, nodes):
    total, width = grad_in.shape
    half_in, half_out = total // 2, grad_out.shape[0] // 4
    spared = tail.shape[0]
    count = half_in // (2 * nodes) + half_out // nodes + spared
    core = (lax.axis_index("dp") % 2).astype(jnp.int32).reshape(1)
    side = lambda i, c: jnp.where(i == 0, 1 - c[0], c[0])
    out = pl.BlockSpec((nodes, count, width), lambda i, c: (0, 0, 0))
    return pl.pallas_call(
        pack_conv_kernel,
        grid_spec=pltpu.PrefetchScalarGridSpec(
            num_scalar_prefetch=1,
            grid=(2,),
            in_specs=[
                pl.BlockSpec((half_in, width // 2), lambda i, c: (side(i, c), part)),
                pl.BlockSpec((half_out, width), lambda i, c: (2 * part + side(i, c), 0)),
                pl.BlockSpec((spared, width), lambda i, c: (0, 0)),
            ],
            out_specs=[out, out],
        ),
        out_shape=[jax.ShapeDtypeStruct((nodes, count, width), bf16)] * 2,
        compiler_params=tight_vmem,
        cost_estimate=cost(0, 2 * (grad_in.size + grad_out.size)),
        name="pack_conv",
    )(core, grad_in, grad_out, tail)


def open_conv_kernel(group, order_ref, *refs):
    *pieces, in_ref, out_w_ref, tail_ref = refs
    rows, lanes = in_ref.shape[0] // (2 * group), in_ref.shape[1]
    deep = out_w_ref.shape[0] // group

    def write(b, read):
        low = 2 * b * rows
        in_ref[low : low + rows] = read(0, rows)[:, :lanes]
        in_ref[low + rows : low + 2 * rows] = read(0, rows)[:, lanes:]
        out_w_ref[b * deep : (b + 1) * deep] = read(rows, rows + deep)
        tail_ref[b] = read(rows + deep, rows + deep + tail_ref.shape[1])

    open_blocks(group, order_ref, pieces, write)


def open_conv(ring, gate, total, deep_total):
    mine = after(ring.total(), gate)
    other = flip(mine, 1)
    _, half, width = mine.shape
    nodes, group = ring.nodes, ring.nodes // 2
    blocks = 2 * nodes
    steps = nodes // group
    rows, deep = total // blocks, deep_total // blocks
    spared = 2 * half - rows // 2 - deep
    at = lambda j, h, order: (h * steps + j, 0)
    return pl.pallas_call(
        lambda *refs: open_conv_kernel(group, *refs),
        grid_spec=pltpu.PrefetchScalarGridSpec(
            num_scalar_prefetch=1,
            grid=(steps, 2),
            in_specs=open_specs(nodes, group, half, width),
            out_specs=[
                pl.BlockSpec((group * rows, width // 2), at),
                pl.BlockSpec((group * deep, width), at),
                pl.BlockSpec(
                    (group, spared, width), lambda j, h, order: (h * steps + j, 0, 0)
                ),
            ],
        ),
        out_shape=[
            jax.ShapeDtypeStruct((total, width // 2), f32),
            jax.ShapeDtypeStruct((deep_total, width), f32),
            jax.ShapeDtypeStruct((blocks, spared, width), f32),
        ],
        compiler_params=tight_vmem,
        cost_estimate=cost(0, 8 * (total + deep_total) * width),
        name="open_conv",
    )(ring.order(), *[mine] * (2 * group), *[other] * (2 * group))


def on_device(
    tokens,
    cotangent,
    route,
    seq_lengths,
    norm1_gain,
    in_weight,
    conv_weight,
    out_weight,
    norm2_gain,
    gate_weight,
    up_weight,
    down_weight,
):
    dp_size = lax.axis_size("dp")
    mp_size = lax.axis_size("mp")
    dp_index = lax.axis_index("dp")
    mp_index = lax.axis_index("mp")
    rows = tokens.shape[0]
    narrow = tokens.shape[1]
    width = norm1_gain.shape[0]
    own = rows // mp_size
    start = mp_index * own
    column = mp_index * narrow
    pair_share = rows // dp_size
    slots = pair_share + pair_share // 2
    paired = mp_size == 2

    if paired:
        core = dp_index % 2
        deep = width // 2
        part_in = lax.dynamic_slice_in_dim(in_weight, core * deep, deep, 1)
        part_out = lax.dynamic_slice_in_dim(out_weight, core * deep, deep, 1)
        part = jnp.concatenate([part_in, part_out.reshape(1, deep, deep)], axis=0)
        there = swap_mp(part)
        route = after(route, part)
        taps = jnp.concatenate([conv_weight, swap_mp(conv_weight)], axis=1)
    else:
        full_in = lax.all_gather(in_weight, "mp", axis=2, tiled=True)
        full_out = lax.all_gather(out_weight, "mp", axis=0, tiled=True)
        taps = lax.all_gather(conv_weight, "mp", axis=1, tiled=True)

    sent_rows, digits, slot_of = pack(route, tokens, dp_size, slots)
    sent_seeds = send_rows(after(slot_of, sent_rows), cotangent, dp_size, slots)
    over = dict(split_axis=0, concat_axis=0, tiled=True)
    got_rows = lax.all_to_all(sent_rows, "dp", **over)
    digits = got_rows if slots <= narrow else lax.all_to_all(digits, "dp", **over)
    got_rows, sent_seeds = lax.optimization_barrier((got_rows, sent_seeds))
    got_seeds = lax.all_to_all(sent_seeds, "dp", **over)
    slot_of = slot_of.reshape(rows, 1)
    window = own + 2 * halo
    if paired:
        bases = jnp.stack([start, own - start]).astype(jnp.int32)
        digits = got_rows if slots <= narrow else digits
        pieces, places = place_rows(bases - halo, digits, got_rows, slots, rows, window)
        there, _ = lax.optimization_barrier((there, pieces))
        here = flip(there, 1)
        both = [jnp.where(core == k, there, here) for k in range(2)]
        other_in = jnp.concatenate([v[:3] for v in both], axis=1)
        other_out = jnp.concatenate([v[3] for v in both], axis=1)
        full_in = jnp.concatenate([in_weight, other_in], axis=2)
        full_out = jnp.concatenate([out_weight, other_out], axis=0)
        input_rows = side_by_side(pieces[0], swap_mp(pieces[1]), mp_index)
        pieces, _ = place_rows(bases, digits, got_seeds, slots, rows, own)
        input_rows = after(input_rows, pieces)
        came = swap_mp(pieces[1])
        seeds_here = came
        seeds_own = side_by_side(pieces[0], came, mp_index)
        seeds_other = side_by_side(pieces[1], swap_mp(after(pieces[0], came)), mp_index)
        place_ids = ((places - start) % rows).reshape(-1, 1)
    else:
        bases = (jnp.arange(mp_size) * own).astype(jnp.int32)
        pieces, places = place_rows(bases, digits, got_rows, slots, rows, own)
        full = lax.all_gather(pieces.reshape(rows, narrow), "mp", axis=1, tiled=True)
        full = jnp.pad(full, ((halo, halo), (0, 0)))
        input_rows = lax.dynamic_slice_in_dim(full, start, window, 0)
        pieces, _ = place_rows(bases, digits, got_seeds, slots, rows, own)
        full = lax.all_gather(pieces.reshape(rows, narrow), "mp", axis=1, tiled=True)
        seeds = rolled(full, -start)
        seeds_own, seeds_other = seeds[:own], seeds[own:]
        seeds_here = seeds_own
        place_ids = places.reshape(-1, 1)

    positions = start - halo + jnp.arange(window, dtype=jnp.int32)
    first_mask, second_mask = seq_masks(seq_lengths[0], positions, rows)
    residual = input_rows.astype(f32)
    scale_one = lax.rsqrt(jnp.mean(residual * residual, axis=1) + epsilon)[:, None]
    normed_one = (residual * scale_one * norm1_gain).astype(bf16)
    projected = jnp.einsum("rd,kdc->krc", normed_one, full_in, preferred_element_type=f32)
    projected = after(projected, seeds_here)
    in_gate, out_gate, value_part = (projected[0], projected[1], projected[2])
    mixed = in_gate * value_part
    lag_one = lag_rows(mixed, 1) * first_mask
    lag_two = lag_rows(mixed, 2) * second_mask
    convolved = taps[2] * mixed + taps[1] * lag_one + taps[0] * lag_two
    gated = (out_gate * convolved).astype(bf16)
    middle = (residual + jnp.dot(gated, full_out, preferred_element_type=f32))[halo:]
    scale_two = lax.rsqrt(jnp.mean(middle * middle, axis=1) + epsilon)[:, None]
    normed_own = (middle[:own] * scale_two[:own] * norm2_gain).astype(bf16)

    weights = (gate_weight, up_weight, down_weight)
    if paired:
        normed_other = swap_mp(normed_own)
        first = feed_forward(normed_own, seeds_own, *weights)
        second = feed_forward(normed_other, seeds_other, *weights)
        sent = jnp.concatenate([second[0], first[0][:halo]], axis=0).astype(bf16)
        came = swap_mp(sent)
        saved = (normed_other, first[3], second[3], first[4], second[4])
        saved += (first[2], second[2], seeds_own, seeds_other)
        away = ff_grads(1 - core, dp_size // 2, after(normed_own, sent), *saved)
        kept = ff_grads(core, dp_size // 2, after(normed_own, away), *saved)
        away = flip(away, 1)
        came, _ = lax.optimization_barrier((came, kept))
        grad_normed_two = jnp.concatenate([first[0], second[0][:halo]], axis=0)
        grad_normed_two = grad_normed_two + came.astype(f32)
        down_came = swap_mp(after(second[1].astype(bf16), came))
        ring = Ring((kept, away))
        grad_normed_two = ring.first(grad_normed_two)
        ring.step()
    else:
        normed_two = rolled(lax.all_gather(normed_own, "mp", axis=0, tiled=True), -start)
        gate_val = jnp.dot(normed_two, gate_weight, preferred_element_type=f32)
        up_val = jnp.dot(normed_two, up_weight, preferred_element_type=f32)
        sigmoid_val = jax.nn.sigmoid(gate_val)
        silu_val = gate_val * sigmoid_val
        hidden = (silu_val * up_val).astype(bf16)
        grad_hidden = nt_dot(seeds, down_weight)
        grad_gate_val = (
            grad_hidden * up_val * sigmoid_val * (1.0 + gate_val * (1.0 - sigmoid_val))
        ).astype(bf16)
        grad_up_val = (grad_hidden * silu_val).astype(bf16)
        normed_terms = nt_dot(grad_gate_val, gate_weight) + nt_dot(grad_up_val, up_weight)
        down_terms = jnp.dot(hidden, down_weight, preferred_element_type=f32)
        full = rolled(lax.psum(rolled(normed_terms, start), "mp"), -start)
        grad_normed_two = full[: own + halo]
        down_sum = rolled(lax.psum(rolled(down_terms, start), "mp"), -start)[:own]
        total_gate = sum_dp(tn_dot(normed_two, grad_gate_val).astype(bf16)).astype(f32)
        total_up = sum_dp(tn_dot(normed_two, grad_up_val).astype(bf16)).astype(f32)
        total_down = sum_dp(tn_dot(hidden, seeds).astype(bf16)).astype(f32)
        block_own = (middle[:own] + down_sum).astype(bf16)

    def to_features(mine):
        if not paired:
            full = lax.all_gather(mine, "mp", axis=0, tiled=True)
            return lax.dynamic_slice_in_dim(full, column, narrow, 1)
        low, high = mine[:, :narrow], mine[:, narrow:]
        other = swap_mp(jnp.where(mp_index == 0, high, low))
        return jnp.concatenate([jnp.where(mp_index == 0, low, high), other], axis=0)

    shape = (dp_size, slots, narrow)
    back_block = min(8 * slots, slots * dp_size)
    home_block = min(rows, 512)

    def leave(piece):
        return take_rows(place_ids, piece, back_block, bf16).reshape(shape)

    def to_home(back):
        return lax.all_to_all(back, "dp", **over)

    def arrive(home, dtype):
        return take_rows(slot_of, home.reshape(-1, narrow), home_block, dtype)

    gain_two_term = jnp.sum((grad_normed_two * middle * scale_two)[:own], axis=0)
    dot_two = jnp.sum(norm2_gain * grad_normed_two * middle, axis=1, keepdims=True)
    grad_middle = (
        jnp.concatenate([seeds_own, seeds_other[:halo]], axis=0).astype(f32)
        + scale_two * norm2_gain * grad_normed_two
        - middle * (scale_two * scale_two * scale_two * dot_two / width)
    )
    grad_mix = grad_middle.astype(bf16)
    grad_gated = jnp.einsum("rd,cd->rc", grad_mix, full_out, preferred_element_type=f32)
    if paired:
        grad_gated = ring.first(grad_gated)
        ring.step()
    grad_conv = grad_gated * out_gate[halo:]
    inner = slice(halo, halo + own)
    conv_terms = jnp.stack(
        [
            jnp.sum(grad_conv[:own] * lag_two[inner], axis=0),
            jnp.sum(grad_conv[:own] * lag_one[inner], axis=0),
            jnp.sum(grad_conv[:own] * mixed[inner], axis=0),
        ],
        axis=0,
    )
    grad_mixed = (
        taps[2] * grad_conv
        + taps[1] * lead_rows(grad_conv * first_mask[halo:], 1)
        + taps[0] * lead_rows(grad_conv * second_mask[halo:], 2)
    )[:own]
    grad_parts = jnp.stack(
        [
            grad_mixed * value_part[inner],
            grad_gated[:own] * convolved[inner],
            grad_mixed * in_gate[inner],
        ],
        axis=0,
    ).astype(bf16)
    grad_in = jnp.einsum(
        "rd,krc->kdc", normed_one[inner], grad_parts, preferred_element_type=f32
    ).astype(bf16)
    grad_out = jnp.einsum(
        "rc,rd->cd", gated[inner], grad_mix[:own], preferred_element_type=f32
    ).astype(bf16)
    taps_end = 2 + conv_weight.shape[0]

    parts_late = grad_parts
    if paired:
        ring.step()
        parts_late = ring.first(grad_parts)
    grad_normed_one = jnp.einsum("krc,kdc->rd", parts_late, full_in, preferred_element_type=f32)
    residual_own = residual[inner]
    scale_own = scale_one[inner]
    gain_one_term = jnp.sum(grad_normed_one * residual_own * scale_own, axis=0)
    dot_one = jnp.sum(norm1_gain * grad_normed_one * residual_own, axis=1, keepdims=True)
    input_own = (
        grad_middle[:own]
        + scale_own * norm1_gain * grad_normed_one
        - residual_own * (scale_own * scale_own * scale_own * dot_one / width)
    ).astype(bf16)

    def packed_half(k, *gates):
        lanes = slice(k * narrow, (k + 1) * narrow)
        terms = jnp.pad(conv_terms[:, lanes], ((0, 16 - taps_end), (0, width - narrow)))
        gains = jnp.stack([gain_one_term, gain_two_term], axis=0)
        ends = after(jnp.concatenate([gains, terms], axis=0).astype(bf16), *gates)
        return pack_conv(grad_in.reshape(-1, width), grad_out, ends, k, dp_size // 2)

    if paired:
        away, other = packed_half(1)
        passed = (other.astype(f32) + flip(away, 1).astype(f32)).astype(bf16)
        down_came = after(down_came, grad_parts)
        block_own = (middle[:own] + (first[1] + down_came.astype(f32))).astype(bf16)
        block_piece = to_features(block_own)
        block_back = leave(block_piece)
        out_home = to_home(block_back)
        ring.step(block_piece)
        ring.step(passed)
        away, own_half = packed_half(0, passed)
        passed = swap_mp(passed)
        input_piece = to_features(input_own)
        ring.step(input_piece)
        input_back = leave(after(input_piece, out_home))
        grad_home = to_home(input_back)
        second = Ring((own_half, flip(away, 1), passed))
        ring.step(*second.held.values(), out_home)
        second.step()
        block_out = arrive(out_home, bf16)
        ring.step(*second.held.values(), grad_home)
        second.step(block_out)
        tokens_grad = arrive(grad_home, f32)
        ring.step(*second.held.values())
        second.step()
        ring.step(*second.held.values(), tokens_grad)
        second.step()
        while ring.steps < 2 * ring.nodes - 2:
            ring.step(*second.held.values())
            second.step()
        mine = ring.total()
        pieces = (mine, flip(mine, 1))
        second.step(mine)
        totals = ()
        for at in range(ring.nodes // 2):
            totals = open_ff(pieces, ring.order(), at, totals, width, gate_weight.shape[1])
            second.step(*totals)
        while second.steps < 2 * second.nodes - 2:
            second.step()
        total_gate, total_up, total_down = totals
        total_in, total_out, ends = open_conv(
            second, total_gate, grad_in.size // (2 * narrow), narrow
        )
        tail = ends[0]
    else:
        block_out = arrive(to_home(leave(to_features(block_own))), bf16)
        tokens_grad = arrive(to_home(leave(to_features(input_own))), f32)
        total_in = lax.psum_scatter(
            grad_in.astype(f32), "mp", scatter_dimension=2, tiled=True
        )
        total_in = sum_dp(total_in.astype(bf16).reshape(-1, narrow)).astype(f32)
        total_out = lax.psum_scatter(
            grad_out.astype(f32), "mp", scatter_dimension=0, tiled=True
        )
        total_out = sum_dp(total_out.astype(bf16)).astype(f32)
        gains = lax.psum(jnp.stack([gain_one_term, gain_two_term]), ("dp", "mp"))
        terms = lax.psum_scatter(conv_terms, "mp", scatter_dimension=1, tiled=True)
        terms = jnp.pad(lax.psum(terms, "dp"), ((0, 0), (0, width - narrow)))
        tail = jnp.concatenate([gains, terms], axis=0)
    total_taps = tail[2:taps_end, :narrow]
    return (
        block_out,
        tokens_grad,
        tail[0],
        total_in.reshape(in_weight.shape),
        total_taps,
        total_out,
        tail[1],
        total_gate,
        total_up,
        total_down,
    )


def solution(mesh):
    in_specs = (
        P("dp", "mp"),
        P("dp", "mp"),
        P("dp"),
        P("dp", None),
        P(),
        P(None, None, "mp"),
        P(None, "mp"),
        P("mp", None),
        P(),
        P(None, "mp"),
        P(None, "mp"),
        P("mp", None),
    )
    out_specs = (
        P("dp", "mp"),
        P("dp", "mp"),
        P(),
        P(None, None, "mp"),
        P(None, "mp"),
        P("mp", None),
        P(),
        P(None, "mp"),
        P(None, "mp"),
        P("mp", None),
    )
    return jax.shard_map(
        on_device, mesh=mesh, in_specs=in_specs, out_specs=out_specs, check_vma=False
    )
```
